32 devices in a mesh: groups: 2 (over x), tp: 8 (over z, y), sp: 2 (over core).
Axes of the slice: x: 2, y: 2, z: 4, core: 2. Of those that a mesh axis runs over, the one named last changes fastest.
Arguments:
- tokens: bfloat16 [1536, 4608], P(('groups', 'tp', 'sp')), parts along dimension 0, may hold values from -48 to 48
- w_query: bfloat16 [4608, 1024], P(None, 'tp'), may hold values from -0.09375 to 0.09375
- w_key: bfloat16 [4608, 512], P(None, 'tp'), may hold values from -0.09375 to 0.09375
- w_value: bfloat16 [4608, 512], P(None, 'tp'), may hold values from -0.09375 to 0.09375
- w_out: bfloat16 [1024, 4608], P('tp'), may hold values from -0.5 to 0.5
- doc_lengths: int32 [16], P('groups'), parts along dimension 0, may hold values from 1 to 192, 768 in all
Outputs:
- attn_out: bfloat16 [1536, 4608], P(('groups', 'tp', 'sp')), parts along dimension 0
The draws below stay inside these ranges and needn't reach their ends.
There are 2 independent parts, one for each index of `groups`. The reference program is written for one: setup_inputs(seed, part) draws one part's arguments, and reference() takes and returns one part's arrays. A program takes and returns all parts, laid end to end along the dimension named above; an argument that names none is the same for every part. Nothing has to cross between parts.
Inputs may be any that keep to these rules, and one draw needn't show every extreme that they name: `doc_lengths`: positive lengths that sum to 768; the largest is exactly a quarter of 768.
All inputs are finite; a program needn't handle non-finite values.
Results may differ from the reference program's by a relative error of at most 0.024.
Values may be sent and summed in bfloat16 or wider, within the bound.
No kernel may reach another device: no remote copies, remote signals or barrier semaphores. Data moves between devices by JAX's collectives and lax.ppermute only.
A program may use at most 128 MiB of HBM per device.

```python
import math
import jax
import jax.numpy as jnp
import numpy as np
from jax import lax

D = 4608
HD = 128
PRE_SCALE = 144
DOCS = 8
HEADS = 8
KV_HEADS = 4
SEQ = 768


def draw_tokens(key, part):
    normal_key = jax.random.fold_in(jax.random.fold_in(key, 11), 0)
    base_draw = jnp.clip(jax.random.normal(normal_key, (SEQ, D), jnp.float32), -6.0, 6.0)
    return base_draw.astype(jnp.bfloat16)


def steps_of(key, dims, shards, smallest, top_value):
    gain = 1.0
    for dim, blocks in shards:
        draws = jax.random.uniform(jax.random.fold_in(jax.random.fold_in(key, 6), dim), (blocks,), jnp.float32, smallest / len(shards), top_value / len(shards))
        gain = gain * jnp.repeat(jnp.exp(draws), dims[dim] // blocks).reshape((-1,) + (1,) * (len(dims) - 1 - dim))
    return gain


def profile(count, total, reach, slope):
    loads = [(1 << 20) // math.isqrt(rank ** slope) + 1 for rank in range(2, count + 1)]
    rest, given = total - reach - (count - 1), [1] * (count - 1)
    while rest > 0:
        candidates = [i for i in range(count - 1) if given[i] < reach]
        pool, budget = sum([loads[i] for i in candidates]), rest
        for i in candidates:
            more = min(reach - given[i], max(1, budget * loads[i] // pool), rest)
            given[i] = given[i] + more
            rest = rest - more
    return np.array([reach] + given)


def ragged(rng, amount, total, limit, skew):
    if amount == 2:
        one = jax.random.randint(rng, (), max(1, total - limit), min(limit, total - 1) + 1)
        return jnp.stack([one, total - one])
    sizes = jnp.asarray(profile(amount, total, limit, skew), jnp.int32)
    twos = (amount - 1) // 2
    source_of, sink = sizes[1:1 + 2 * twos:2], sizes[2:2 + 2 * twos:2]
    margin = jnp.minimum(source_of - 1, limit - sink)
    shifted = jax.random.randint(jax.random.fold_in(rng, 1), (twos,), 0, 1 << 20) % (margin + 1)
    sizes = sizes.at[1:1 + 2 * twos:2].set(source_of - shifted).at[2:2 + 2 * twos:2].set(sink + shifted)
    return sizes[jax.random.permutation(jax.random.fold_in(rng, 2), amount)]


def noise(own_key, shape, deviation, bound, cuts=(), held_as=jnp.bfloat16):
    result = deviation * jax.random.normal(own_key, shape, jnp.float32)
    if cuts:
        result = result * steps_of(own_key, shape, cuts, -0.22, 0.18)
    return jnp.clip(result, -bound, bound).astype(held_as)


def setup_inputs(seed: int = 0, part: int = 0) -> dict:
    key_list = jax.random.split(jax.random.key(seed), 7)
    part_splits = jax.random.split(jax.random.fold_in(key_list[6], part), 7)
    return {
        "tokens": draw_tokens(jax.random.fold_in(jax.random.fold_in(key_list[6], part), 71), part),
        "w_query": noise(key_list[1], (D, HEADS * HD), D ** -0.5, 0.09375, ((1, 8),)),
        "w_key": noise(key_list[2], (D, KV_HEADS * HD), D ** -0.5, 0.09375, ((1, 8),)),
        "w_value": noise(key_list[3], (D, KV_HEADS * HD), D ** -0.5, 0.09375, ((1, 8),)),
        "w_out": noise(key_list[4], (HEADS * HD, D), HD ** -0.5, 0.5, ((0, 8),)),
        "doc_lengths": ragged(part_splits[5], DOCS, SEQ, SEQ // 4, 2).astype(jnp.int32),
    }


def rotate(matrix, places):
    half_width = matrix.shape[1] // 2
    spread = jnp.power(10000.0, -(jnp.arange(half_width, dtype=jnp.float32) * (2.0 / matrix.shape[1])))
    angles = places.astype(jnp.float32)[:, None] * spread[None, :]
    cosine = jnp.cos(angles)
    sine_part = jnp.sin(angles)
    lower_part = matrix[:, :half_width]
    upper_part = matrix[:, half_width:]
    return jnp.concatenate([lower_part * cosine - upper_part * sine_part, upper_part * cosine + lower_part * sine_part], axis=1)


def doc_index(places, doc_ends):
    return jnp.sum((places[:, None] >= doc_ends[None, :]).astype(jnp.int32), axis=1)


def reference(tokens, w_query, w_key, w_value, w_out, doc_lengths):
    length = tokens.shape[0]
    places = jnp.arange(length, dtype=jnp.int32)
    doc_ends = jnp.cumsum(doc_lengths).astype(jnp.int32)
    doc_ids = doc_index(places, doc_ends)
    allowed = (doc_ids[:, None] == doc_ids[None, :]) & (places[None, :] <= places[:, None])
    key_raw = lax.optimization_barrier(jnp.dot(tokens, w_key, preferred_element_type=jnp.float32).astype(jnp.bfloat16))
    value_all = jnp.dot(tokens, w_value, preferred_element_type=jnp.float32).astype(jnp.bfloat16)

    def head_step(running_sum, head_index):
        w_head = lax.dynamic_slice_in_dim(w_query, head_index * HD, HD, 1)
        queries = (rotate(jnp.dot(tokens, w_head, preferred_element_type=jnp.float32), places) * PRE_SCALE ** -0.5).astype(jnp.bfloat16)
        pair_index = head_index // 2
        key_part = lax.dynamic_slice_in_dim(key_raw, pair_index * HD, HD, 1).astype(jnp.float32)
        key_rows = rotate(key_part, places).astype(jnp.bfloat16)
        value_rows = lax.dynamic_slice_in_dim(value_all, pair_index * HD, HD, 1)
        scores = jnp.dot(queries, key_rows.T, preferred_element_type=jnp.float32)
        largest = jnp.max(jnp.where(allowed, scores, -1e30), axis=1, keepdims=True)
        weights = jnp.where(allowed, jnp.exp(scores - largest), 0.0)
        denominator = jnp.sum(weights, axis=1, keepdims=True)
        attended = (jnp.dot(weights.astype(jnp.bfloat16), value_rows, preferred_element_type=jnp.float32) / denominator).astype(jnp.bfloat16)
        w_head_out = lax.dynamic_slice_in_dim(w_out, head_index * HD, HD, 0)
        partial_value = lax.optimization_barrier(jnp.dot(attended, w_head_out, preferred_element_type=jnp.float32).astype(jnp.bfloat16))
        return running_sum + partial_value.astype(jnp.float32), None

    initial = jnp.zeros((length, tokens.shape[1]), jnp.float32)
    summed, _ = lax.scan(head_step, initial, jnp.arange(HEADS, dtype=jnp.int32))
    return summed.astype(jnp.bfloat16)
```

```python
import jax
import jax.numpy as jnp
from jax import lax
from jax.sharding import PartitionSpec as P

PRE_SCALE = 144

masked_low = -1e30


def swap_tp(block, flip, only=None):
    count = lax.axis_size("tp")
    route = [(t, t ^ flip) for t in range(count) if only is None or only(t)]
    return lax.ppermute(block, "tp", route)


def swap_sp(block):
    count = lax.axis_size("sp")
    return lax.ppermute(block, "sp", [(s, s ^ 1) for s in range(count)])


def fence(*values):
    return lax.optimization_barrier(values)


def angles_of(places, head_dim):
    half_width = head_dim // 2
    spread = jnp.power(
        10000.0, -(jnp.arange(half_width, dtype=jnp.float32) * (2.0 / head_dim))
    )
    angles = places.astype(jnp.float32)[:, None] * spread[None, :]
    return jnp.cos(angles), jnp.sin(angles)


def rotate(matrix, cosine, sine_part):
    half_width = matrix.shape[1] // 2
    lower_part = matrix[:, :half_width]
    upper_part = matrix[:, half_width:]
    return jnp.concatenate(
        [
            lower_part * cosine - upper_part * sine_part,
            upper_part * cosine + lower_part * sine_part,
        ],
        axis=1,
    )


def doc_index(places, doc_ends):
    return jnp.sum((places[:, None] >= doc_ends[None, :]).astype(jnp.int32), axis=1)


def gather_slabs(tokens, slabs, slab):
    if slabs != 4:
        return [tokens] + [swap_tp(tokens, 2 * k) for k in range(1, slabs)]
    far = swap_tp(tokens, 4)
    near = swap_tp(tokens, 2)
    far, again = fence(far, tokens)
    inner = lambda t: (t >> 1) in (1, 2)
    relayed = swap_tp(far, 2, inner)
    middle = swap_tp(again, 6, inner)
    last = jnp.where((slab == 1) | (slab == 2), middle, relayed)
    return [tokens, near, far, last]


def local(tokens, w_query, w_key, w_value, w_out, doc_lengths):
    rows, width = tokens.shape
    tp_count = lax.axis_size("tp")
    sp_count = lax.axis_size("sp")
    sp_place = lax.axis_index("sp")
    tp_place = lax.axis_index("tp")
    slabs = tp_count // 2
    slab = tp_place // 2
    side = tp_place % 2
    head_dim = w_query.shape[1]
    half_dim = w_key.shape[1]
    doc_ends = jnp.cumsum(doc_lengths)

    depth = width // sp_count
    w_own = jnp.concatenate([w_query, w_key, w_value], axis=1)
    share = lax.dynamic_slice_in_dim(w_own, sp_place * depth, depth, 0)
    share = swap_tp(share, 1)
    blocks = gather_slabs(tokens, slabs, slab)
    other = swap_sp(share)
    low = jnp.where(sp_place == 0, share, other)
    high = jnp.where(sp_place == 0, other, share)
    w_pair = jnp.concatenate([low, high], axis=0)
    out_depth = head_dim // sp_count
    out_share = swap_tp(lax.dynamic_slice_in_dim(w_out, sp_place * out_depth, out_depth, 0), 1)
    out_other = swap_sp(out_share)

    gathered = jnp.concatenate(blocks, axis=0)
    own = jnp.dot(gathered, w_own, preferred_element_type=jnp.float32)
    pair = jnp.dot(gathered, w_pair, preferred_element_type=jnp.float32)

    row_ids = jnp.arange(rows, dtype=jnp.int32)
    slab_ids = slab ^ jnp.arange(slabs, dtype=jnp.int32)

    def places_of(at_side, at_sp):
        starts = ((slab_ids * 2 + at_side) * sp_count + at_sp) * rows
        return (starts[:, None] + row_ids[None, :]).reshape(-1)

    places = places_of(side, sp_place)
    cosine, sine_part = angles_of(places, head_dim)

    def half(a, lo, hi):
        return jnp.where(
            side == 0,
            jnp.concatenate([own[:, lo:hi], pair[:, lo:hi]], axis=1),
            jnp.concatenate([pair[:, lo:hi], own[:, lo:hi]], axis=1),
        ).astype(jnp.bfloat16)

    key_raw = half(0, head_dim, head_dim + half_dim)
    value_rows = half(0, head_dim + half_dim, head_dim + 2 * half_dim)
    key_rows = rotate(key_raw.astype(jnp.float32), cosine, sine_part).astype(jnp.bfloat16)
    queries = jnp.concatenate(
        [
            rotate(own[:, :head_dim], cosine, sine_part),
            rotate(pair[:, :head_dim], cosine, sine_part),
        ],
        axis=0,
    )
    queries = (queries * PRE_SCALE ** (-0.5)).astype(jnp.bfloat16)

    key_value = jnp.concatenate([key_rows, value_rows], axis=1)
    both = jnp.concatenate([key_value, swap_tp(key_value, 1)], axis=0)
    every = lax.all_gather(both, "sp", axis=0, tiled=True)
    key_places = jnp.concatenate(
        [places_of(b, s) for s in range(sp_count) for b in (side, 1 - side)]
    )
    key_docs = doc_index(key_places, doc_ends)
    query_docs = doc_index(places, doc_ends)
    allowed = (key_places[None, :] <= places[:, None]) & (key_docs[None, :] == query_docs[:, None])
    allowed = jnp.concatenate([allowed, allowed], axis=0)
    scores = jnp.einsum(
        "qd,kd->qk", queries, every[:, :head_dim], preferred_element_type=jnp.float32
    )
    largest = jnp.max(jnp.where(allowed, scores, masked_low), axis=1, keepdims=True)
    weights = jnp.where(allowed, jnp.exp(scores - largest), 0.0)
    denominator = jnp.sum(weights, axis=1, keepdims=True)
    mixed = jnp.dot(
        weights.astype(jnp.bfloat16), every[:, head_dim:], preferred_element_type=jnp.float32
    )
    mixed = (mixed / denominator).astype(jnp.bfloat16)
    count = slabs * rows
    mixed = jnp.concatenate([mixed[:count], mixed[count:]], axis=1)
    first = mixed[:, head_dim : head_dim + out_depth]
    second = mixed[:, head_dim + out_depth :]
    mixed = jnp.concatenate(
        [
            mixed[:, :head_dim],
            jnp.where(sp_place == 0, first, second),
            jnp.where(sp_place == 0, second, first),
        ],
        axis=1,
    )
    w_both = jnp.concatenate([w_out, out_share, out_other], axis=0)
    partial = jnp.dot(mixed, w_both, preferred_element_type=jnp.float32)
    sent = partial.astype(jnp.bfloat16)
    total = partial[:rows]
    for k in range(1, slabs):
        total = total + swap_tp(sent[k * rows : (k + 1) * rows], 2 * k).astype(jnp.float32)
    return total.astype(jnp.bfloat16)


def solution(mesh):
    placed = (
        P(("groups", "tp", "sp"), None),
        P(None, "tp"),
        P(None, "tp"),
        P(None, "tp"),
        P("tp", None),
        P("groups"),
    )
    return jax.shard_map(
        local,
        mesh=mesh,
        in_specs=placed,
        out_specs=P(("groups", "tp", "sp"), None),
        check_vma=False,
    )
```

```python
import jax
import jax.numpy as jnp
from jax import lax
from jax.experimental import pallas as pl
from jax.experimental.pallas import tpu as pltpu
from jax.sharding import PartitionSpec as P

PRE_SCALE = 144

masked_low = -1e30


def swap_tp(block, flip, only=None):
    count = lax.axis_size("tp")
    route = [(t, t ^ flip) for t in range(count) if only is None or only(t)]
    return lax.ppermute(block, "tp", route)


def swap_sp(block):
    count = lax.axis_size("sp")
    return lax.ppermute(block, "sp", [(s, s ^ 1) for s in range(count)])


def swap_in_slab(block, group_flip, tp_flip):
    groups = lax.axis_size("groups")
    count = lax.axis_size("tp")
    route = [
        (g * count + t, (g ^ group_flip) * count + (t ^ tp_flip))
        for g in range(groups)
        for t in range(count)
    ]
    return lax.ppermute(block, ("groups", "tp"), route)


def fence(*values):
    return lax.optimization_barrier(values)


def angles_of(places, head_dim):
    half_width = head_dim // 2
    spread = jnp.power(
        10000.0, -(jnp.arange(half_width, dtype=jnp.float32) * (2.0 / head_dim))
    )
    angles = places.astype(jnp.float32)[:, None] * spread[None, :]
    return jnp.cos(angles), jnp.sin(angles)


def rotate(matrix, cosine, sine_part):
    half_width = matrix.shape[1] // 2
    lower_part = matrix[:, :half_width]
    upper_part = matrix[:, half_width:]
    return jnp.concatenate(
        [
            lower_part * cosine - upper_part * sine_part,
            upper_part * cosine + lower_part * sine_part,
        ],
        axis=1,
    )


def doc_index(places, doc_ends):
    return jnp.sum((places[:, None] >= doc_ends[None, :]).astype(jnp.int32), axis=1)


def gather_slabs(tokens, slabs, slab):
    if slabs != 4:
        return [tokens] + [swap_tp(tokens, 2 * k) for k in range(1, slabs)]
    far = swap_tp(tokens, 4)
    near = swap_tp(tokens, 2)
    far, again = fence(far, tokens)
    inner = lambda t: (t >> 1) in (1, 2)
    relayed = swap_tp(far, 2, inner)
    middle = swap_tp(again, 6, inner)
    last = jnp.where((slab == 1) | (slab == 2), middle, relayed)
    return [tokens, near, far, last]


def project_kernel(peers, *refs):
    stacked, pieces, outs = refs[:peers], refs[peers:-peers], refs[-peers:]
    depth = pieces[0].shape[0]
    total = None
    for i, piece in enumerate(pieces):
        rows = jnp.concatenate([m[:, i * depth : (i + 1) * depth] for m in stacked], axis=0)
        term = jnp.dot(rows, piece[...], preferred_element_type=jnp.float32)
        total = term if total is None else total + term
    count = stacked[0].shape[0]
    for i, out in enumerate(outs):
        out[...] = total[i * count : (i + 1) * count].astype(out.dtype)


def project(stacked, pieces):
    rows, inner = stacked[0].shape
    depth, width = pieces[0].shape
    peers = len(stacked)
    step = width // 3 if width % 384 == 0 else width
    return pl.pallas_call(
        lambda *refs: project_kernel(peers, *refs),
        grid=(width // step,),
        in_specs=[pl.BlockSpec((rows, inner), lambda i: (0, 0))] * peers
        + [pl.BlockSpec((depth, step), lambda i: (0, i))] * len(pieces),
        out_specs=[pl.BlockSpec((rows, step), lambda i: (0, i))] * peers,
        out_shape=[jax.ShapeDtypeStruct((rows, width), jnp.bfloat16)] * peers,
        name="project",
    )(*stacked, *pieces)


def local(tokens, w_query, w_key, w_value, w_out, doc_lengths):
    rows, width = tokens.shape
    tp_count = lax.axis_size("tp")
    sp_count = lax.axis_size("sp")
    sp_place = lax.axis_index("sp")
    tp_place = lax.axis_index("tp")
    slabs = tp_count // 2
    slab = tp_place // 2
    side = tp_place % 2
    head_dim = w_query.shape[1]
    half_dim = w_key.shape[1]

    depth = width // sp_count
    w_own = jnp.concatenate([w_query, w_key, w_value], axis=1)
    share = jnp.concatenate(
        [
            lax.dynamic_slice_in_dim(w, sp_place * depth, depth, 0)
            for w in (w_query, w_key, w_value)
        ],
        axis=1,
    )
    blocks = gather_slabs(tokens, slabs, slab)
    share_here, out_weight, doc_lengths = fence(share, w_out, doc_lengths)
    share = swap_tp(share_here, 1)
    doc_ends = jnp.cumsum(doc_lengths)
    other = swap_sp(share)
    low = jnp.where(sp_place == 0, share, other)
    high = jnp.where(sp_place == 0, other, share)
    w_pair = jnp.concatenate([low, high], axis=0)

    quarter = w_out.shape[1] // 4
    mine = (lax.axis_index("groups") % 2) * 2 + side
    route = [
        ((t * sp_count + s), ((t ^ 1) * sp_count + s))
        for t in range(tp_count)
        for s in range(sp_count)
        if s == t % 2
    ]
    out_sent = lax.dynamic_slice_in_dim(out_weight, (mine ^ 1) * quarter, quarter, 1)
    out_kept = lax.dynamic_slice_in_dim(out_weight, mine * quarter, quarter, 1)
    out_came = lax.ppermute(out_sent, ("tp", "sp"), route)
    out_head = jnp.where(side == sp_place, out_kept, out_came)
    out_head = fence(out_head, blocks[-1])[0]
    out_blocks = gather_slabs(out_head, slabs, slab)
    out_pieces = []
    for piece in out_blocks:
        out_pieces += [piece, swap_sp(piece)]

    gathered = jnp.concatenate(blocks, axis=0)
    own = jnp.dot(gathered, w_own, preferred_element_type=jnp.float32)
    pair = jnp.dot(gathered, w_pair, preferred_element_type=jnp.float32)

    row_ids = jnp.arange(rows, dtype=jnp.int32)
    slab_ids = slab ^ jnp.arange(slabs, dtype=jnp.int32)

    def places_of(at_side, at_sp):
        starts = ((slab_ids * 2 + at_side) * sp_count + at_sp) * rows
        return (starts[:, None] + row_ids[None, :]).reshape(-1)

    places = places_of(side, sp_place)
    cosine, sine_part = angles_of(places, head_dim)

    def half(a, lo, hi):
        return jnp.where(
            side == 0,
            jnp.concatenate([own[:, lo:hi], pair[:, lo:hi]], axis=1),
            jnp.concatenate([pair[:, lo:hi], own[:, lo:hi]], axis=1),
        ).astype(jnp.bfloat16)

    key_raw = half(0, head_dim, head_dim + half_dim)
    value_rows = half(0, head_dim + half_dim, head_dim + 2 * half_dim)
    key_rows = rotate(key_raw.astype(jnp.float32), cosine, sine_part).astype(jnp.bfloat16)
    queries = jnp.concatenate(
        [
            rotate(own[:, :head_dim], cosine, sine_part),
            rotate(pair[:, :head_dim], cosine, sine_part),
        ],
        axis=0,
    )
    queries = (queries * PRE_SCALE ** (-0.5)).astype(jnp.bfloat16)

    key_value = jnp.concatenate([key_rows, value_rows], axis=1)
    both = jnp.concatenate([key_value, swap_tp(key_value, 1)], axis=0)
    every = lax.all_gather(both, "sp", axis=0, tiled=True)
    key_places = jnp.concatenate(
        [places_of(b, s) for s in range(sp_count) for b in (side, 1 - side)]
    )
    key_docs = doc_index(key_places, doc_ends)
    query_docs = doc_index(places, doc_ends)
    allowed = (key_places[None, :] <= places[:, None]) & (key_docs[None, :] == query_docs[:, None])
    allowed = jnp.concatenate([allowed, allowed], axis=0)
    scores = jnp.einsum(
        "qd,kd->qk", queries, every[:, :head_dim], preferred_element_type=jnp.float32
    )
    largest = jnp.max(jnp.where(allowed, scores, masked_low), axis=1, keepdims=True)
    weights = jnp.where(allowed, jnp.exp(scores - largest), 0.0)
    denominator = jnp.sum(weights, axis=1, keepdims=True)
    mixed = jnp.dot(
        weights.astype(jnp.bfloat16), every[:, head_dim:], preferred_element_type=jnp.float32
    )
    mixed = (mixed / denominator).astype(jnp.bfloat16)
    count = slabs * rows
    lower, upper = mixed[:count], mixed[count:]
    straight = side == sp_place
    mixed = jnp.concatenate(
        [jnp.where(straight, lower, upper), jnp.where(straight, upper, lower)], axis=1
    )
    parts = [mixed[:rows]]
    for k in range(1, slabs):
        parts.append(swap_tp(mixed[k * rows : (k + 1) * rows], 2 * k))
    merged = jnp.concatenate(parts, axis=1)
    peers = ((0, 0), (0, 1), (1, 0), (1, 1))
    stacked = [merged] + [swap_in_slab(merged, g, t) for g, t in peers[1:]]
    outs = project(stacked, out_pieces)
    outs = [outs[0]] + [swap_in_slab(o, g, t) for o, (g, t) in zip(outs[1:], peers[1:])]
    swap_y = side == 1
    swap_x = lax.axis_index("groups") % 2 == 1
    rows_of = lambda a, b: (jnp.where(swap_y, b, a), jnp.where(swap_y, a, b))
    near = rows_of(outs[0], outs[1])
    far = rows_of(outs[2], outs[3])
    return jnp.concatenate(
        [jnp.where(swap_x, f, n) for n, f in zip(near, far)]
        + [jnp.where(swap_x, n, f) for n, f in zip(near, far)],
        axis=1,
    )


def solution(mesh):
    placed = (
        P(("groups", "tp", "sp"), None),
        P(None, "tp"),
        P(None, "tp"),
        P(None, "tp"),
        P("tp", None),
        P("groups"),
    )
    return jax.shard_map(
        local,
        mesh=mesh,
        in_specs=placed,
        out_specs=P(("groups", "tp", "sp"), None),
        check_vma=False,
    )
```

```python
import jax
import jax.numpy as jnp
from jax import lax
from jax.experimental import pallas as pl
from jax.experimental.pallas import tpu as pltpu
from jax.sharding import PartitionSpec as P

PRE_SCALE = 144

masked_low = -1e30


def swap_tp(block, flip, only=None):
    count = lax.axis_size("tp")
    route = [(t, t ^ flip) for t in range(count) if only is None or only(t)]
    return lax.ppermute(block, "tp", route)


def swap_sp(block):
    count = lax.axis_size("sp")
    return lax.ppermute(block, "sp", [(s, s ^ 1) for s in range(count)])


def swap_in_slab(block, group_flip, tp_flip):
    groups = lax.axis_size("groups")
    count = lax.axis_size("tp")
    route = [
        (g * count + t, (g ^ group_flip) * count + (t ^ tp_flip))
        for g in range(groups)
        for t in range(count)
    ]
    return lax.ppermute(block, ("groups", "tp"), route)


def fence(*values):
    return lax.optimization_barrier(values)


def angles_of(places, head_dim):
    half_width = head_dim // 2
    spread = jnp.power(
        10000.0, -(jnp.arange(half_width, dtype=jnp.float32) * (2.0 / head_dim))
    )
    angles = places.astype(jnp.float32)[:, None] * spread[None, :]
    return jnp.cos(angles), jnp.sin(angles)


def rotate(matrix, cosine, sine_part):
    half_width = matrix.shape[1] // 2
    lower_part = matrix[:, :half_width]
    upper_part = matrix[:, half_width:]
    return jnp.concatenate(
        [
            lower_part * cosine - upper_part * sine_part,
            upper_part * cosine + lower_part * sine_part,
        ],
        axis=1,
    )


def doc_index(places, doc_ends):
    return jnp.sum((places[:, None] >= doc_ends[None, :]).astype(jnp.int32), axis=1)


def gather_first(block, slabs):
    if slabs != 4:
        return [swap_tp(block, 2 * k) for k in range(1, slabs)]
    return [swap_tp(block, 2), swap_tp(block, 4)]


def gather_last(block, came, slabs):
    if slabs != 4:
        return ()
    inner = lambda t: (t >> 1) in (1, 2)
    relayed = swap_tp(came[1], 2, inner)
    return (swap_tp(block, 6, inner), relayed)


def pick_last(last, slab):
    return [jnp.where((slab == 1) | (slab == 2), last[0], last[1])] if last else []


def project_kernel(peers, *refs):
    stacked, pieces, outs = refs[:peers], refs[peers:-peers], refs[-peers:]
    depth = pieces[0].shape[0]
    total = None
    for i, piece in enumerate(pieces):
        rows = jnp.concatenate([m[:, i * depth : (i + 1) * depth] for m in stacked], axis=0)
        term = jnp.dot(rows, piece[...], preferred_element_type=jnp.float32)
        total = term if total is None else total + term
    count = stacked[0].shape[0]
    for i, out in enumerate(outs):
        out[...] = total[i * count : (i + 1) * count].astype(out.dtype)


def project(stacked, pieces):
    rows, _ = stacked[0].shape
    _, width = pieces[0].shape
    peers = len(stacked)
    whole = pl.BlockSpec(memory_space=pltpu.VMEM)
    return pl.pallas_call(
        lambda *refs: project_kernel(peers, *refs),
        in_specs=[whole] * (peers + len(pieces)),
        out_specs=[whole] * peers,
        out_shape=[jax.ShapeDtypeStruct((rows, width), jnp.bfloat16)] * peers,
        name="project",
    )(*stacked, *pieces)


def local(tokens, w_query, w_key, w_value, w_out, doc_lengths):
    rows, width = tokens.shape
    tp_count = lax.axis_size("tp")
    sp_count = lax.axis_size("sp")
    sp_place = lax.axis_index("sp")
    tp_place = lax.axis_index("tp")
    slabs = tp_count // 2
    slab = tp_place // 2
    side = tp_place % 2
    head_dim = w_query.shape[1]
    half_dim = w_key.shape[1]

    depth = width // sp_count
    quarter = w_out.shape[1] // 4
    mine = (lax.axis_index("groups") % 2) * 2 + side
    wkv_own = jnp.concatenate([w_key.T, w_value.T], axis=0)
    share_q = lax.dynamic_slice_in_dim(w_query, sp_place * depth, depth, 0)
    share_kv = lax.dynamic_slice_in_dim(wkv_own, sp_place * depth, depth, 1)
    out_sent = lax.dynamic_slice_in_dim(w_out, (mine ^ 1) * quarter, quarter, 1)
    share_q, share_kv, out_sent, tokens, doc_lengths = fence(
        share_q, share_kv, out_sent, tokens, doc_lengths
    )
    came = gather_first(tokens, slabs)
    route = [
        ((t * sp_count + s), ((t ^ 1) * sp_count + s))
        for t in range(tp_count)
        for s in range(sp_count)
        if s == t % 2
    ]
    out_came = lax.ppermute(out_sent, ("tp", "sp"), route)
    came_q = swap_tp(share_q, 1)
    came_kv = swap_tp(share_kv, 1)
    other_q = swap_sp(came_q)
    other_kv = swap_sp(came_kv)
    ordered = lambda a, b, axis: jnp.concatenate(
        [jnp.where(sp_place == 0, a, b), jnp.where(sp_place == 0, b, a)], axis=axis
    )
    wq_pair = ordered(came_q, other_q, 0)
    wkv_pair = ordered(came_kv, other_kv, 1)
    out_kept = lax.dynamic_slice_in_dim(w_out, mine * quarter, quarter, 1)
    out_head = jnp.where(side == sp_place, out_kept, out_came)

    if slabs == 4:
        again, came[1] = fence(tokens, came[1])
        last = gather_last(again, came, slabs)
    else:
        last = ()
    blocks = [tokens] + came + pick_last(last, slab)
    out_first = gather_first(out_head, slabs)

    plain = lambda a, w: jnp.dot(a, w, preferred_element_type=jnp.float32)
    turned = lambda a, w: jnp.einsum("rk,ck->rc", a, w, preferred_element_type=jnp.float32)
    head = jnp.concatenate([tokens] + came, axis=0)
    tail = blocks[1 + len(came) :]

    def over(product, weight):
        results = [product(block, weight) for block in [head] + tail]
        return jnp.concatenate(results, axis=0) if tail else results[0]

    own_q, own_kv = over(plain, w_query), over(turned, wkv_own)
    pair_q, pair_kv = over(plain, wq_pair), over(turned, wkv_pair)

    doc_ends = jnp.cumsum(doc_lengths)
    row_ids = jnp.arange(rows, dtype=jnp.int32)
    slab_ids = slab ^ jnp.arange(slabs, dtype=jnp.int32)

    def places_of(at_side, at_sp):
        starts = ((slab_ids * 2 + at_side) * sp_count + at_sp) * rows
        return (starts[:, None] + row_ids[None, :]).reshape(-1)

    places = places_of(side, sp_place)
    cosine, sine_part = angles_of(places, head_dim)

    def half(lo, hi):
        return jnp.where(
            side == 0,
            jnp.concatenate([own_kv[:, lo:hi], pair_kv[:, lo:hi]], axis=1),
            jnp.concatenate([pair_kv[:, lo:hi], own_kv[:, lo:hi]], axis=1),
        ).astype(jnp.bfloat16)

    key_raw = half(0, half_dim)
    value_rows = half(half_dim, 2 * half_dim)
    key_rows = rotate(key_raw.astype(jnp.float32), cosine, sine_part).astype(jnp.bfloat16)
    queries = jnp.concatenate(
        [rotate(own_q, cosine, sine_part), rotate(pair_q, cosine, sine_part)], axis=0
    )
    queries = (queries * PRE_SCALE ** (-0.5)).astype(jnp.bfloat16)

    key_value = jnp.concatenate([key_rows, value_rows], axis=1)
    both = jnp.concatenate([key_value, swap_tp(key_value, 1)], axis=0)
    every = lax.all_gather(both, "sp", axis=0, tiled=True)
    key_places = jnp.concatenate(
        [places_of(b, s) for s in range(sp_count) for b in (side, 1 - side)]
    )
    key_docs = doc_index(key_places, doc_ends)
    query_docs = doc_index(places, doc_ends)
    allowed = (key_places[None, :] <= places[:, None]) & (key_docs[None, :] == query_docs[:, None])
    allowed = jnp.concatenate([allowed, allowed], axis=0)
    scores = jnp.einsum(
        "qd,kd->qk", queries, every[:, :head_dim], preferred_element_type=jnp.float32
    )
    largest = jnp.max(jnp.where(allowed, scores, masked_low), axis=1, keepdims=True)
    weights = jnp.where(allowed, jnp.exp(scores - largest), 0.0)
    denominator = jnp.sum(weights, axis=1, keepdims=True)
    mixed = jnp.dot(
        weights.astype(jnp.bfloat16), every[:, head_dim:], preferred_element_type=jnp.float32
    )
    mixed = (mixed / denominator).astype(jnp.bfloat16)
    count = slabs * rows
    lower, upper = mixed[:count], mixed[count:]
    straight = side == sp_place
    mixed = jnp.concatenate(
        [jnp.where(straight, lower, upper), jnp.where(straight, upper, lower)], axis=1
    )
    parts = [mixed[:rows]]
    for k in range(1, slabs):
        parts.append(swap_tp(mixed[k * rows : (k + 1) * rows], 2 * k))
    out_last = gather_last(out_head, out_first, slabs)
    merged = jnp.concatenate(parts, axis=1)
    peers = ((0, 0), (1, 0), (0, 1), (1, 1))
    stacked = [merged] + [swap_in_slab(merged, g, t) for g, t in peers[1:]]
    if slabs == 4:
        *out_last, stacked[1] = fence(*out_last, stacked[1])
    out_pieces = []
    for piece in [out_head] + out_first + pick_last(out_last, slab):
        out_pieces += [piece, swap_sp(piece)]
    outs = project(stacked, out_pieces)
    outs = [outs[0]] + [swap_in_slab(o, g, t) for o, (g, t) in zip(outs[1:], peers[1:])]
    swap_y = side == 1
    swap_x = lax.axis_index("groups") % 2 == 1
    rows_of = lambda a, b: (jnp.where(swap_y, b, a), jnp.where(swap_y, a, b))
    near = rows_of(outs[0], outs[2])
    far = rows_of(outs[1], outs[3])
    return jnp.concatenate(
        [jnp.where(swap_x, f, n) for n, f in zip(near, far)]
        + [jnp.where(swap_x, n, f) for n, f in zip(near, far)],
        axis=1,
    )


def solution(mesh):
    placed = (
        P(("groups", "tp", "sp"), None),
        P(None, "tp"),
        P(None, "tp"),
        P(None, "tp"),
        P("tp", None),
        P("groups"),
    )

    return jax.shard_map(
        local,
        mesh=mesh,
        in_specs=placed,
        out_specs=P(("groups", "tp", "sp"), None),
        check_vma=False,
    )
```

```python
import jax
import jax.numpy as jnp
from jax import lax
from jax.experimental import pallas as pl
from jax.experimental.pallas import tpu as pltpu
from jax.sharding import PartitionSpec as P

PRE_SCALE = 144

masked_low = -1e30


def swap_tp(block, flip, only=None):
    count = lax.axis_size("tp")
    route = [(t, t ^ flip) for t in range(count) if only is None or only(t)]
    return lax.ppermute(block, "tp", route)


def swap_sp(block):
    count = lax.axis_size("sp")
    return lax.ppermute(block, "sp", [(s, s ^ 1) for s in range(count)])


def swap_in_slab(block, group_flip, tp_flip):
    groups = lax.axis_size("groups")
    count = lax.axis_size("tp")
    route = [
        (g * count + t, (g ^ group_flip) * count + (t ^ tp_flip))
        for g in range(groups)
        for t in range(count)
    ]
    return lax.ppermute(block, ("groups", "tp"), route)


def fence(*values):
    return lax.optimization_barrier(values)


def angles_of(places, head_dim):
    half_width = head_dim // 2
    spread = jnp.power(
        10000.0, -(jnp.arange(half_width, dtype=jnp.float32) * (2.0 / head_dim))
    )
    angles = places.astype(jnp.float32)[:, None] * spread[None, :]
    return jnp.cos(angles), jnp.sin(angles)


def doc_index(places, doc_ends):
    return jnp.sum((places[:, None] >= doc_ends[None, :]).astype(jnp.int32), axis=1)


def gather_first(block, slabs):
    if slabs != 4:
        return [swap_tp(block, 2 * k) for k in range(1, slabs)]
    return [swap_tp(block, 2), swap_tp(block, 4)]


def gather_last(block, came):
    inner = lambda t: (t >> 1) in (1, 2)
    relayed = swap_tp(came[1], 2, inner)
    return [swap_tp(block, 6, inner), relayed]


def call(kernel, shapes, flags, operands, scratch=()):
    size = sum(x.size * x.dtype.itemsize for x in operands)
    params = None
    if size < 16 << 20:
        operands = [pltpu.with_memory_space_constraint(x, pltpu.VMEM) for x in operands]
        params = pltpu.CompilerParams(vmem_limit_bytes=16 << 20)
    whole = pl.BlockSpec(memory_space=pltpu.VMEM)
    return pl.pallas_call(
        kernel,
        in_specs=[pl.BlockSpec(memory_space=pltpu.SMEM)] + [whole] * len(operands),
        out_specs=[whole] * len(shapes),
        out_shape=[jax.ShapeDtypeStruct(*shape) for shape in shapes],
        scratch_shapes=list(scratch),
        compiler_params=params,
    )(flags, *operands)


def plain(a, w):
    return jnp.dot(a, w, preferred_element_type=jnp.float32)


def turned(a, w):
    return lax.dot_general(a, w, (((1,), (1,)), ((), ())), preferred_element_type=jnp.float32)


def rows_at(blocks, offset, size):
    parts = [block[:, pl.ds(pl.multiple_of(offset, 128), size)] for block in blocks]
    return jnp.concatenate(parts, axis=0) if len(parts) > 1 else parts[0]


def pair_query(blocks, quarters, sp, group):
    size = quarters[0].shape[0]
    total = None
    for i, weight in enumerate(quarters):
        at = (sp ^ (i >> 1)) * 2 + (group ^ (i & 1))
        term = plain(rows_at(blocks, at * size, size), weight[...])
        total = term if total is None else total + term
    return total


def early_kernel(flags, *refs):
    blocks, (w_query, w_kv), quarters, out = refs[:-7], refs[-7:-5], refs[-5:-1], refs[-1]
    head = w_query.shape[1]
    rows = jnp.concatenate([block[...] for block in blocks], axis=0)
    out[:, :head] = plain(rows, w_query[...])
    out[:, head : 2 * head] = turned(rows, w_kv[...])
    out[:, 2 * head :] = pair_query(blocks, quarters, flags[0], flags[3])


def tail_kernel(flags, *refs):
    early, middle, relayed, w_query, w_kv, w_kv_came, w_kv_other, cosine, sine_part = refs[:9]
    quarters, blocks = refs[9:13], refs[13:-3]
    queries, key_value, last = refs[-3:]
    sp, side, inner, group = flags[0], flags[1], flags[2], flags[3]
    head = w_query.shape[1]
    half_head = head // 2
    last[...] = jnp.where(inner != 0, middle[...], relayed[...])
    depth = w_kv_came.shape[1]
    join = lambda a, b: jnp.concatenate([a, b], axis=0)
    own_query = join(early[:, :head], plain(last[...], w_query[...]))
    own_kv = join(early[:, head : 2 * head], turned(last[...], w_kv[...]))
    pair_q = join(early[:, 2 * head :], pair_query([last], quarters, sp, group))
    every = list(blocks) + [last]
    pair_kv = turned(rows_at(every, sp * depth, depth), w_kv_came[...]) + turned(
        rows_at(every, (1 - sp) * depth, depth), w_kv_other[...]
    )
    spin = lambda v: v * cosine[...] + pltpu.roll(v, half_head, 1) * sine_part[...]
    scale = PRE_SCALE ** (-0.5)
    count = own_query.shape[0]
    queries[:count] = (spin(own_query) * scale).astype(queries.dtype)
    queries[count:] = (spin(pair_q) * scale).astype(queries.dtype)
    lane = lax.broadcasted_iota(jnp.int32, own_kv.shape, 1)
    low = lane < half_head
    even = side == 0
    first = jnp.where(even, own_kv, pair_kv)
    second = jnp.where(even, pair_kv, own_kv)
    key_raw = jnp.where(low, first, pltpu.roll(second, half_head, 1))
    key_raw = key_raw.astype(jnp.bfloat16).astype(jnp.float32)
    key_value[:, :head] = spin(key_raw).astype(key_value.dtype)
    value = jnp.where(low, pltpu.roll(first, half_head, 1), second)
    key_value[:, head:] = value.astype(key_value.dtype)


def project_kernel(peers, flags, *refs):
    stacked, pieces, outs = refs[:peers], refs[peers:-peers], refs[-peers:]
    count, width = outs[0].shape
    rows = jnp.concatenate([m[...] for m in stacked], axis=0)
    step = 384 if width % 384 == 0 else width
    for at in range(0, width, step):
        weight = jnp.concatenate([p[:, at : at + step] for p in pieces], axis=0)
        total = plain(rows, weight)
        for i, out in enumerate(outs):
            out[:, at : at + step] = total[i * count : (i + 1) * count].astype(out.dtype)


def assemble_kernel(flags, *refs):
    pieces, out = refs[:-1], refs[-1]
    width = pieces[0].shape[1]
    for i, piece in enumerate(pieces):
        at = pl.multiple_of((flags[4] ^ i) * width, 128)
        out[:, pl.ds(at, width)] = piece[...]


def local(tokens, w_query, w_key, w_value, w_out, doc_lengths):
    rows, width = tokens.shape
    tp_count = lax.axis_size("tp")
    sp_count = lax.axis_size("sp")
    sp_place = lax.axis_index("sp")
    tp_place = lax.axis_index("tp")
    slabs = tp_count // 2
    slab = tp_place // 2
    side = tp_place % 2
    head_dim = w_query.shape[1]

    group = lax.axis_index("groups") % 2
    depth = width // sp_count
    quarter = w_out.shape[1] // 4
    mine = group * 2 + side
    inner = ((slab == 1) | (slab == 2)).astype(jnp.int32)
    flags = jnp.stack([sp_place, side, inner, group, mine]).astype(jnp.int32)
    wkv_own = jnp.concatenate([w_key.T, w_value.T], axis=0)
    share_q = lax.dynamic_slice_in_dim(
        w_query, (sp_place * 2 + group) * (depth // 2), depth // 2, 0
    )
    share_kv = lax.dynamic_slice_in_dim(wkv_own, sp_place * depth, depth, 1)
    out_sent = lax.dynamic_slice_in_dim(w_out, (mine ^ 1) * quarter, quarter, 1)
    share_q, share_kv, out_sent, tokens, doc_lengths, out_weight = fence(
        share_q, share_kv, out_sent, tokens, doc_lengths, w_out
    )
    came = gather_first(tokens, slabs)
    route = [
        ((t * sp_count + s), ((t ^ 1) * sp_count + s))
        for t in range(tp_count)
        for s in range(sp_count)
        if s == t % 2
    ]
    out_came = lax.ppermute(out_sent, ("tp", "sp"), route)
    came_q = swap_tp(share_q, 1)
    cross_q = swap_in_slab(came_q, 1, 0)
    came_kv = swap_tp(share_kv, 1)
    other_kv = swap_sp(came_kv)
    quarters = [came_q, cross_q, swap_sp(came_q), swap_sp(cross_q)]
    out_kept = lax.dynamic_slice_in_dim(out_weight, mine * quarter, quarter, 1)
    out_head = jnp.where(side == sp_place, out_kept, out_came)
    out_first = gather_first(out_head, slabs)

    if slabs == 4:
        last = gather_last(tokens, came)
        firsts = [tokens] + came
    else:
        last = [came[-1], came[-1]]
        firsts = [tokens] + came[:-1]
    early = call(
        early_kernel,
        [((len(firsts) * rows, 3 * head_dim), jnp.float32)],
        flags,
        [*firsts, w_query, wkv_own, *quarters],
    )[0]

    doc_ends = jnp.cumsum(doc_lengths)
    row_ids = jnp.arange(rows, dtype=jnp.int32)
    slab_ids = slab ^ jnp.arange(slabs, dtype=jnp.int32)

    def places_of(at_side, at_sp):
        starts = ((slab_ids * 2 + at_side) * sp_count + at_sp) * rows
        return (starts[:, None] + row_ids[None, :]).reshape(-1)

    places = places_of(side, sp_place)
    cosine, sine_part = angles_of(places, head_dim)
    cosine = jnp.concatenate([cosine, cosine], axis=1)
    sine_part = jnp.concatenate([-sine_part, sine_part], axis=1)
    total_rows = slabs * rows
    queries, key_value = call(
        tail_kernel,
        [((2 * total_rows, head_dim), jnp.bfloat16), ((total_rows, 2 * head_dim), jnp.bfloat16)],
        flags,
        [early, *last, w_query, wkv_own, came_kv, other_kv, cosine, sine_part]
        + quarters
        + firsts,
        [pltpu.VMEM((rows, width), jnp.bfloat16)],
    )
    both = jnp.concatenate([key_value, swap_tp(key_value, 1)], axis=0)
    every = lax.all_gather(both, "sp", axis=0, tiled=True)
    key_places = jnp.concatenate(
        [places_of(b, s) for s in range(sp_count) for b in (side, 1 - side)]
    )
    key_docs = doc_index(key_places, doc_ends)
    query_docs = doc_index(places, doc_ends)
    allowed = (key_places[None, :] <= places[:, None]) & (key_docs[None, :] == query_docs[:, None])
    allowed = jnp.concatenate([allowed, allowed], axis=0)
    scores = jnp.einsum(
        "qd,kd->qk", queries, every[:, :head_dim], preferred_element_type=jnp.float32
    )
    largest = jnp.max(jnp.where(allowed, scores, masked_low), axis=1, keepdims=True)
    weights = jnp.where(allowed, jnp.exp(scores - largest), 0.0)
    denominator = jnp.sum(weights, axis=1, keepdims=True)
    mixed = jnp.dot(
        weights.astype(jnp.bfloat16), every[:, head_dim:], preferred_element_type=jnp.float32
    )
    mixed = (mixed / denominator).astype(jnp.bfloat16)
    count = slabs * rows
    lower, upper = mixed[:count], mixed[count:]
    straight = side == sp_place
    mixed = jnp.concatenate(
        [jnp.where(straight, lower, upper), jnp.where(straight, upper, lower)], axis=1
    )
    parts = [mixed[:rows]]
    for k in range(1, slabs):
        parts.append(swap_tp(mixed[k * rows : (k + 1) * rows], 2 * k))
    out_last = gather_last(out_head, out_first) if slabs == 4 else []
    merged = jnp.concatenate(parts, axis=1)
    peers = ((0, 0), (1, 0), (0, 1), (1, 1))
    stacked = [merged] + [swap_in_slab(merged, g, t) for g, t in peers[1:]]
    if slabs == 4:
        *out_last, stacked[1] = fence(*out_last, stacked[1])
    out_pieces = []
    picked = [jnp.where(inner != 0, *out_last)] if out_last else []
    for piece in [out_head] + out_first + picked:
        out_pieces += [piece, swap_sp(piece)]
    outs = call(
        lambda *refs: project_kernel(len(peers), *refs),
        [((rows, quarter), jnp.bfloat16)] * len(peers),
        flags,
        stacked + out_pieces,
    )
    outs = [outs[0]] + [swap_in_slab(o, g, t) for o, (g, t) in zip(outs[1:], peers[1:])]
    pieces = [outs[0], outs[2], outs[1], outs[3]]
    return call(assemble_kernel, [((rows, width), jnp.bfloat16)], flags, pieces)[0]


def solution(mesh):
    placed = (
        P(("groups", "tp", "sp"), None),
        P(None, "tp"),
        P(None, "tp"),
        P(None, "tp"),
        P("tp", None),
        P("groups"),
    )

    return jax.shard_map(
        local,
        mesh=mesh,
        in_specs=placed,
        out_specs=P(("groups", "tp", "sp"), None),
        check_vma=False,
    )
```

```python
import jax
import jax.numpy as jnp
from jax import lax
from jax.experimental import pallas as pl
from jax.experimental.pallas import tpu as pltpu
from jax.sharding import PartitionSpec as P

PRE_SCALE = 144

masked_low = -1e30


def swap_tp(block, flip, only=None):
    count = lax.axis_size("tp")
    route = [(t, t ^ flip) for t in range(count) if only is None or only(t)]
    return lax.ppermute(block, "tp", route)


def swap_sp(block):
    count = lax.axis_size("sp")
    return lax.ppermute(block, "sp", [(s, s ^ 1) for s in range(count)])


def swap_by_core(block, flips, only=lambda t: True):
    count, cores = lax.axis_size("tp"), lax.axis_size("sp")
    route = [
        (t * cores + s, (t ^ flips[s]) * cores + s)
        for t in range(count)
        for s in range(cores)
        if only(t)
    ]
    return lax.ppermute(block, ("tp", "sp"), route)


def swap_in_slab(block, group_flip, tp_flip):
    groups = lax.axis_size("groups")
    count = lax.axis_size("tp")
    route = [
        (g * count + t, (g ^ group_flip) * count + (t ^ tp_flip))
        for g in range(groups)
        for t in range(count)
    ]
    return lax.ppermute(block, ("groups", "tp"), route)


def fence(*values):
    return lax.optimization_barrier(values)


def call(kernel, shapes, flags, operands, scratch=(), outs=pltpu.VMEM):
    size = sum(x.size * x.dtype.itemsize for x in operands)
    params = None
    if size < 16 << 20:
        operands = [pltpu.with_memory_space_constraint(x, pltpu.VMEM) for x in operands]
        params = pltpu.CompilerParams(vmem_limit_bytes=16 << 20)
    whole = pl.BlockSpec(memory_space=pltpu.VMEM)
    return pl.pallas_call(
        kernel,
        in_specs=[pl.BlockSpec(memory_space=pltpu.SMEM)] + [whole] * len(operands),
        out_specs=[pl.BlockSpec(memory_space=outs)] * len(shapes),
        out_shape=[jax.ShapeDtypeStruct(*shape) for shape in shapes],
        scratch_shapes=list(scratch),
        compiler_params=params,
    )(flags, *operands)


def plain(a, w):
    return jnp.dot(a, w, preferred_element_type=jnp.float32)


def turned(a, w):
    return lax.dot_general(a, w, (((1,), (1,)), ((), ())), preferred_element_type=jnp.float32)


def rows_at(blocks, offset, size):
    parts = [block[:, pl.ds(pl.multiple_of(offset, 128), size)] for block in blocks]
    return jnp.concatenate(parts, axis=0) if len(parts) > 1 else parts[0]


def products(blocks, weights, sp, group):
    w_query, w_kv, kv_came, kv_other, *quarters = weights
    rows = jnp.concatenate([block[...] for block in blocks], axis=0)
    own_query = plain(rows, w_query[...])
    own_kv = turned(rows, w_kv[...])
    size = quarters[0].shape[0]
    pair_query = None
    for i, weight in enumerate(quarters):
        at = (sp ^ (i >> 1)) * 2 + (group ^ (i & 1))
        term = plain(rows_at(blocks, at * size, size), weight[...])
        pair_query = term if pair_query is None else pair_query + term
    depth = kv_came.shape[1]
    pair_kv = turned(rows_at(blocks, sp * depth, depth), kv_came[...]) + turned(
        rows_at(blocks, (1 - sp) * depth, depth), kv_other[...]
    )
    return own_query, own_kv, pair_query, pair_kv


def early_kernel(flags, *refs):
    blocks, weights, out = refs[:-9], refs[-9:-1], refs[-1]
    head = weights[0].shape[1]
    for i, part in enumerate(products(blocks, weights, flags[0], flags[3])):
        out[:, i * head : (i + 1) * head] = part


def tail_kernel(flags, early, middle, relayed, cosine, sine_part, *refs):
    weights, (queries, key_value, last) = refs[:8], refs[8:]
    side, inner = flags[1], flags[2]
    head = weights[0].shape[1]
    half_head = head // 2
    last[...] = jnp.where(inner != 0, middle[...], relayed[...])
    late = products([last], weights, flags[0], flags[3])
    join = lambda i: jnp.concatenate([early[:, i * head : (i + 1) * head], late[i]], axis=0)
    own_query, own_kv, pair_query, pair_kv = [join(i) for i in range(4)]
    spin = lambda v: v * cosine[...] + pltpu.roll(v, half_head, 1) * sine_part[...]
    scale = PRE_SCALE ** (-0.5)
    count = own_query.shape[0]
    queries[:count] = (spin(own_query) * scale).astype(queries.dtype)
    queries[count:] = (spin(pair_query) * scale).astype(queries.dtype)
    lane = lax.broadcasted_iota(jnp.int32, own_kv.shape, 1)
    low = lane < half_head
    even = side == 0
    first = jnp.where(even, own_kv, pair_kv)
    second = jnp.where(even, pair_kv, own_kv)
    key_raw = jnp.where(low, first, pltpu.roll(second, half_head, 1))
    key_raw = key_raw.astype(jnp.bfloat16).astype(jnp.float32)
    key_value[:, :head] = spin(key_raw).astype(key_value.dtype)
    value = jnp.where(low, pltpu.roll(first, half_head, 1), second)
    key_value[:, head:] = value.astype(key_value.dtype)


def project_kernel(peers, split, flags, *refs):
    stacked, pieces, outs = refs[:peers], list(refs[peers:-peers]), refs[-peers:]
    count, width = outs[0].shape
    rows = jnp.concatenate([m[...] for m in stacked], axis=0)
    step = 384 if width % 384 == 0 else width
    received = flags[2] != flags[0]
    for at in range(0, width, step):
        parts = [p[:, at : at + step] for p in pieces]
        if split:
            parts[-2:] = [jnp.where(received, parts[-2], parts[-1])]
        total = plain(rows, jnp.concatenate(parts, axis=0))
        for i, out in enumerate(outs):
            out[:, at : at + step] = total[i * count : (i + 1) * count].astype(out.dtype)


def assemble_kernel(flags, *refs):
    pieces, out, sems = refs[:-2], refs[-2], refs[-1]
    width = pieces[0].shape[1]
    copies = []
    for i, piece in enumerate(pieces):
        at = pl.multiple_of((flags[4] ^ i) * width, 128)
        copies.append(pltpu.make_async_copy(piece, out.at[:, pl.ds(at, width)], sems.at[i]))
        copies[-1].start()
    for copy in copies:
        copy.wait()


def local(tokens, w_query, w_key, w_value, w_out, doc_lengths):
    rows, width = tokens.shape
    tp_count = lax.axis_size("tp")
    sp_count = lax.axis_size("sp")
    sp_place = lax.axis_index("sp")
    tp_place = lax.axis_index("tp")
    group = lax.axis_index("groups") % 2
    slabs = tp_count // 2
    slab = tp_place // 2
    side = tp_place % 2
    head_dim = w_query.shape[1]
    short = slabs == 4
    is_inner = lambda t: (t >> 1) in (1, 2)

    if short:
        far = swap_tp(tokens, 4)
        middle = swap_tp(tokens, 6, is_inner)
        near = swap_tp(tokens, 2)
        relayed = swap_tp(far, 2, is_inner)
        firsts, last = [tokens, near, far], [middle, relayed]
    else:
        came = [swap_tp(tokens, 2 * k) for k in range(1, slabs)]
        firsts, last = [tokens] + came[:-1], [came[-1], came[-1]]

    depth = width // sp_count
    quarter = w_out.shape[1] // 4
    mine = group * 2 + side
    inner = ((slab == 1) | (slab == 2)).astype(jnp.int32)
    flags = jnp.stack([sp_place, side, inner, group, mine]).astype(jnp.int32)
    w_kv = jnp.concatenate([w_key.T, w_value.T], axis=0)
    share_q = lax.dynamic_slice_in_dim(
        w_query, (sp_place * 2 + group) * (depth // 2), depth // 2, 0
    )
    share_kv = lax.dynamic_slice_in_dim(w_kv, sp_place * depth, depth, 1)
    share_q, share_kv, doc_lengths, w_out = fence(share_q, share_kv, doc_lengths, w_out)
    came_q = swap_tp(share_q, 1)
    cross_q = swap_in_slab(came_q, 1, 0)
    came_kv = swap_tp(share_kv, 1)
    half_rows = head_dim // sp_count
    out_sent = lax.dynamic_slice(
        w_out, (sp_place * half_rows, (mine ^ 1) * quarter), (half_rows, quarter)
    )
    out_came = swap_tp(out_sent, 1)
    out_other = swap_sp(out_came)
    weights = [w_query, w_kv, came_kv, swap_sp(came_kv), came_q, cross_q]
    weights += [swap_sp(came_q), swap_sp(cross_q)]
    early = call(
        early_kernel, [((len(firsts) * rows, 4 * head_dim), jnp.float32)], flags, firsts + weights
    )[0]

    in_order = lambda a, b, flag: [jnp.where(flag, a, b), jnp.where(flag, b, a)]
    low, high = in_order(out_came, out_other, sp_place == 0)
    out_pair = jnp.concatenate([low, high], axis=0)
    out_kept = lax.dynamic_slice_in_dim(w_out, mine * quarter, quarter, 1)
    out_own = jnp.concatenate(in_order(out_kept, out_pair, side == 0), axis=0)
    if short:
        out_first = swap_by_core(out_own, (2, 4))
        out_swapped = swap_sp(out_first)

    doc_ends = jnp.cumsum(doc_lengths)
    count = slabs * rows

    def place_of(index, flip_side, flip_core):
        at = (slab ^ (index // rows)) * 2 + (side ^ flip_side)
        return (at * sp_count + (sp_place ^ flip_core)) * rows + index % rows

    table = lambda shape, axis: lax.broadcasted_iota(jnp.int32, shape, axis)
    lane = table((count, head_dim), 1)
    row_places = place_of(table((count, head_dim), 0), 0, 0)
    half_head = head_dim // 2
    powers = (lane % half_head).astype(jnp.float32) * (2.0 / head_dim)
    angles = row_places.astype(jnp.float32) * jnp.power(10000.0, -powers)
    cosine = jnp.cos(angles)
    sine_part = jnp.where(lane < half_head, -jnp.sin(angles), jnp.sin(angles))
    places = place_of(jnp.arange(count, dtype=jnp.int32), 0, 0)
    ends = jnp.where(doc_ends[None, :] <= places[:, None], doc_ends[None, :], 0)
    starts = jnp.max(ends, axis=1)
    key_index = table((count, 4 * count), 1)
    key_places = place_of(key_index % count, key_index // count % 2, key_index // count // 2)
    query_places = place_of(table((count, 4 * count), 0), 0, 0)
    allowed = (key_places <= query_places) & (key_places >= starts[:, None])

    queries, key_value = call(
        tail_kernel,
        [((2 * count, head_dim), jnp.bfloat16), ((count, 2 * head_dim), jnp.bfloat16)],
        flags,
        [early, *last, cosine, sine_part] + weights,
        [pltpu.VMEM((rows, width), jnp.bfloat16)],
    )

    beside = swap_tp(key_value, 1)
    every = [key_value, beside, swap_sp(key_value), swap_sp(beside)]
    every = jnp.concatenate(every, axis=0)
    allowed = jnp.concatenate([allowed, allowed], axis=0)
    scores = jnp.einsum(
        "qd,kd->qk", queries, every[:, :head_dim], preferred_element_type=jnp.float32
    )
    largest = jnp.max(jnp.where(allowed, scores, masked_low), axis=1, keepdims=True)
    e = jnp.where(allowed, jnp.exp(scores - largest), 0.0)
    denominator = jnp.sum(e, axis=1, keepdims=True)
    mixed = plain(e.astype(jnp.bfloat16), every[:, head_dim:])
    mixed = (mixed / denominator).astype(jnp.bfloat16)
    mixed = jnp.concatenate(in_order(mixed[:count], mixed[count:], side == 0), axis=1)

    parts = [mixed[:rows]]
    for k in range(1, slabs):
        parts.append(swap_tp(mixed[k * rows : (k + 1) * rows], 2 * k))
    if short:
        parts[1:3] = in_order(parts[1], parts[2], sp_place == 0)
    merged = jnp.concatenate(parts, axis=1)
    peers = ((0, 0), (0, 1), (1, 0), (1, 1))
    stacked = [merged] + [swap_in_slab(merged, g, t) for g, t in peers[1:]]
    if short:
        out_sent = jnp.where(sp_place == 1, out_first, out_own)
        out_last = swap_by_core(out_sent, (6, 2), is_inner)
        out_last, stacked[2] = fence(out_last, stacked[2])
        pieces = [out_own, out_first, out_swapped, out_last, swap_sp(out_last)]
    else:
        pieces = [out_own]
        mine_of = lax.dynamic_slice_in_dim(out_own, sp_place * head_dim, head_dim, 0)
        for k in range(1, slabs):
            piece = swap_tp(mine_of, 2 * k)
            both = in_order(piece, swap_sp(piece), sp_place == 0)
            pieces.append(jnp.concatenate(both, axis=0))
    outs = call(
        lambda *refs: project_kernel(len(peers), short, *refs),
        [((rows, quarter), jnp.bfloat16)] * len(peers),
        flags,
        stacked + pieces,
    )
    outs = [outs[0]] + [swap_in_slab(o, g, t) for o, (g, t) in zip(outs[1:], peers[1:])]
    sems = [pltpu.SemaphoreType.DMA((len(outs),))]
    shape = ((rows, width), jnp.bfloat16)
    return call(assemble_kernel, [shape], flags, outs, sems, pl.ANY)[0]


def solution(mesh):
    placed = (
        P(("groups", "tp", "sp"), None),
        P(None, "tp"),
        P(None, "tp"),
        P(None, "tp"),
        P("tp", None),
        P("groups"),
    )

    return jax.shard_map(
        local,
        mesh=mesh,
        in_specs=placed,
        out_specs=P(("groups", "tp", "sp"), None),
        check_vma=False,
    )
```

```python
import jax
import jax.numpy as jnp
import numpy as np
from jax import lax
from jax.experimental import pallas as pl
from jax.experimental.pallas import tpu as pltpu
from jax.sharding import PartitionSpec as P

PRE_SCALE = 144

masked_low = -1e30


def swap_tp(block, flip, only=None):
    count = lax.axis_size("tp")
    route = [(t, t ^ flip) for t in range(count) if only is None or only(t)]
    return lax.ppermute(block, "tp", route)


def swap_sp(block):
    count = lax.axis_size("sp")
    return lax.ppermute(block, "sp", [(s, s ^ 1) for s in range(count)])


def swap_by_core(block, flips, only=lambda t: True):
    count, cores = lax.axis_size("tp"), lax.axis_size("sp")
    route = [
        (t * cores + s, (t ^ flips[s]) * cores + s)
        for t in range(count)
        for s in range(cores)
        if only(t)
    ]
    return lax.ppermute(block, ("tp", "sp"), route)


def swap_in_slab(block, group_flip, tp_flip):
    groups = lax.axis_size("groups")
    count = lax.axis_size("tp")
    route = [
        (g * count + t, (g ^ group_flip) * count + (t ^ tp_flip))
        for g in range(groups)
        for t in range(count)
    ]
    return lax.ppermute(block, ("groups", "tp"), route)


def fence(*values):
    return lax.optimization_barrier(values)


def call(kernel, shapes, scalars, operands, scratch=(), outs=pltpu.VMEM, far=(), limit=16):
    size = sum(x.size * x.dtype.itemsize for x in operands)
    params = None
    if size < 8 << 20:
        operands = [pltpu.with_memory_space_constraint(x, pltpu.VMEM) for x in operands]
        params = pltpu.CompilerParams(vmem_limit_bytes=limit << 20)
    specs = [pl.BlockSpec(memory_space=pltpu.SMEM)] * len(scalars)
    specs += [pl.BlockSpec(memory_space=pltpu.VMEM)] * len(operands)
    specs += [pl.BlockSpec(memory_space=pl.ANY)] * len(far)
    return pl.pallas_call(
        kernel,
        in_specs=specs,
        out_specs=[pl.BlockSpec(memory_space=outs)] * len(shapes),
        out_shape=[jax.ShapeDtypeStruct(*shape) for shape in shapes],
        scratch_shapes=list(scratch),
        compiler_params=params,
    )(*scalars, *operands, *far)


def plain(a, w):
    return jnp.dot(a, w, preferred_element_type=jnp.float32)


def turned(a, w):
    return lax.dot_general(a, w, (((1,), (1,)), ((), ())), preferred_element_type=jnp.float32)


def rows_at(blocks, offset, size):
    parts = [block[:, pl.ds(pl.multiple_of(offset, 128), size)] for block in blocks]
    return jnp.concatenate(parts, axis=0) if len(parts) > 1 else parts[0]


def products(blocks, weights, sp, group):
    w_query, w_key, w_value, kv_came, kv_other, *quarters = weights
    rows = jnp.concatenate([block[...] for block in blocks], axis=0)
    own_query = plain(rows, w_query[...])
    own_kv = turned(rows, jnp.concatenate([w_key[...], w_value[...]], axis=0))
    size = quarters[0].shape[0]
    pair_query = None
    for i, weight in enumerate(quarters):
        at = (sp ^ (i >> 1)) * 2 + (group ^ (i & 1))
        term = plain(rows_at(blocks, at * size, size), weight[...])
        pair_query = term if pair_query is None else pair_query + term
    depth = kv_came.shape[1]
    pair_kv = turned(rows_at(blocks, sp * depth, depth), kv_came[...]) + turned(
        rows_at(blocks, (1 - sp) * depth, depth), kv_other[...]
    )
    return own_query, own_kv, pair_query, pair_kv


def early_kernel(flags, *refs):
    blocks, weights, out = refs[:-10], refs[-10:-1], refs[-1]
    head = weights[0].shape[1]
    for i, part in enumerate(products(blocks, weights, flags[0], flags[3])):
        out[:, i * head : (i + 1) * head] = part


def tail_kernel(flags, early, middle, relayed, cosine, sine_part, *refs):
    weights, (queries, key_value, last) = refs[:9], refs[9:]
    side, inner = flags[1], flags[2]
    head = weights[0].shape[1]
    half_head = head // 2
    last[...] = jnp.where(inner != 0, middle[...], relayed[...])
    late = products([last], weights, flags[0], flags[3])
    join = lambda i: jnp.concatenate([early[:, i * head : (i + 1) * head], late[i]], axis=0)
    own_query, own_kv, pair_query, pair_kv = [join(i) for i in range(4)]
    spin = lambda v: v * cosine[...] + pltpu.roll(v, half_head, 1) * sine_part[...]
    scale = PRE_SCALE ** (-0.5)
    count = own_query.shape[0]
    queries[:count] = (spin(own_query) * scale).astype(queries.dtype)
    queries[count:] = (spin(pair_query) * scale).astype(queries.dtype)
    lane = lax.broadcasted_iota(jnp.int32, own_kv.shape, 1)
    low = lane < half_head
    even = side == 0
    first = jnp.where(even, own_kv, pair_kv)
    second = jnp.where(even, pair_kv, own_kv)
    key_raw = jnp.where(low, first, pltpu.roll(second, half_head, 1))
    key_raw = key_raw.astype(jnp.bfloat16).astype(jnp.float32)
    key_value[:, :head] = spin(key_raw).astype(key_value.dtype)
    value = jnp.where(low, pltpu.roll(first, half_head, 1), second)
    key_value[:, head:] = value.astype(key_value.dtype)


def place_of(flags, index, flip_side, flip_core, slabs, rows, cores):
    block = jnp.zeros_like(index)
    for k in range(1, slabs):
        block = block + (index >= k * rows).astype(jnp.int32)
    at = (flags[5] ^ block) * 2 + (flags[1] ^ flip_side)
    return (at * cores + (flags[0] ^ flip_core)) * rows + index - block * rows


def tables_kernel(slabs, cores, flags, spread, cosine, sine_part):
    shape = cosine.shape
    index = lax.broadcasted_iota(jnp.int32, shape, 0)
    places = place_of(flags, index, 0, 0, slabs, shape[0] // slabs, cores)
    angles = places.astype(jnp.float32) * spread[...]
    cosine[...] = jnp.cos(angles)
    sines = jnp.sin(angles)
    low = lax.broadcasted_iota(jnp.int32, shape, 1) < shape[1] // 2
    sine_part[...] = jnp.where(low, -sines, sines)


def attend_kernel(slabs, cores, flags, lengths, queries, *refs):
    pieces, outs = refs[:4], refs[4:]
    count, head = pieces[0].shape[0], queries.shape[1]
    rows = count // slabs
    place = lambda shape, axis, a, b: place_of(
        flags, lax.broadcasted_iota(jnp.int32, shape, axis), a, b, slabs, rows, cores
    )
    end = 0
    ends = []
    for i in range(lengths.shape[0]):
        end = end + lengths[i]
        ends.append(end)
    step = min(count, 4 * rows)
    even = flags[1] == 0
    for at in range(0, count, step):
        index = at + lax.broadcasted_iota(jnp.int32, (step, 1), 0)
        query_places = place_of(flags, index, 0, 0, slabs, rows, cores)
        starts = jnp.zeros_like(query_places)
        for end in ends:
            starts = jnp.where(query_places >= end, end, starts)
        masks = []
        for c in range(4):
            key_places = place((1, count), 1, c % 2, c // 2)
            masks.append((key_places <= query_places) & (key_places >= starts))
        mixed = []
        for h in range(2):
            query = queries[h * count + at : h * count + at + step]
            scores = [
                jnp.where(mask, turned(query, piece[:, :head]), masked_low)
                for piece, mask in zip(pieces, masks)
            ]
            largest = scores[0]
            for part in scores[1:]:
                largest = jnp.maximum(largest, part)
            largest = jnp.max(largest, axis=1, keepdims=True)
            total, acc = 0.0, 0.0
            for part, piece, mask in zip(scores, pieces, masks):
                e = jnp.where(mask, jnp.exp(part - largest), 0.0)
                total = total + e
                acc = acc + plain(e.astype(jnp.bfloat16), piece[:, head:])
            total = jnp.sum(total, axis=1, keepdims=True)
            mixed.append((acc / total).astype(jnp.bfloat16))
        low = jnp.where(even, mixed[0], mixed[1])
        high = jnp.where(even, mixed[1], mixed[0])
        for k in range(step // rows):
            out = outs[at // rows + k]
            out[:, :head] = low[k * rows : (k + 1) * rows]
            out[:, head:] = high[k * rows : (k + 1) * rows]


def head_kernel(flags, came, other, w_out, out, sem):
    head, quarter = w_out.shape[0], out.shape[1]
    half_rows = came.shape[0]
    own = pl.ds(pl.multiple_of(flags[1] * head, head), head)
    columns = pl.ds(pl.multiple_of(flags[4] * quarter, 128), quarter)
    copy = pltpu.make_async_copy(w_out.at[:, columns], out.at[own], sem)
    copy.start()
    for i, piece in enumerate((came, other)):
        at = (1 - flags[1]) * head + (flags[0] ^ i) * half_rows
        out[pl.ds(pl.multiple_of(at, half_rows), half_rows)] = piece[...]
    copy.wait()


def project_kernel(peers, split, flags, *refs):
    stacked, pieces, outs = refs[:peers], list(refs[peers:-peers]), refs[-peers:]
    count, width = outs[0].shape
    rows = jnp.concatenate([m[...] for m in stacked], axis=0)
    step = 384 if width % 384 == 0 else width
    received = flags[2] != flags[0]
    for at in range(0, width, step):
        parts = [p[:, at : at + step] for p in pieces]
        if split:
            parts[-2:] = [jnp.where(received, parts[-2], parts[-1])]
        total = plain(rows, jnp.concatenate(parts, axis=0))
        for i, out in enumerate(outs):
            out[:, at : at + step] = total[i * count : (i + 1) * count].astype(out.dtype)


def assemble_kernel(flags, *refs):
    pieces, out, sems = refs[:-2], refs[-2], refs[-1]
    width = pieces[0].shape[1]
    copies = []
    for i, piece in enumerate(pieces):
        at = pl.multiple_of((flags[4] ^ i) * width, 128)
        copies.append(pltpu.make_async_copy(piece, out.at[:, pl.ds(at, width)], sems.at[i]))
        copies[-1].start()
    for copy in copies:
        copy.wait()


def local(tokens, w_query, w_key, w_value, w_out, doc_lengths):
    rows, width = tokens.shape
    tp_count = lax.axis_size("tp")
    sp_count = lax.axis_size("sp")
    sp_place = lax.axis_index("sp")
    tp_place = lax.axis_index("tp")
    group = lax.axis_index("groups") % 2
    slabs = tp_count // 2
    slab = tp_place // 2
    side = tp_place % 2
    head_dim = w_query.shape[1]
    short = slabs == 4
    is_inner = lambda t: (t >> 1) in (1, 2)

    if short:
        far = swap_tp(tokens, 4)
        near = swap_tp(tokens, 2)
        middle = swap_tp(tokens, 6, is_inner)
        relayed = swap_tp(far, 2, is_inner)
        firsts, last = [tokens, near, far], [middle, relayed]
    else:
        came = [swap_tp(tokens, 2 * k) for k in range(1, slabs)]
        firsts, last = [tokens] + came[:-1], [came[-1], came[-1]]

    depth = width // sp_count
    quarter = w_out.shape[1] // 4
    half_rows = head_dim // sp_count
    mine = group * 2 + side
    inner = ((slab == 1) | (slab == 2)).astype(jnp.int32)
    flags = jnp.stack([sp_place, side, inner, group, mine, slab]).astype(jnp.int32)
    turned_kv = [w_key.T, w_value.T]
    share_q = lax.dynamic_slice_in_dim(
        w_query, (sp_place * 2 + group) * (depth // 2), depth // 2, 0
    )
    share_kv = jnp.concatenate(
        [lax.dynamic_slice_in_dim(w, sp_place * depth, depth, 1) for w in turned_kv], axis=0
    )
    core_low = sp_place == 0
    sent_at = (sp_place * half_rows, (mine ^ 1) * quarter)
    share_q, share_kv, doc_lengths, w_out, flags, core_low, sent_at = fence(
        share_q, share_kv, doc_lengths, w_out, flags, core_low, sent_at
    )
    came_q = swap_tp(share_q, 1)
    cross_q = swap_in_slab(came_q, 1, 0)
    came_kv = swap_tp(share_kv, 1)
    out_sent = lax.dynamic_slice(w_out, sent_at, (half_rows, quarter))
    out_came = swap_tp(out_sent, 1)
    out_other = swap_sp(out_came)
    weights = [w_query, *turned_kv, came_kv, swap_sp(came_kv), came_q, cross_q]
    weights += [swap_sp(came_q), swap_sp(cross_q)]
    early = call(
        early_kernel, [((len(firsts) * rows, 4 * head_dim), jnp.float32)], [flags], firsts + weights
    )[0]

    in_order = lambda a, b, flag: [jnp.where(flag, a, b), jnp.where(flag, b, a)]
    out_own = call(
        head_kernel,
        [((2 * head_dim, quarter), jnp.bfloat16)],
        [flags],
        [out_came, out_other],
        [pltpu.SemaphoreType.DMA(())],
        far=[w_out],
    )[0]
    if short:
        out_first = swap_by_core(out_own, (2, 4))
        out_swapped = swap_sp(out_first)

    count = slabs * rows
    half_head = head_dim // 2
    powers = np.arange(head_dim, dtype=np.float32) % half_head * np.float32(2.0 / head_dim)
    spread = jnp.asarray(np.power(np.float32(10000.0), -powers)[None, :])
    tables = call(
        lambda *refs: tables_kernel(slabs, sp_count, *refs),
        [((count, head_dim), jnp.float32)] * 2,
        [flags],
        [spread],
    )
    queries, key_value = call(
        tail_kernel,
        [((2 * count, head_dim), jnp.bfloat16), ((count, 2 * head_dim), jnp.bfloat16)],
        [flags],
        [early, *last, *tables] + weights,
        [pltpu.VMEM((rows, width), jnp.bfloat16)],
    )

    beside = swap_tp(key_value, 1)
    every = [key_value, beside, swap_sp(key_value), swap_sp(beside)]
    mixed = call(
        lambda *refs: attend_kernel(slabs, sp_count, *refs),
        [((rows, 2 * head_dim), jnp.bfloat16)] * slabs,
        [flags, doc_lengths],
        [queries] + every,
        limit=16 if short else 56,
    )

    parts = [mixed[0]]
    for k in range(1, slabs):
        parts.append(swap_tp(mixed[k], 2 * k))
    if short:
        parts[1:3] = in_order(parts[1], parts[2], core_low)
    merged = jnp.concatenate(parts, axis=1)
    peers = ((0, 0), (0, 1), (1, 0), (1, 1))
    stacked = [merged] + [swap_in_slab(merged, g, t) for g, t in peers[1:]]
    if short:
        out_sent = jnp.where(core_low, out_own, out_first)
        out_last = swap_by_core(out_sent, (6, 2), is_inner)
        out_last, stacked[2] = fence(out_last, stacked[2])
        pieces = [out_own, out_first, out_swapped, out_last, swap_sp(out_last)]
    else:
        pieces = [out_own]
        mine_of = lax.dynamic_slice_in_dim(out_own, sp_place * head_dim, head_dim, 0)
        for k in range(1, slabs):
            piece = swap_tp(mine_of, 2 * k)
            both = in_order(piece, swap_sp(piece), core_low)
            pieces.append(jnp.concatenate(both, axis=0))
    outs = call(
        lambda *refs: project_kernel(len(peers), short, *refs),
        [((rows, quarter), jnp.bfloat16)] * len(peers),
        [flags],
        stacked + pieces,
    )
    outs = [outs[0]] + [swap_in_slab(o, g, t) for o, (g, t) in zip(outs[1:], peers[1:])]
    sems = [pltpu.SemaphoreType.DMA((len(outs),))]
    shape = ((rows, width), jnp.bfloat16)
    return call(assemble_kernel, [shape], [flags], outs, sems, pl.ANY)[0]


def solution(mesh):
    placed = (
        P(("groups", "tp", "sp"), None),
        P(None, "tp"),
        P(None, "tp"),
        P(None, "tp"),
        P("tp", None),
        P("groups"),
    )

    return jax.shard_map(
        local,
        mesh=mesh,
        in_specs=placed,
        out_specs=P(("groups", "tp", "sp"), None),
        check_vma=False,
    )
```

```python
import jax
import jax.numpy as jnp
import numpy as np
from jax import lax
from jax.experimental import pallas as pl
from jax.experimental.pallas import tpu as pltpu
from jax.sharding import PartitionSpec as P

PRE_SCALE = 144

masked_low = -1e30


def swap_tp(block, flip, only=None):
    count = lax.axis_size("tp")
    route = [(t, t ^ flip) for t in range(count) if only is None or only(t)]
    return lax.ppermute(block, "tp", route)


def swap_sp(block):
    count = lax.axis_size("sp")
    return lax.ppermute(block, "sp", [(s, s ^ 1) for s in range(count)])


def swap_by_core(block, flips, only):
    count, cores = lax.axis_size("tp"), lax.axis_size("sp")
    route = [
        (t * cores + s, (t ^ flips[s]) * cores + s)
        for t in range(count)
        for s in range(cores)
        if only(t)
    ]
    return lax.ppermute(block, ("tp", "sp"), route)


def swap_in_slab(block, group_flip, tp_flip):
    groups = lax.axis_size("groups")
    count = lax.axis_size("tp")
    route = [
        (g * count + t, (g ^ group_flip) * count + (t ^ tp_flip))
        for g in range(groups)
        for t in range(count)
    ]
    return lax.ppermute(block, ("groups", "tp"), route)


def fence(*values):
    return lax.optimization_barrier(values)


def call(kernel, shapes, scalars, operands, scratch=(), outs=pltpu.VMEM, far=(), limit=16):
    size = sum(x.size * x.dtype.itemsize for x in operands)
    params = None
    if size < 8 << 20:
        operands = [pltpu.with_memory_space_constraint(x, pltpu.VMEM) for x in operands]
        params = pltpu.CompilerParams(vmem_limit_bytes=limit << 20)
    specs = [pl.BlockSpec(memory_space=pltpu.SMEM)] * len(scalars)
    specs += [pl.BlockSpec(memory_space=pltpu.VMEM)] * len(operands)
    specs += [pl.BlockSpec(memory_space=pltpu.HBM)] * len(far)
    far = [pltpu.with_memory_space_constraint(x, pltpu.HBM) for x in far]
    return pl.pallas_call(
        kernel,
        in_specs=specs,
        out_specs=[pl.BlockSpec(memory_space=outs)] * len(shapes),
        out_shape=[jax.ShapeDtypeStruct(*shape) for shape in shapes],
        scratch_shapes=list(scratch),
        compiler_params=params,
    )(*scalars, *operands, *far)


def plain(a, w):
    return jnp.dot(a, w, preferred_element_type=jnp.float32)


def turned(a, w):
    return lax.dot_general(a, w, (((1,), (1,)), ((), ())), preferred_element_type=jnp.float32)


def rows_at(blocks, offset, size):
    parts = [block[:, pl.ds(pl.multiple_of(offset, 128), size)] for block in blocks]
    return jnp.concatenate(parts, axis=0) if len(parts) > 1 else parts[0]


def products(blocks, weights, sp, group):
    w_query, w_key, w_value, kv_came, kv_other, *quarters = weights
    rows = jnp.concatenate([block[...] for block in blocks], axis=0)
    own_query = plain(rows, w_query[...])
    own_kv = turned(rows, jnp.concatenate([w_key[...], w_value[...]], axis=0))
    size = quarters[0].shape[0]
    pair_query = None
    for i, weight in enumerate(quarters):
        at = (sp ^ (i >> 1)) * 2 + (group ^ (i & 1))
        term = plain(rows_at(blocks, at * size, size), weight[...])
        pair_query = term if pair_query is None else pair_query + term
    depth = kv_came.shape[1]
    pair_kv = turned(rows_at(blocks, sp * depth, depth), kv_came[...]) + turned(
        rows_at(blocks, (1 - sp) * depth, depth), kv_other[...]
    )
    return own_query, own_kv, pair_query, pair_kv


def early_kernel(flags, *refs):
    blocks, weights, out = refs[:-10], refs[-10:-1], refs[-1]
    head = weights[0].shape[1]
    for i, part in enumerate(products(blocks, weights, flags[0], flags[3])):
        out[:, i * head : (i + 1) * head] = part


def tail_kernel(flags, early, middle, relayed, cosine, sine_part, *refs):
    weights, (queries, key_value, last) = refs[:9], refs[9:]
    side, inner = flags[1], flags[2]
    head = weights[0].shape[1]
    half_head = head // 2
    last[...] = jnp.where(inner != 0, middle[...], relayed[...])
    late = products([last], weights, flags[0], flags[3])
    join = lambda i: jnp.concatenate([early[:, i * head : (i + 1) * head], late[i]], axis=0)
    own_query, own_kv, pair_query, pair_kv = [join(i) for i in range(4)]
    spin = lambda v: v * cosine[...] + pltpu.roll(v, half_head, 1) * sine_part[...]
    scale = PRE_SCALE ** (-0.5)
    count = own_query.shape[0]
    queries[:count] = (spin(own_query) * scale).astype(queries.dtype)
    queries[count:] = (spin(pair_query) * scale).astype(queries.dtype)
    lane = lax.broadcasted_iota(jnp.int32, own_kv.shape, 1)
    low = lane < half_head
    even = side == 0
    first = jnp.where(even, own_kv, pair_kv)
    second = jnp.where(even, pair_kv, own_kv)
    key_raw = jnp.where(low, first, pltpu.roll(second, half_head, 1))
    key_raw = key_raw.astype(jnp.bfloat16).astype(jnp.float32)
    key_value[:, :head] = spin(key_raw).astype(key_value.dtype)
    value = jnp.where(low, pltpu.roll(first, half_head, 1), second)
    key_value[:, head:] = value.astype(key_value.dtype)


def place_of(flags, index, flip_side, flip_core, slabs, rows, cores):
    block = jnp.zeros_like(index)
    for k in range(1, slabs):
        block = block + (index >= k * rows).astype(jnp.int32)
    at = (flags[5] ^ block) * 2 + (flags[1] ^ flip_side)
    return (at * cores + (flags[0] ^ flip_core)) * rows + index - block * rows


def tables_kernel(slabs, cores, flags, spread, cosine, sine_part):
    shape = cosine.shape
    index = lax.broadcasted_iota(jnp.int32, shape, 0)
    places = place_of(flags, index, 0, 0, slabs, shape[0] // slabs, cores)
    angles = places.astype(jnp.float32) * spread[...]
    cosine[...] = jnp.cos(angles)
    sines = jnp.sin(angles)
    low = lax.broadcasted_iota(jnp.int32, shape, 1) < shape[1] // 2
    sine_part[...] = jnp.where(low, -sines, sines)


def attend_kernel(slabs, cores, flags, lengths, queries, *refs):
    pieces, outs = refs[:4], refs[4:]
    count, head = pieces[0].shape[0], queries.shape[1]
    rows = count // slabs
    place = lambda shape, axis, a, b: place_of(
        flags, lax.broadcasted_iota(jnp.int32, shape, axis), a, b, slabs, rows, cores
    )
    end = 0
    ends = []
    for i in range(lengths.shape[0]):
        end = end + lengths[i]
        ends.append(end)
    step = min(count, 4 * rows)
    even = flags[1] == 0
    for at in range(0, count, step):
        index = at + lax.broadcasted_iota(jnp.int32, (step, 1), 0)
        query_places = place_of(flags, index, 0, 0, slabs, rows, cores)
        starts = jnp.zeros_like(query_places)
        for end in ends:
            starts = jnp.where(query_places >= end, end, starts)
        masks = []
        for c in range(4):
            key_places = place((1, count), 1, c % 2, c // 2)
            masks.append((key_places <= query_places) & (key_places >= starts))
        mixed = []
        for h in range(2):
            query = queries[h * count + at : h * count + at + step]
            scores = [
                jnp.where(mask, turned(query, piece[:, :head]), masked_low)
                for piece, mask in zip(pieces, masks)
            ]
            largest = scores[0]
            for part in scores[1:]:
                largest = jnp.maximum(largest, part)
            largest = jnp.max(largest, axis=1, keepdims=True)
            total, acc = 0.0, 0.0
            for part, piece, mask in zip(scores, pieces, masks):
                e = jnp.where(mask, jnp.exp(part - largest), 0.0)
                total = total + e
                acc = acc + plain(e.astype(jnp.bfloat16), piece[:, head:])
            total = jnp.sum(total, axis=1, keepdims=True)
            mixed.append((acc / total).astype(jnp.bfloat16))
        low = jnp.where(even, mixed[0], mixed[1])
        high = jnp.where(even, mixed[1], mixed[0])
        for k in range(step // rows):
            out = outs[at // rows + k]
            out[:, :head] = low[k * rows : (k + 1) * rows]
            out[:, head:] = high[k * rows : (k + 1) * rows]


def cut_kernel(flags, w_query, w_key, w_value, w_out, share_q, share_kv, out_sent, sems):
    sp, group = flags[0], flags[3]
    head = w_key.shape[0]
    quarter_depth, depth = share_q.shape[0], share_kv.shape[1]
    half_rows, quarter = out_sent.shape
    rows = pl.ds(pl.multiple_of((sp * 2 + group) * quarter_depth, 128), quarter_depth)
    deep = pl.ds(pl.multiple_of(sp * depth, 128), depth)
    columns = pl.ds(pl.multiple_of((flags[4] ^ 1) * quarter, 128), quarter)
    heads = pl.ds(pl.multiple_of(sp * half_rows, half_rows), half_rows)
    moves = (
        (w_query.at[rows], share_q),
        (w_key.at[:, deep], share_kv.at[:head]),
        (w_value.at[:, deep], share_kv.at[head:]),
        (w_out.at[heads, columns], out_sent),
    )
    copies = [pltpu.make_async_copy(a, b, sems.at[i]) for i, (a, b) in enumerate(moves)]
    for copy in copies:
        copy.start()
    for copy in copies:
        copy.wait()


def head_kernel(flags, came, other, w_out, out, out_head, sem):
    head, quarter = w_out.shape[0], out.shape[1]
    half_rows = came.shape[0]
    own = pl.ds(pl.multiple_of(flags[1] * head, head), head)
    columns = pl.ds(pl.multiple_of(flags[4] * quarter, 128), quarter)
    copy = pltpu.make_async_copy(w_out.at[:, columns], out.at[own], sem)
    copy.start()
    for i, piece in enumerate((came, other)):
        at = (1 - flags[1]) * head + (flags[0] ^ i) * half_rows
        out[pl.ds(pl.multiple_of(at, half_rows), half_rows)] = piece[...]
    copy.wait()
    out_head[...] = out[pl.ds(pl.multiple_of(flags[0] * head, head), head)]


def project_kernel(peers, split, flags, *refs):
    stacked, pieces, outs = refs[:peers], list(refs[peers:-peers]), refs[-peers:]
    count, width = outs[0].shape
    rows = jnp.concatenate([m[...] for m in stacked], axis=0)
    step = 384 if width % 384 == 0 else width
    low, inner = flags[0] == 0, flags[2] != 0
    for at in range(0, width, step):
        parts = [p[:, at : at + step] for p in pieces]
        if split:
            own, outer, outer2, near, near2, far, far2, last, last2 = parts
            pick = lambda flag, a, b: jnp.where(flag, a, b)
            heads = lambda a, b: jnp.concatenate([pick(low, a, b), pick(low, b, a)], axis=0)
            parts = [
                own,
                pick(inner, pick(low, outer2, outer), heads(near, near2)),
                pick(inner, pick(low, outer, outer2), heads(far, far2)),
                pick(low == inner, last2, last),
            ]
        total = plain(rows, jnp.concatenate(parts, axis=0))
        for i, out in enumerate(outs):
            out[:, at : at + step] = total[i * count : (i + 1) * count].astype(out.dtype)


def assemble_kernel(flags, *refs):
    pieces, out, sems = refs[:-2], refs[-2], refs[-1]
    width = pieces[0].shape[1]
    copies = []
    for i, piece in enumerate(pieces):
        at = pl.multiple_of((flags[4] ^ i) * width, 128)
        copies.append(pltpu.make_async_copy(piece, out.at[:, pl.ds(at, width)], sems.at[i]))
        copies[-1].start()
    for copy in copies:
        copy.wait()


def local(tokens, w_query, w_key, w_value, w_out, doc_lengths):
    rows, width = tokens.shape
    tp_count = lax.axis_size("tp")
    sp_count = lax.axis_size("sp")
    sp_place = lax.axis_index("sp")
    tp_place = lax.axis_index("tp")
    group = lax.axis_index("groups") % 2
    slabs = tp_count // 2
    slab = tp_place // 2
    side = tp_place % 2
    head_dim = w_query.shape[1]
    short = slabs == 4
    is_inner = lambda t: (t >> 1) in (1, 2)

    if short:
        far = swap_tp(tokens, 4)
        near = swap_tp(tokens, 2)
        middle = swap_tp(tokens, 6, is_inner)
        relayed = swap_tp(far, 2, is_inner)
        firsts, last = [tokens, near, far], [middle, relayed]
    else:
        came = [swap_tp(tokens, 2 * k) for k in range(1, slabs)]
        firsts, last = [tokens] + came[:-1], [came[-1], came[-1]]

    depth = width // sp_count
    quarter = w_out.shape[1] // 4
    half_rows = head_dim // sp_count
    mine = group * 2 + side
    inner = ((slab == 1) | (slab == 2)).astype(jnp.int32)
    flags = jnp.stack([sp_place, side, inner, group, mine, slab]).astype(jnp.int32)
    turned_kv = [w_key.T, w_value.T]
    core_low = sp_place == 0
    flags, doc_lengths, core_low = fence(flags, doc_lengths, core_low)
    share_q, share_kv, out_sent = call(
        cut_kernel,
        [
            ((depth // 2, head_dim), jnp.bfloat16),
            ((head_dim, depth), jnp.bfloat16),
            ((half_rows, quarter), jnp.bfloat16),
        ],
        [flags],
        [],
        [pltpu.SemaphoreType.DMA((4,))],
        pltpu.VMEM if short else pl.ANY,
        [w_query, *turned_kv, w_out],
    )
    came_q = swap_tp(share_q, 1)
    cross_q = swap_in_slab(came_q, 1, 0)
    came_kv = swap_tp(share_kv, 1)
    out_came = swap_tp(out_sent, 1)
    out_other = swap_sp(out_came)
    weights = [w_query, *turned_kv, came_kv, swap_sp(came_kv), came_q, cross_q]
    weights += [swap_sp(came_q), swap_sp(cross_q)]
    early = call(
        early_kernel, [((len(firsts) * rows, 4 * head_dim), jnp.float32)], [flags], firsts + weights
    )[0]

    in_order = lambda a, b, flag: [jnp.where(flag, a, b), jnp.where(flag, b, a)]
    out_own, out_head = call(
        head_kernel,
        [((2 * head_dim, quarter), jnp.bfloat16), ((head_dim, quarter), jnp.bfloat16)],
        [flags],
        [out_came, out_other],
        [pltpu.SemaphoreType.DMA(())],
        far=[w_out],
    )
    if short:
        is_outer = lambda t: not is_inner(t)
        out_outer = swap_by_core(out_own, (4, 2), is_outer)
        out_near = swap_by_core(out_head, (2, 2), is_inner)
        out_far = swap_by_core(out_head, (4, 4), is_inner)
        held = [out_outer, swap_sp(out_outer), out_near, swap_sp(out_near)]
        held += [out_far, swap_sp(out_far)]

    count = slabs * rows
    half_head = head_dim // 2
    powers = np.arange(head_dim, dtype=np.float32) % half_head * np.float32(2.0 / head_dim)
    spread = jnp.asarray(np.power(np.float32(10000.0), -powers)[None, :])
    tables = call(
        lambda *refs: tables_kernel(slabs, sp_count, *refs),
        [((count, head_dim), jnp.float32)] * 2,
        [flags],
        [spread],
    )
    queries, key_value = call(
        tail_kernel,
        [((2 * count, head_dim), jnp.bfloat16), ((count, 2 * head_dim), jnp.bfloat16)],
        [flags],
        [early, *last, *tables] + weights,
        [pltpu.VMEM((rows, width), jnp.bfloat16)],
    )

    beside = swap_tp(key_value, 1)
    every = [key_value, beside, swap_sp(key_value), swap_sp(beside)]
    mixed = call(
        lambda *refs: attend_kernel(slabs, sp_count, *refs),
        [((rows, 2 * head_dim), jnp.bfloat16)] * slabs,
        [flags, doc_lengths],
        [queries] + every,
        limit=16 if short else 56,
    )
    mixed = list(mixed)

    if short:
        out_outer, mixed[1] = fence(out_outer, mixed[1])
        out_sent = jnp.where(core_low, out_outer, out_own)
    parts = [mixed[0]]
    for k in range(1, slabs):
        parts.append(swap_tp(mixed[k], 2 * k))
    merged = jnp.concatenate(parts, axis=1)
    peers = ((0, 0), (0, 1), (1, 0), (1, 1))
    stacked = [merged] + [swap_in_slab(merged, g, t) for g, t in peers[1:]]
    if short:
        out_last = swap_by_core(out_sent, (2, 6), is_inner)
        out_last, stacked[2] = fence(out_last, stacked[2])
        pieces = [out_own, *held, out_last, swap_sp(out_last)]
    else:
        pieces = [out_own]
        for k in range(1, slabs):
            piece = swap_tp(out_head, 2 * k)
            both = in_order(piece, swap_sp(piece), core_low)
            pieces.append(jnp.concatenate(both, axis=0))
    outs = call(
        lambda *refs: project_kernel(len(peers), short, *refs),
        [((rows, quarter), jnp.bfloat16)] * len(peers),
        [flags],
        stacked + pieces,
    )
    outs = [outs[0]] + [swap_in_slab(o, g, t) for o, (g, t) in zip(outs[1:], peers[1:])]
    sems = [pltpu.SemaphoreType.DMA((len(outs),))]
    shape = ((rows, width), jnp.bfloat16)
    return call(assemble_kernel, [shape], [flags], outs, sems, pl.ANY)[0]


def solution(mesh):
    placed = (
        P(("groups", "tp", "sp"), None),
        P(None, "tp"),
        P(None, "tp"),
        P(None, "tp"),
        P("tp", None),
        P("groups"),
    )

    return jax.shard_map(
        local,
        mesh=mesh,
        in_specs=placed,
        out_specs=P(("groups", "tp", "sp"), None),
        check_vma=False,
    )
```

```python
import jax
import jax.numpy as jnp
import numpy as np
from jax import lax
from jax.experimental import pallas as pl
from jax.experimental.pallas import tpu as pltpu
from jax.sharding import PartitionSpec as P

PRE_SCALE = 144

masked_low = -1e30


def swap_tp(block, flip, only=None):
    count = lax.axis_size("tp")
    route = [(t, t ^ flip) for t in range(count) if only is None or only(t)]
    return lax.ppermute(block, "tp", route)


def swap_sp(block):
    count = lax.axis_size("sp")
    return lax.ppermute(block, "sp", [(s, s ^ 1) for s in range(count)])


def swap_by_core(block, flips, only):
    count, cores = lax.axis_size("tp"), lax.axis_size("sp")
    route = [
        (t * cores + s, (t ^ flips[s]) * cores + s)
        for t in range(count)
        for s in range(cores)
        if only(t)
    ]
    return lax.ppermute(block, ("tp", "sp"), route)


def swap_in_slab(block, group_flip, tp_flip):
    groups = lax.axis_size("groups")
    count = lax.axis_size("tp")
    route = [
        (g * count + t, (g ^ group_flip) * count + (t ^ tp_flip))
        for g in range(groups)
        for t in range(count)
    ]
    return lax.ppermute(block, ("groups", "tp"), route)


def fence(*values):
    return lax.optimization_barrier(values)


def call(kernel, shapes, scalars, operands, scratch=(), outs=pltpu.VMEM, far=(), limit=16):
    size = sum(x.size * x.dtype.itemsize for x in operands)
    params = None
    if size < 8 << 20:
        operands = [pltpu.with_memory_space_constraint(x, pltpu.VMEM) for x in operands]
        params = pltpu.CompilerParams(vmem_limit_bytes=limit << 20)
    specs = [pl.BlockSpec(memory_space=pltpu.SMEM)] * len(scalars)
    specs += [pl.BlockSpec(memory_space=pltpu.VMEM)] * len(operands)
    specs += [pl.BlockSpec(memory_space=pl.ANY)] * len(far)
    return pl.pallas_call(
        kernel,
        in_specs=specs,
        out_specs=[pl.BlockSpec(memory_space=outs)] * len(shapes),
        out_shape=[jax.ShapeDtypeStruct(*shape) for shape in shapes],
        scratch_shapes=list(scratch),
        compiler_params=params,
    )(*scalars, *operands, *far)


def plain(a, w):
    return jnp.dot(a, w, preferred_element_type=jnp.float32)


def turned(a, w):
    return lax.dot_general(a, w, (((1,), (1,)), ((), ())), preferred_element_type=jnp.float32)


def rows_at(blocks, offset, size):
    parts = [block[:, pl.ds(pl.multiple_of(offset, 128), size)] for block in blocks]
    return jnp.concatenate(parts, axis=0) if len(parts) > 1 else parts[0]


def products(blocks, weights, sp, group):
    w_query, w_key, w_value, kv_came, kv_other, *quarters = weights
    rows = jnp.concatenate([block[...] for block in blocks], axis=0)
    own_query = plain(rows, w_query[...])
    own_kv = turned(rows, jnp.concatenate([w_key[...], w_value[...]], axis=0))
    size = quarters[0].shape[0]
    pair_query = None
    for i, weight in enumerate(quarters):
        at = (sp ^ (i >> 1)) * 2 + (group ^ (i & 1))
        term = plain(rows_at(blocks, at * size, size), weight[...])
        pair_query = term if pair_query is None else pair_query + term
    depth = kv_came.shape[1]
    pair_kv = turned(rows_at(blocks, sp * depth, depth), kv_came[...]) + turned(
        rows_at(blocks, (1 - sp) * depth, depth), kv_other[...]
    )
    return own_query, own_kv, pair_query, pair_kv


def early_kernel(flags, *refs):
    blocks, weights, out = refs[:-10], refs[-10:-1], refs[-1]
    head = weights[0].shape[1]
    for i, part in enumerate(products(blocks, weights, flags[0], flags[3])):
        out[:, i * head : (i + 1) * head] = part


def tail_kernel(flags, early, middle, relayed, cosine, sine_part, *refs):
    weights, (queries, key_value, last) = refs[:9], refs[9:]
    side, inner = flags[1], flags[2]
    head = weights[0].shape[1]
    half_head = head // 2
    last[...] = jnp.where(inner != 0, middle[...], relayed[...])
    late = products([last], weights, flags[0], flags[3])
    join = lambda i: jnp.concatenate([early[:, i * head : (i + 1) * head], late[i]], axis=0)
    own_query, own_kv, pair_query, pair_kv = [join(i) for i in range(4)]
    spin = lambda v: v * cosine[...] + pltpu.roll(v, half_head, 1) * sine_part[...]
    scale = PRE_SCALE ** (-0.5)
    count = own_query.shape[0]
    queries[:count] = (spin(own_query) * scale).astype(queries.dtype)
    queries[count:] = (spin(pair_query) * scale).astype(queries.dtype)
    lane = lax.broadcasted_iota(jnp.int32, own_kv.shape, 1)
    low = lane < half_head
    even = side == 0
    first = jnp.where(even, own_kv, pair_kv)
    second = jnp.where(even, pair_kv, own_kv)
    key_raw = jnp.where(low, first, pltpu.roll(second, half_head, 1))
    key_raw = key_raw.astype(jnp.bfloat16).astype(jnp.float32)
    key_value[:, :head] = spin(key_raw).astype(key_value.dtype)
    value = jnp.where(low, pltpu.roll(first, half_head, 1), second)
    key_value[:, head:] = value.astype(key_value.dtype)


def place_of(flags, index, flip_side, flip_core, slabs, rows, cores):
    block = jnp.zeros_like(index)
    for k in range(1, slabs):
        block = block + (index >= k * rows).astype(jnp.int32)
    at = (flags[5] ^ block) * 2 + (flags[1] ^ flip_side)
    return (at * cores + (flags[0] ^ flip_core)) * rows + index - block * rows


def tables_kernel(slabs, cores, flags, spread, cosine, sine_part):
    shape = cosine.shape
    index = lax.broadcasted_iota(jnp.int32, shape, 0)
    places = place_of(flags, index, 0, 0, slabs, shape[0] // slabs, cores)
    angles = places.astype(jnp.float32) * spread[...]
    cosine[...] = jnp.cos(angles)
    sines = jnp.sin(angles)
    low = lax.broadcasted_iota(jnp.int32, shape, 1) < shape[1] // 2
    sine_part[...] = jnp.where(low, -sines, sines)


def attend_kernel(slabs, cores, flags, lengths, queries, *refs):
    pieces, outs = refs[:4], refs[4:]
    count, head = pieces[0].shape[0], queries.shape[1]
    rows = count // slabs
    place = lambda shape, axis, a, b: place_of(
        flags, lax.broadcasted_iota(jnp.int32, shape, axis), a, b, slabs, rows, cores
    )
    end = 0
    ends = []
    for i in range(lengths.shape[0]):
        end = end + lengths[i]
        ends.append(end)
    step = min(count, 4 * rows)
    even = flags[1] == 0
    for at in range(0, count, step):
        index = at + lax.broadcasted_iota(jnp.int32, (step, 1), 0)
        query_places = place_of(flags, index, 0, 0, slabs, rows, cores)
        starts = jnp.zeros_like(query_places)
        for end in ends:
            starts = jnp.where(query_places >= end, end, starts)
        masks = []
        for c in range(4):
            key_places = place((1, count), 1, c % 2, c // 2)
            masks.append((key_places <= query_places) & (key_places >= starts))
        mixed = []
        for h in range(2):
            query = queries[h * count + at : h * count + at + step]
            scores = [
                jnp.where(mask, turned(query, piece[:, :head]), masked_low)
                for piece, mask in zip(pieces, masks)
            ]
            largest = scores[0]
            for part in scores[1:]:
                largest = jnp.maximum(largest, part)
            largest = jnp.max(largest, axis=1, keepdims=True)
            total, acc = 0.0, 0.0
            for part, piece, mask in zip(scores, pieces, masks):
                e = jnp.where(mask, jnp.exp(part - largest), 0.0)
                total = total + e
                acc = acc + plain(e.astype(jnp.bfloat16), piece[:, head:])
            total = jnp.sum(total, axis=1, keepdims=True)
            mixed.append((acc / total).astype(jnp.bfloat16))
        low = jnp.where(even, mixed[0], mixed[1])
        high = jnp.where(even, mixed[1], mixed[0])
        for k in range(step // rows):
            out = outs[at // rows + k]
            out[:, :head] = low[k * rows : (k + 1) * rows]
            out[:, head:] = high[k * rows : (k + 1) * rows]


def cut_kernel(flags, w_query, w_key, w_value, w_out, share_q, share_kv, out_sent, sems):
    sp, group = flags[0], flags[3]
    head = w_key.shape[0]
    quarter_depth, depth = share_q.shape[0], share_kv.shape[1]
    half_rows, quarter = out_sent.shape
    rows = pl.ds(pl.multiple_of((sp * 2 + group) * quarter_depth, 128), quarter_depth)
    deep = pl.ds(pl.multiple_of(sp * depth, 128), depth)
    columns = pl.ds(pl.multiple_of((flags[4] ^ 1) * quarter, 128), quarter)
    heads = pl.ds(pl.multiple_of(sp * half_rows, half_rows), half_rows)
    moves = (
        (w_query.at[rows], share_q),
        (w_key.at[:, deep], share_kv.at[:head]),
        (w_value.at[:, deep], share_kv.at[head:]),
        (w_out.at[heads, columns], out_sent),
    )
    copies = [pltpu.make_async_copy(a, b, sems.at[i]) for i, (a, b) in enumerate(moves)]
    for copy in copies:
        copy.start()
    for copy in copies:
        copy.wait()


def head_kernel(flags, came, other, w_out, out, sem):
    head, quarter = w_out.shape[0], out.shape[1]
    half_rows = came.shape[0]
    own = pl.ds(pl.multiple_of(flags[1] * head, head), head)
    columns = pl.ds(pl.multiple_of(flags[4] * quarter, 128), quarter)
    copy = pltpu.make_async_copy(w_out.at[:, columns], out.at[own], sem)
    copy.start()
    for i, piece in enumerate((came, other)):
        at = (1 - flags[1]) * head + (flags[0] ^ i) * half_rows
        out[pl.ds(pl.multiple_of(at, half_rows), half_rows)] = piece[...]
    copy.wait()


def project_kernel(peers, split, flags, *refs):
    stacked, pieces, outs = refs[:peers], list(refs[peers:-peers]), refs[-peers:]
    count, width = outs[0].shape
    rows = jnp.concatenate([m[...] for m in stacked], axis=0)
    step = 384 if width % 384 == 0 else width
    low, inner = flags[0] == 0, flags[2] != 0
    for at in range(0, width, step):
        parts = [p[:, at : at + step] for p in pieces]
        if split:
            own, outer, outer2, inside, inside2, last, last2 = parts
            pick = lambda flag, a, b: jnp.where(flag, a, b)
            parts = [
                own,
                pick(inner, pick(low, outer2, outer), pick(low, inside, inside2)),
                pick(inner, pick(low, outer, outer2), pick(low, inside2, inside)),
                pick(low == inner, last2, last),
            ]
        total = plain(rows, jnp.concatenate(parts, axis=0))
        for i, out in enumerate(outs):
            out[:, at : at + step] = total[i * count : (i + 1) * count].astype(out.dtype)


def assemble_kernel(flags, *refs):
    pieces, out, sems = refs[:-2], refs[-2], refs[-1]
    width = pieces[0].shape[1]
    copies = []
    for i, piece in enumerate(pieces):
        at = pl.multiple_of((flags[4] ^ i) * width, 128)
        copies.append(pltpu.make_async_copy(piece, out.at[:, pl.ds(at, width)], sems.at[i]))
        copies[-1].start()
    for copy in copies:
        copy.wait()


def local(tokens, w_query, w_key, w_value, w_out, doc_lengths):
    rows, width = tokens.shape
    tp_count = lax.axis_size("tp")
    sp_count = lax.axis_size("sp")
    sp_place = lax.axis_index("sp")
    tp_place = lax.axis_index("tp")
    group = lax.axis_index("groups") % 2
    slabs = tp_count // 2
    slab = tp_place // 2
    side = tp_place % 2
    head_dim = w_query.shape[1]
    short = slabs == 4
    is_inner = lambda t: (t >> 1) in (1, 2)

    if short:
        far = swap_tp(tokens, 4)
        near = swap_tp(tokens, 2)
        middle = swap_tp(tokens, 6, is_inner)
        relayed = swap_tp(far, 2, is_inner)
        firsts, last = [tokens, near, far], [middle, relayed]
    else:
        came = [swap_tp(tokens, 2 * k) for k in range(1, slabs)]
        firsts, last = [tokens] + came[:-1], [came[-1], came[-1]]

    depth = width // sp_count
    quarter = w_out.shape[1] // 4
    half_rows = head_dim // sp_count
    mine = group * 2 + side
    inner = ((slab == 1) | (slab == 2)).astype(jnp.int32)
    flags = jnp.stack([sp_place, side, inner, group, mine, slab]).astype(jnp.int32)
    turned_kv = [w_key.T, w_value.T]
    core_low = sp_place == 0
    flags, doc_lengths, core_low = fence(flags, doc_lengths, core_low)
    share_q, share_kv, out_sent = call(
        cut_kernel,
        [
            ((depth // 2, head_dim), jnp.bfloat16),
            ((head_dim, depth), jnp.bfloat16),
            ((half_rows, quarter), jnp.bfloat16),
        ],
        [flags],
        [],
        [pltpu.SemaphoreType.DMA((4,))],
        pltpu.VMEM if short else pl.ANY,
        [pltpu.with_memory_space_constraint(x, pltpu.HBM) for x in (w_query, *turned_kv, w_out)],
    )
    came_q = swap_tp(share_q, 1)
    cross_q = swap_in_slab(came_q, 1, 0)
    came_kv = swap_tp(share_kv, 1)
    out_came = swap_tp(out_sent, 1)
    out_other = swap_sp(out_came)
    weights = [w_query, *turned_kv, came_kv, swap_sp(came_kv), came_q, cross_q]
    weights += [swap_sp(came_q), swap_sp(cross_q)]
    early = call(
        early_kernel, [((len(firsts) * rows, 4 * head_dim), jnp.float32)], [flags], firsts + weights
    )[0]

    in_order = lambda a, b, flag: [jnp.where(flag, a, b), jnp.where(flag, b, a)]
    out_own = call(
        head_kernel,
        [((2 * head_dim, quarter), jnp.bfloat16)],
        [flags],
        [out_came, out_other],
        [pltpu.SemaphoreType.DMA(())],
        far=[w_out],
    )[0]
    if short:
        is_outer = lambda t: not is_inner(t)
        out_outer = swap_by_core(out_own, (4, 2), is_outer)
        out_inner = swap_by_core(out_own, (2, 4), is_inner)
        held = [out_outer, swap_sp(out_outer)]
        held += [out_inner, swap_sp(out_inner)]

    count = slabs * rows
    half_head = head_dim // 2
    powers = np.arange(head_dim, dtype=np.float32) % half_head * np.float32(2.0 / head_dim)
    spread = jnp.asarray(np.power(np.float32(10000.0), -powers)[None, :])
    tables = call(
        lambda *refs: tables_kernel(slabs, sp_count, *refs),
        [((count, head_dim), jnp.float32)] * 2,
        [flags],
        [spread],
    )
    queries, key_value = call(
        tail_kernel,
        [((2 * count, head_dim), jnp.bfloat16), ((count, 2 * head_dim), jnp.bfloat16)],
        [flags],
        [early, *last, *tables] + weights,
        [pltpu.VMEM((rows, width), jnp.bfloat16)],
    )

    beside = swap_tp(key_value, 1)
    every = [key_value, beside, swap_sp(key_value), swap_sp(beside)]
    mixed = call(
        lambda *refs: attend_kernel(slabs, sp_count, *refs),
        [((rows, 2 * head_dim), jnp.bfloat16)] * slabs,
        [flags, doc_lengths],
        [queries] + every,
        limit=16 if short else 56,
    )

    mixed = list(mixed)
    if short:
        out_outer, mixed[1] = fence(out_outer, mixed[1])
        out_sent = jnp.where(core_low, out_outer, out_own)
    parts = [mixed[0]]
    for k in range(1, slabs):
        parts.append(swap_tp(mixed[k], 2 * k))
    merged = jnp.concatenate(parts, axis=1)
    peers = ((0, 0), (0, 1), (1, 0), (1, 1))
    stacked = [merged] + [swap_in_slab(merged, g, t) for g, t in peers[1:]]
    if short:
        out_last = swap_by_core(out_sent, (2, 6), is_inner)
        out_last, stacked[2] = fence(out_last, stacked[2])
        pieces = [out_own, *held, out_last, swap_sp(out_last)]
    else:
        pieces = [out_own]
        mine_of = lax.dynamic_slice_in_dim(out_own, sp_place * head_dim, head_dim, 0)
        for k in range(1, slabs):
            piece = swap_tp(mine_of, 2 * k)
            both = in_order(piece, swap_sp(piece), core_low)
            pieces.append(jnp.concatenate(both, axis=0))
    outs = call(
        lambda *refs: project_kernel(len(peers), short, *refs),
        [((rows, quarter), jnp.bfloat16)] * len(peers),
        [flags],
        stacked + pieces,
    )
    outs = [outs[0]] + [swap_in_slab(o, g, t) for o, (g, t) in zip(outs[1:], peers[1:])]
    sems = [pltpu.SemaphoreType.DMA((len(outs),))]
    shape = ((rows, width), jnp.bfloat16)
    return call(assemble_kernel, [shape], [flags], outs, sems, pl.ANY)[0]


def solution(mesh):
    placed = (
        P(("groups", "tp", "sp"), None),
        P(None, "tp"),
        P(None, "tp"),
        P(None, "tp"),
        P("tp", None),
        P("groups"),
    )

    return jax.shard_map(
        local,
        mesh=mesh,
        in_specs=placed,
        out_specs=P(("groups", "tp", "sp"), None),
        check_vma=False,
    )
```

```python
import jax
import jax.numpy as jnp
import numpy as np
from jax import lax
from jax.experimental import pallas as pl
from jax.experimental.pallas import tpu as pltpu
from jax.sharding import PartitionSpec as P

PRE_SCALE = 144

masked_low = -1e30


def swap_tp(block, flip, only=None):
    count = lax.axis_size("tp")
    route = [(t, t ^ flip) for t in range(count) if only is None or only(t)]
    return lax.ppermute(block, "tp", route)


def swap_sp(block):
    count = lax.axis_size("sp")
    return lax.ppermute(block, "sp", [(s, s ^ 1) for s in range(count)])


def swap_by_core(block, flips, only=lambda t: True):
    count, cores = lax.axis_size("tp"), lax.axis_size("sp")
    route = [
        (t * cores + s, (t ^ flips[s]) * cores + s)
        for t in range(count)
        for s in range(cores)
        if only(t)
    ]
    return lax.ppermute(block, ("tp", "sp"), route)


def swap_in_slab(block, group_flip, tp_flip):
    groups = lax.axis_size("groups")
    count = lax.axis_size("tp")
    route = [
        (g * count + t, (g ^ group_flip) * count + (t ^ tp_flip))
        for g in range(groups)
        for t in range(count)
    ]
    return lax.ppermute(block, ("groups", "tp"), route)


def fence(*values):
    return lax.optimization_barrier(values)


def call(kernel, shapes, scalars, operands, scratch=(), outs=pltpu.VMEM, far=(), limit=16):
    size = sum(x.size * x.dtype.itemsize for x in operands)
    params = None
    if size < 8 << 20:
        operands = [pltpu.with_memory_space_constraint(x, pltpu.VMEM) for x in operands]
        params = pltpu.CompilerParams(vmem_limit_bytes=limit << 20)
    specs = [pl.BlockSpec(memory_space=pltpu.SMEM)] * len(scalars)
    specs += [pl.BlockSpec(memory_space=pltpu.VMEM)] * len(operands)
    specs += [pl.BlockSpec(memory_space=pl.ANY)] * len(far)
    return pl.pallas_call(
        kernel,
        in_specs=specs,
        out_specs=[pl.BlockSpec(memory_space=outs)] * len(shapes),
        out_shape=[jax.ShapeDtypeStruct(*shape) for shape in shapes],
        scratch_shapes=list(scratch),
        compiler_params=params,
    )(*scalars, *operands, *far)


def plain(a, w):
    return jnp.dot(a, w, preferred_element_type=jnp.float32)


def turned(a, w):
    return lax.dot_general(a, w, (((1,), (1,)), ((), ())), preferred_element_type=jnp.float32)


def rows_at(blocks, offset, size):
    parts = [block[:, pl.ds(pl.multiple_of(offset, 128), size)] for block in blocks]
    return jnp.concatenate(parts, axis=0) if len(parts) > 1 else parts[0]


def products(blocks, weights, sp, group):
    w_query, w_key, w_value, kv_came, kv_other, *quarters = weights
    rows = jnp.concatenate([block[...] for block in blocks], axis=0)
    own_query = plain(rows, w_query[...])
    own_kv = turned(rows, jnp.concatenate([w_key[...], w_value[...]], axis=0))
    size = quarters[0].shape[0]
    pair_query = None
    for i, weight in enumerate(quarters):
        at = (sp ^ (i >> 1)) * 2 + (group ^ (i & 1))
        term = plain(rows_at(blocks, at * size, size), weight[...])
        pair_query = term if pair_query is None else pair_query + term
    depth = kv_came.shape[1]
    pair_kv = turned(rows_at(blocks, sp * depth, depth), kv_came[...]) + turned(
        rows_at(blocks, (1 - sp) * depth, depth), kv_other[...]
    )
    return own_query, own_kv, pair_query, pair_kv


def early_kernel(short, flags, *refs):
    blocks, weights, (out, near) = list(refs[:-11]), refs[-11:-2], refs[-2:]
    if short:
        near[...] = jnp.where(flags[2] != 0, blocks[1][...], blocks[2][...])
        blocks[1:3] = [near]
    head = weights[0].shape[1]
    for i, part in enumerate(products(blocks, weights, flags[0], flags[3])):
        out[:, i * head : (i + 1) * head] = part


def tail_kernel(flags, early, middle, relayed, cosine, sine_part, *refs):
    weights, (queries, key_value, last) = refs[:9], refs[9:]
    side, inner = flags[1], flags[2]
    head = weights[0].shape[1]
    half_head = head // 2
    last[...] = jnp.where(inner != 0, middle[...], relayed[...])
    late = products([last], weights, flags[0], flags[3])
    join = lambda i: jnp.concatenate([early[:, i * head : (i + 1) * head], late[i]], axis=0)
    own_query, own_kv, pair_query, pair_kv = [join(i) for i in range(4)]
    spin = lambda v: v * cosine[...] + pltpu.roll(v, half_head, 1) * sine_part[...]
    scale = PRE_SCALE ** (-0.5)
    count = own_query.shape[0]
    queries[:count] = (spin(own_query) * scale).astype(queries.dtype)
    queries[count:] = (spin(pair_query) * scale).astype(queries.dtype)
    lane = lax.broadcasted_iota(jnp.int32, own_kv.shape, 1)
    low = lane < half_head
    even = side == 0
    first = jnp.where(even, own_kv, pair_kv)
    second = jnp.where(even, pair_kv, own_kv)
    key_raw = jnp.where(low, first, pltpu.roll(second, half_head, 1))
    key_raw = key_raw.astype(jnp.bfloat16).astype(jnp.float32)
    key_value[:, :head] = spin(key_raw).astype(key_value.dtype)
    value = jnp.where(low, pltpu.roll(first, half_head, 1), second)
    key_value[:, head:] = value.astype(key_value.dtype)


def place_of(flags, index, flip_side, flip_core, slabs, rows, cores):
    block = jnp.zeros_like(index)
    for k in range(1, slabs):
        block = block + (index >= k * rows).astype(jnp.int32)
    at = (flags[5] ^ block) * 2 + (flags[1] ^ flip_side)
    return (at * cores + (flags[0] ^ flip_core)) * rows + index - block * rows


def tables_kernel(slabs, cores, flags, spread, cosine, sine_part):
    shape = cosine.shape
    index = lax.broadcasted_iota(jnp.int32, shape, 0)
    places = place_of(flags, index, 0, 0, slabs, shape[0] // slabs, cores)
    angles = places.astype(jnp.float32) * spread[...]
    cosine[...] = jnp.cos(angles)
    sines = jnp.sin(angles)
    low = lax.broadcasted_iota(jnp.int32, shape, 1) < shape[1] // 2
    sine_part[...] = jnp.where(low, -sines, sines)


def attend_kernel(slabs, cores, flags, lengths, queries, *refs):
    pieces, outs = refs[:4], refs[4:]
    count, head = pieces[0].shape[0], queries.shape[1]
    rows = count // slabs
    place = lambda shape, axis, a, b: place_of(
        flags, lax.broadcasted_iota(jnp.int32, shape, axis), a, b, slabs, rows, cores
    )
    end = 0
    ends = []
    for i in range(lengths.shape[0]):
        end = end + lengths[i]
        ends.append(end)
    step = min(count, 4 * rows)
    even = flags[1] == 0
    for at in range(0, count, step):
        index = at + lax.broadcasted_iota(jnp.int32, (step, 1), 0)
        query_places = place_of(flags, index, 0, 0, slabs, rows, cores)
        starts = jnp.zeros_like(query_places)
        for end in ends:
            starts = jnp.where(query_places >= end, end, starts)
        masks = []
        for c in range(4):
            key_places = place((1, count), 1, c % 2, c // 2)
            masks.append((key_places <= query_places) & (key_places >= starts))
        mixed = []
        for h in range(2):
            query = queries[h * count + at : h * count + at + step]
            scores = [
                jnp.where(mask, turned(query, piece[:, :head]), masked_low)
                for piece, mask in zip(pieces, masks)
            ]
            largest = scores[0]
            for part in scores[1:]:
                largest = jnp.maximum(largest, part)
            largest = jnp.max(largest, axis=1, keepdims=True)
            total, acc = 0.0, 0.0
            for part, piece, mask in zip(scores, pieces, masks):
                e = jnp.where(mask, jnp.exp(part - largest), 0.0)
                total = total + e
                acc = acc + plain(e.astype(jnp.bfloat16), piece[:, head:])
            total = jnp.sum(total, axis=1, keepdims=True)
            mixed.append((acc / total).astype(jnp.bfloat16))
        low = jnp.where(even, mixed[0], mixed[1])
        high = jnp.where(even, mixed[1], mixed[0])
        for k in range(step // rows):
            out = outs[at // rows + k]
            out[:, :head] = low[k * rows : (k + 1) * rows]
            out[:, head:] = high[k * rows : (k + 1) * rows]


def cut_kernel(flags, w_query, w_key, w_value, w_out, share_q, share_kv, out_sent, sems):
    sp, group = flags[0], flags[3]
    head = w_key.shape[0]
    quarter_depth, depth = share_q.shape[0], share_kv.shape[1]
    half_rows, quarter = out_sent.shape
    rows = pl.ds(pl.multiple_of((sp * 2 + group) * quarter_depth, 128), quarter_depth)
    deep = pl.ds(pl.multiple_of(sp * depth, 128), depth)
    columns = pl.ds(pl.multiple_of((flags[4] ^ 1) * quarter, 128), quarter)
    heads = pl.ds(pl.multiple_of(sp * half_rows, half_rows), half_rows)
    moves = (
        (w_query.at[rows], share_q),
        (w_key.at[:, deep], share_kv.at[:head]),
        (w_value.at[:, deep], share_kv.at[head:]),
        (w_out.at[heads, columns], out_sent),
    )
    copies = [pltpu.make_async_copy(a, b, sems.at[i]) for i, (a, b) in enumerate(moves)]
    for copy in copies:
        copy.start()
    for copy in copies:
        copy.wait()


def head_kernel(flags, came, other, w_out, out, sem):
    head, quarter = w_out.shape[0], out.shape[1]
    half_rows = came.shape[0]
    own = pl.ds(pl.multiple_of(flags[1] * head, head), head)
    columns = pl.ds(pl.multiple_of(flags[4] * quarter, 128), quarter)
    copy = pltpu.make_async_copy(w_out.at[:, columns], out.at[own], sem)
    copy.start()
    for i, piece in enumerate((came, other)):
        at = (1 - flags[1]) * head + (flags[0] ^ i) * half_rows
        out[pl.ds(pl.multiple_of(at, half_rows), half_rows)] = piece[...]
    copy.wait()


def project_kernel(peers, split, flags, *refs):
    stacked, pieces, outs = refs[:peers], list(refs[peers:-peers]), refs[-peers:]
    count, width = outs[0].shape
    rows = jnp.concatenate([m[...] for m in stacked], axis=0)
    step = 384 if width % 384 == 0 else width
    received = flags[2] != flags[0]
    for at in range(0, width, step):
        parts = [p[:, at : at + step] for p in pieces]
        if split:
            parts[-2:] = [jnp.where(received, parts[-2], parts[-1])]
        total = plain(rows, jnp.concatenate(parts, axis=0))
        for i, out in enumerate(outs):
            out[:, at : at + step] = total[i * count : (i + 1) * count].astype(out.dtype)


def assemble_kernel(flags, *refs):
    pieces, out, sems = refs[:-2], refs[-2], refs[-1]
    width = pieces[0].shape[1]
    copies = []
    for i, piece in enumerate(pieces):
        at = pl.multiple_of((flags[4] ^ i) * width, 128)
        copies.append(pltpu.make_async_copy(piece, out.at[:, pl.ds(at, width)], sems.at[i]))
        copies[-1].start()
    for copy in copies:
        copy.wait()


def local(tokens, w_query, w_key, w_value, w_out, doc_lengths):
    rows, width = tokens.shape
    tp_count = lax.axis_size("tp")
    sp_count = lax.axis_size("sp")
    sp_place = lax.axis_index("sp")
    tp_place = lax.axis_index("tp")
    group = lax.axis_index("groups") % 2
    slabs = tp_count // 2
    slab = tp_place // 2
    side = tp_place % 2
    head_dim = w_query.shape[1]
    short = slabs == 4
    is_inner = lambda t: (t >> 1) in (1, 2)

    if short:
        is_outer = lambda t: not is_inner(t)
        near_out = swap_tp(tokens, 2, is_outer)
        far = swap_tp(tokens, 4)
        near_in = swap_tp(tokens, 2, is_inner)
        middle = swap_tp(tokens, 6, is_inner)
        relayed = swap_tp(far, 2, is_inner)
        firsts, last = [tokens, near_out, near_in, far], [middle, relayed]
    else:
        came = [swap_tp(tokens, 2 * k) for k in range(1, slabs)]
        firsts, last = [tokens] + came[:-1], [came[-1], came[-1]]

    depth = width // sp_count
    quarter = w_out.shape[1] // 4
    half_rows = head_dim // sp_count
    mine = group * 2 + side
    inner = ((slab == 1) | (slab == 2)).astype(jnp.int32)
    flags = jnp.stack([sp_place, side, inner, group, mine, slab]).astype(jnp.int32)
    turned_kv = [w_key.T, w_value.T]
    core_low = sp_place == 0
    flags, doc_lengths, core_low = fence(flags, doc_lengths, core_low)
    share_q, share_kv, out_sent = call(
        cut_kernel,
        [
            ((depth // 2, head_dim), jnp.bfloat16),
            ((head_dim, depth), jnp.bfloat16),
            ((half_rows, quarter), jnp.bfloat16),
        ],
        [flags],
        [],
        [pltpu.SemaphoreType.DMA((4,))],
        pltpu.VMEM if short else pl.ANY,
        [pltpu.with_memory_space_constraint(x, pltpu.HBM) for x in (w_query, *turned_kv, w_out)],
    )
    came_q = swap_tp(share_q, 1)
    cross_q = swap_in_slab(came_q, 1, 0)
    came_kv = swap_tp(share_kv, 1)
    out_came = swap_tp(out_sent, 1)
    out_other = swap_sp(out_came)
    weights = [w_query, *turned_kv, came_kv, swap_sp(came_kv), came_q, cross_q]
    weights += [swap_sp(came_q), swap_sp(cross_q)]
    early = call(
        lambda *refs: early_kernel(short, *refs),
        [(((slabs - 1) * rows, 4 * head_dim), jnp.float32)],
        [flags],
        firsts + weights,
        [pltpu.VMEM((rows, width), jnp.bfloat16)],
    )[0]

    in_order = lambda a, b, flag: [jnp.where(flag, a, b), jnp.where(flag, b, a)]
    out_own = call(
        head_kernel,
        [((2 * head_dim, quarter), jnp.bfloat16)],
        [flags],
        [out_came, out_other],
        [pltpu.SemaphoreType.DMA(())],
        far=[w_out],
    )[0]
    if short:
        out_first = swap_by_core(out_own, (2, 4))
        out_swapped = swap_sp(out_first)

    count = slabs * rows
    half_head = head_dim // 2
    powers = np.arange(head_dim, dtype=np.float32) % half_head * np.float32(2.0 / head_dim)
    spread = jnp.asarray(np.power(np.float32(10000.0), -powers)[None, :])
    tables = call(
        lambda *refs: tables_kernel(slabs, sp_count, *refs),
        [((count, head_dim), jnp.float32)] * 2,
        [flags],
        [spread],
    )
    queries, key_value = call(
        tail_kernel,
        [((2 * count, head_dim), jnp.bfloat16), ((count, 2 * head_dim), jnp.bfloat16)],
        [flags],
        [early, *last, *tables] + weights,
        [pltpu.VMEM((rows, width), jnp.bfloat16)],
    )

    beside = swap_tp(key_value, 1)
    every = [key_value, beside, swap_sp(key_value), swap_sp(beside)]
    mixed = call(
        lambda *refs: attend_kernel(slabs, sp_count, *refs),
        [((rows, 2 * head_dim), jnp.bfloat16)] * slabs,
        [flags, doc_lengths],
        [queries] + every,
        limit=16 if short else 56,
    )

    parts = [mixed[0]]
    for k in range(1, slabs):
        parts.append(swap_tp(mixed[k], 2 * k))
    if short:
        parts[1:3] = in_order(parts[1], parts[2], core_low)
    merged = jnp.concatenate(parts, axis=1)
    peers = ((0, 0), (0, 1), (1, 0), (1, 1))
    stacked = [merged] + [swap_in_slab(merged, g, t) for g, t in peers[1:]]
    if short:
        out_sent = jnp.where(core_low, out_own, out_first)
        out_last = swap_by_core(out_sent, (6, 2), is_inner)
        out_last, stacked[2] = fence(out_last, stacked[2])
        pieces = [out_own, out_first, out_swapped, out_last, swap_sp(out_last)]
    else:
        pieces = [out_own]
        mine_of = lax.dynamic_slice_in_dim(out_own, sp_place * head_dim, head_dim, 0)
        for k in range(1, slabs):
            piece = swap_tp(mine_of, 2 * k)
            both = in_order(piece, swap_sp(piece), core_low)
            pieces.append(jnp.concatenate(both, axis=0))
    outs = call(
        lambda *refs: project_kernel(len(peers), short, *refs),
        [((rows, quarter), jnp.bfloat16)] * len(peers),
        [flags],
        stacked + pieces,
    )
    outs = [outs[0]] + [swap_in_slab(o, g, t) for o, (g, t) in zip(outs[1:], peers[1:])]
    sems = [pltpu.SemaphoreType.DMA((len(outs),))]
    shape = ((rows, width), jnp.bfloat16)
    return call(assemble_kernel, [shape], [flags], outs, sems, pl.ANY)[0]


def solution(mesh):
    placed = (
        P(("groups", "tp", "sp"), None),
        P(None, "tp"),
        P(None, "tp"),
        P(None, "tp"),
        P("tp", None),
        P("groups"),
    )

    return jax.shard_map(
        local,
        mesh=mesh,
        in_specs=placed,
        out_specs=P(("groups", "tp", "sp"), None),
        check_vma=False,
    )
```

```python
import jax
import jax.numpy as jnp
import numpy as np
from jax import lax
from jax.experimental import pallas as pl
from jax.experimental.pallas import tpu as pltpu
from jax.sharding import PartitionSpec as P

PRE_SCALE = 144

masked_low = -1e30


def swap_tp(block, flip, only=None):
    count = lax.axis_size("tp")
    route = [(t, t ^ flip) for t in range(count) if only is None or only(t)]
    return lax.ppermute(block, "tp", route)


def swap_sp(block):
    count = lax.axis_size("sp")
    return lax.ppermute(block, "sp", [(s, s ^ 1) for s in range(count)])


def swap_in_slab(block, group_flip, tp_flip):
    groups = lax.axis_size("groups")
    count = lax.axis_size("tp")
    route = [
        (g * count + t, (g ^ group_flip) * count + (t ^ tp_flip))
        for g in range(groups)
        for t in range(count)
    ]
    return lax.ppermute(block, ("groups", "tp"), route)


def fence(*values):
    return lax.optimization_barrier(values)


def call(kernel, shapes, scalars, operands, scratch=(), outs=pltpu.VMEM, far=(), limit=16):
    size = sum(x.size * x.dtype.itemsize for x in operands)
    params = None
    if size < 8 << 20:
        operands = [pltpu.with_memory_space_constraint(x, pltpu.VMEM) for x in operands]
        params = pltpu.CompilerParams(vmem_limit_bytes=limit << 20)
    specs = [pl.BlockSpec(memory_space=pltpu.SMEM)] * len(scalars)
    specs += [pl.BlockSpec(memory_space=pltpu.VMEM)] * len(operands)
    specs += [pl.BlockSpec(memory_space=pl.ANY)] * len(far)
    return pl.pallas_call(
        kernel,
        in_specs=specs,
        out_specs=[pl.BlockSpec(memory_space=outs)] * len(shapes),
        out_shape=[jax.ShapeDtypeStruct(*shape) for shape in shapes],
        scratch_shapes=list(scratch),
        compiler_params=params,
    )(*scalars, *operands, *far)


def plain(a, w):
    return jnp.dot(a, w, preferred_element_type=jnp.float32)


def turned(a, w):
    return lax.dot_general(a, w, (((1,), (1,)), ((), ())), preferred_element_type=jnp.float32)


def rows_at(blocks, offset, size):
    parts = [block[:, pl.ds(pl.multiple_of(offset, 128), size)] for block in blocks]
    return jnp.concatenate(parts, axis=0) if len(parts) > 1 else parts[0]


def products(blocks, weights, sp, group):
    w_query, w_key, w_value, kv_came, kv_other, *quarters = weights
    rows = jnp.concatenate([block[...] for block in blocks], axis=0)
    own_query = plain(rows, w_query[...])
    own_kv = turned(rows, jnp.concatenate([w_key[...], w_value[...]], axis=0))
    size = quarters[0].shape[0]
    pair_query = None
    for i, weight in enumerate(quarters):
        at = (sp ^ (i >> 1)) * 2 + (group ^ (i & 1))
        term = plain(rows_at(blocks, at * size, size), weight[...])
        pair_query = term if pair_query is None else pair_query + term
    depth = kv_came.shape[1]
    pair_kv = turned(rows_at(blocks, sp * depth, depth), kv_came[...]) + turned(
        rows_at(blocks, (1 - sp) * depth, depth), kv_other[...]
    )
    return own_query, own_kv, pair_query, pair_kv


def early_kernel(flags, *refs):
    blocks, weights, out = refs[:-10], refs[-10:-1], refs[-1]
    head = weights[0].shape[1]
    for i, part in enumerate(products(blocks, weights, flags[0], flags[3])):
        out[:, i * head : (i + 1) * head] = part


def tail_kernel(flags, early, middle, relayed, cosine, sine_part, *refs):
    weights, (queries, key_value, last) = refs[:9], refs[9:]
    side, inner = flags[1], flags[2]
    head = weights[0].shape[1]
    half_head = head // 2
    last[...] = jnp.where(inner != 0, middle[...], relayed[...])
    late = products([last], weights, flags[0], flags[3])
    join = lambda i: jnp.concatenate([early[:, i * head : (i + 1) * head], late[i]], axis=0)
    own_query, own_kv, pair_query, pair_kv = [join(i) for i in range(4)]
    spin = lambda v: v * cosine[...] + pltpu.roll(v, half_head, 1) * sine_part[...]
    scale = PRE_SCALE ** (-0.5)
    count = own_query.shape[0]
    queries[:count] = (spin(own_query) * scale).astype(queries.dtype)
    queries[count:] = (spin(pair_query) * scale).astype(queries.dtype)
    lane = lax.broadcasted_iota(jnp.int32, own_kv.shape, 1)
    low = lane < half_head
    even = side == 0
    first = jnp.where(even, own_kv, pair_kv)
    second = jnp.where(even, pair_kv, own_kv)
    key_raw = jnp.where(low, first, pltpu.roll(second, half_head, 1))
    key_raw = key_raw.astype(jnp.bfloat16).astype(jnp.float32)
    key_value[:, :head] = spin(key_raw).astype(key_value.dtype)
    value = jnp.where(low, pltpu.roll(first, half_head, 1), second)
    key_value[:, head:] = value.astype(key_value.dtype)


def place_of(flags, index, flip_side, flip_core, slabs, rows, cores):
    block = jnp.zeros_like(index)
    for k in range(1, slabs):
        block = block + (index >= k * rows).astype(jnp.int32)
    at = (flags[5] ^ block) * 2 + (flags[1] ^ flip_side)
    return (at * cores + (flags[0] ^ flip_core)) * rows + index - block * rows


def tables_kernel(slabs, cores, flags, spread, cosine, sine_part):
    shape = cosine.shape
    index = lax.broadcasted_iota(jnp.int32, shape, 0)
    places = place_of(flags, index, 0, 0, slabs, shape[0] // slabs, cores)
    angles = places.astype(jnp.float32) * spread[...]
    cosine[...] = jnp.cos(angles)
    sines = jnp.sin(angles)
    low = lax.broadcasted_iota(jnp.int32, shape, 1) < shape[1] // 2
    sine_part[...] = jnp.where(low, -sines, sines)


def attend_kernel(slabs, cores, flags, lengths, queries, *refs):
    pieces, outs = refs[:4], refs[4:]
    count, head = pieces[0].shape[0], queries.shape[1]
    rows = count // slabs
    place = lambda shape, axis, a, b: place_of(
        flags, lax.broadcasted_iota(jnp.int32, shape, axis), a, b, slabs, rows, cores
    )
    end = 0
    ends = []
    for i in range(lengths.shape[0]):
        end = end + lengths[i]
        ends.append(end)
    step = min(count, 4 * rows)
    even = flags[1] == 0
    for at in range(0, count, step):
        index = at + lax.broadcasted_iota(jnp.int32, (step, 1), 0)
        query_places = place_of(flags, index, 0, 0, slabs, rows, cores)
        starts = jnp.zeros_like(query_places)
        for end in ends:
            starts = jnp.where(query_places >= end, end, starts)
        masks = []
        for c in range(4):
            key_places = place((1, count), 1, c % 2, c // 2)
            masks.append((key_places <= query_places) & (key_places >= starts))
        mixed = []
        for h in range(2):
            query = queries[h * count + at : h * count + at + step]
            scores = [
                jnp.where(mask, turned(query, piece[:, :head]), masked_low)
                for piece, mask in zip(pieces, masks)
            ]
            largest = scores[0]
            for part in scores[1:]:
                largest = jnp.maximum(largest, part)
            largest = jnp.max(largest, axis=1, keepdims=True)
            total, acc = 0.0, 0.0
            for part, piece, mask in zip(scores, pieces, masks):
                e = jnp.where(mask, jnp.exp(part - largest), 0.0)
                total = total + e
                acc = acc + plain(e.astype(jnp.bfloat16), piece[:, head:])
            total = jnp.sum(total, axis=1, keepdims=True)
            mixed.append((acc / total).astype(jnp.bfloat16))
        low = jnp.where(even, mixed[0], mixed[1])
        high = jnp.where(even, mixed[1], mixed[0])
        for k in range(step // rows):
            out = outs[at // rows + k]
            out[:, :head] = low[k * rows : (k + 1) * rows]
            out[:, head:] = high[k * rows : (k + 1) * rows]


def cut_kernel(flags, w_query, w_key, w_value, w_out, share_q, share_kv, out_sent, sems):
    sp, group = flags[0], flags[3]
    head = w_key.shape[0]
    quarter_depth, depth = share_q.shape[0], share_kv.shape[1]
    half_rows, quarter = out_sent.shape
    rows = pl.ds(pl.multiple_of((sp * 2 + group) * quarter_depth, 128), quarter_depth)
    deep = pl.ds(pl.multiple_of(sp * depth, 128), depth)
    columns = pl.ds(pl.multiple_of((flags[4] ^ 1) * quarter, 128), quarter)
    heads = pl.ds(pl.multiple_of(sp * half_rows, half_rows), half_rows)
    moves = (
        (w_query.at[rows], share_q),
        (w_key.at[:, deep], share_kv.at[:head]),
        (w_value.at[:, deep], share_kv.at[head:]),
        (w_out.at[heads, columns], out_sent),
    )
    copies = [pltpu.make_async_copy(a, b, sems.at[i]) for i, (a, b) in enumerate(moves)]
    for copy in copies:
        copy.start()
    for copy in copies:
        copy.wait()


def head_kernel(flags, came, other, w_out, out, out_head, sem):
    head, quarter = w_out.shape[0], out.shape[1]
    half_rows = came.shape[0]
    own = pl.ds(pl.multiple_of(flags[1] * head, head), head)
    columns = pl.ds(pl.multiple_of(flags[4] * quarter, 128), quarter)
    copy = pltpu.make_async_copy(w_out.at[:, columns], out.at[own], sem)
    copy.start()
    for i, piece in enumerate((came, other)):
        at = (1 - flags[1]) * head + (flags[0] ^ i) * half_rows
        out[pl.ds(pl.multiple_of(at, half_rows), half_rows)] = piece[...]
    copy.wait()
    out_head[...] = out[pl.ds(pl.multiple_of(flags[0] * head, head), head)]


def project_kernel(peers, flags, *refs):
    stacked, pieces, outs = refs[:peers], list(refs[peers:-peers]), refs[-peers:]
    count, width = outs[0].shape
    rows = jnp.concatenate([m[...] for m in stacked], axis=0)
    step = 384 if width % 384 == 0 else width
    low = flags[0] == 0
    for at in range(0, width, step):
        tiles = [p[:, at : at + step] for p in pieces]
        parts = tiles[:1]
        for mine, other in zip(tiles[1::2], tiles[2::2]):
            parts += [jnp.where(low, mine, other), jnp.where(low, other, mine)]
        total = plain(rows, jnp.concatenate(parts, axis=0))
        for i, out in enumerate(outs):
            out[:, at : at + step] = total[i * count : (i + 1) * count].astype(out.dtype)


def merge_kernel(flags, *refs):
    parts, out = refs[:-1], refs[-1]
    width = parts[0].shape[1]
    for i, part in enumerate(parts):
        out[:, i * width : (i + 1) * width] = part[...]


def assemble_kernel(flags, *refs):
    pieces, out, sems = refs[:-2], refs[-2], refs[-1]
    width = pieces[0].shape[1]
    copies = []
    for i, piece in enumerate(pieces):
        at = pl.multiple_of((flags[4] ^ i) * width, 128)
        copies.append(pltpu.make_async_copy(piece, out.at[:, pl.ds(at, width)], sems.at[i]))
        copies[-1].start()
    for copy in copies:
        copy.wait()


def local(tokens, w_query, w_key, w_value, w_out, doc_lengths):
    rows, width = tokens.shape
    tp_count = lax.axis_size("tp")
    sp_count = lax.axis_size("sp")
    sp_place = lax.axis_index("sp")
    tp_place = lax.axis_index("tp")
    group = lax.axis_index("groups") % 2
    slabs = tp_count // 2
    slab = tp_place // 2
    side = tp_place % 2
    head_dim = w_query.shape[1]
    short = slabs == 4
    is_inner = lambda t: (t >> 1) in (1, 2)

    if short:
        far = swap_tp(tokens, 4)
        near = swap_tp(tokens, 2)
        middle = swap_tp(tokens, 6, is_inner)
        relayed = swap_tp(far, 2, is_inner)
        firsts, last = [tokens, near, far], [middle, relayed]
    else:
        came = [swap_tp(tokens, 2 * k) for k in range(1, slabs)]
        firsts, last = [tokens] + came[:-1], [came[-1], came[-1]]

    depth = width // sp_count
    quarter = w_out.shape[1] // 4
    half_rows = head_dim // sp_count
    mine = group * 2 + side
    inner = ((slab == 1) | (slab == 2)).astype(jnp.int32)
    flags = jnp.stack([sp_place, side, inner, group, mine, slab]).astype(jnp.int32)
    turned_kv = [w_key.T, w_value.T]
    is_inside = inner != 0
    flags, doc_lengths, is_inside = fence(flags, doc_lengths, is_inside)
    share_q, share_kv, out_sent = call(
        cut_kernel,
        [
            ((depth // 2, head_dim), jnp.bfloat16),
            ((head_dim, depth), jnp.bfloat16),
            ((half_rows, quarter), jnp.bfloat16),
        ],
        [flags],
        [],
        [pltpu.SemaphoreType.DMA((4,))],
        pltpu.VMEM if short else pl.ANY,
        [pltpu.with_memory_space_constraint(x, pltpu.HBM) for x in (w_query, *turned_kv, w_out)],
    )
    came_q = swap_tp(share_q, 1)
    cross_q = swap_in_slab(came_q, 1, 0)
    came_kv = swap_tp(share_kv, 1)
    out_came = swap_tp(out_sent, 1)
    out_other = swap_sp(out_came)
    weights = [w_query, *turned_kv, came_kv, swap_sp(came_kv), came_q, cross_q]
    weights += [swap_sp(came_q), swap_sp(cross_q)]
    early = call(
        early_kernel, [((len(firsts) * rows, 4 * head_dim), jnp.float32)], [flags], firsts + weights
    )[0]

    out_own, out_head = call(
        head_kernel,
        [((2 * head_dim, quarter), jnp.bfloat16), ((head_dim, quarter), jnp.bfloat16)],
        [flags],
        [out_came, out_other],
        [pltpu.SemaphoreType.DMA(())],
        far=[w_out],
    )
    if short:
        out_far = swap_tp(out_head, 4)
        out_near = swap_tp(out_head, 2)

    count = slabs * rows
    half_head = head_dim // 2
    powers = np.arange(head_dim, dtype=np.float32) % half_head * np.float32(2.0 / head_dim)
    spread = jnp.asarray(np.power(np.float32(10000.0), -powers)[None, :])
    tables = call(
        lambda *refs: tables_kernel(slabs, sp_count, *refs),
        [((count, head_dim), jnp.float32)] * 2,
        [flags],
        [spread],
    )
    queries, key_value = call(
        tail_kernel,
        [((2 * count, head_dim), jnp.bfloat16), ((count, 2 * head_dim), jnp.bfloat16)],
        [flags],
        [early, *last, *tables] + weights,
        [pltpu.VMEM((rows, width), jnp.bfloat16)],
    )

    beside = swap_tp(key_value, 1)
    every = [key_value, beside, swap_sp(key_value), swap_sp(beside)]
    mixed = call(
        lambda *refs: attend_kernel(slabs, sp_count, *refs),
        [((rows, 2 * head_dim), jnp.bfloat16)] * slabs,
        [flags, doc_lengths],
        [queries] + every,
        limit=16 if short else 56,
    )

    parts = [mixed[0]]
    for k in range(1, slabs):
        parts.append(swap_tp(mixed[k], 2 * k))
    shape = ((rows, slabs * 2 * head_dim), jnp.bfloat16)
    merged = call(merge_kernel, [shape], [flags], parts)[0]
    peers = ((0, 0), (0, 1), (1, 0), (1, 1))
    stacked = [merged] + [swap_in_slab(merged, g, t) for g, t in peers[1:]]
    if short:
        out_relay = swap_tp(out_far, 2, is_inner)
        out_middle = swap_tp(out_head, 6, is_inner)
        out_relay, out_middle, stacked[2] = fence(out_relay, out_middle, stacked[2])
        others = [out_near, out_far, jnp.where(is_inside, out_middle, out_relay)]
    else:
        others = [swap_tp(out_head, 2 * k) for k in range(1, slabs)]
    pieces = [out_own]
    for piece in others:
        pieces += [piece, swap_sp(piece)]
    outs = call(
        lambda *refs: project_kernel(len(peers), *refs),
        [((rows, quarter), jnp.bfloat16)] * len(peers),
        [flags],
        stacked + pieces,
    )
    outs = [outs[0]] + [swap_in_slab(o, g, t) for o, (g, t) in zip(outs[1:], peers[1:])]
    sems = [pltpu.SemaphoreType.DMA((len(outs),))]
    shape = ((rows, width), jnp.bfloat16)
    return call(assemble_kernel, [shape], [flags], outs, sems, pl.ANY)[0]


def solution(mesh):
    placed = (
        P(("groups", "tp", "sp"), None),
        P(None, "tp"),
        P(None, "tp"),
        P(None, "tp"),
        P("tp", None),
        P("groups"),
    )

    return jax.shard_map(
        local,
        mesh=mesh,
        in_specs=placed,
        out_specs=P(("groups", "tp", "sp"), None),
        check_vma=False,
    )
```

```python
import jax
import jax.numpy as jnp
import numpy as np
from jax import lax
from jax.experimental import pallas as pl
from jax.experimental.pallas import tpu as pltpu
from jax.sharding import PartitionSpec as P

PRE_SCALE = 144

masked_low = -1e30


def swap_tp(block, flip, only=None):
    count = lax.axis_size("tp")
    route = [(t, t ^ flip) for t in range(count) if only is None or only(t)]
    return lax.ppermute(block, "tp", route)


def swap_sp(block):
    count = lax.axis_size("sp")
    return lax.ppermute(block, "sp", [(s, s ^ 1) for s in range(count)])


def swap_by_core(block, flips, only=lambda t: True):
    count, cores = lax.axis_size("tp"), lax.axis_size("sp")
    route = [
        (t * cores + s, (t ^ flips[s]) * cores + s)
        for t in range(count)
        for s in range(cores)
        if only(t)
    ]
    return lax.ppermute(block, ("tp", "sp"), route)


def swap_in_slab(block, group_flip, tp_flip):
    groups = lax.axis_size("groups")
    count = lax.axis_size("tp")
    route = [
        (g * count + t, (g ^ group_flip) * count + (t ^ tp_flip))
        for g in range(groups)
        for t in range(count)
    ]
    return lax.ppermute(block, ("groups", "tp"), route)


def fence(*values):
    return lax.optimization_barrier(values)


def call(kernel, shapes, scalars, operands, scratch=(), outs=pltpu.VMEM, far=(), limit=16):
    size = sum(x.size * x.dtype.itemsize for x in operands)
    params = None
    if size < 8 << 20:
        operands = [pltpu.with_memory_space_constraint(x, pltpu.VMEM) for x in operands]
        params = pltpu.CompilerParams(vmem_limit_bytes=limit << 20)
    specs = [pl.BlockSpec(memory_space=pltpu.SMEM)] * len(scalars)
    specs += [pl.BlockSpec(memory_space=pltpu.VMEM)] * len(operands)
    specs += [pl.BlockSpec(memory_space=pl.ANY)] * len(far)
    return pl.pallas_call(
        kernel,
        in_specs=specs,
        out_specs=[pl.BlockSpec(memory_space=outs)] * len(shapes),
        out_shape=[jax.ShapeDtypeStruct(*shape) for shape in shapes],
        scratch_shapes=list(scratch),
        compiler_params=params,
    )(*scalars, *operands, *far)


def plain(a, w):
    return jnp.dot(a, w, preferred_element_type=jnp.float32)


def turned(a, w):
    return lax.dot_general(a, w, (((1,), (1,)), ((), ())), preferred_element_type=jnp.float32)


def rows_at(blocks, offset, size):
    parts = [block[:, pl.ds(pl.multiple_of(offset, 128), size)] for block in blocks]
    return jnp.concatenate(parts, axis=0) if len(parts) > 1 else parts[0]


def products(blocks, weights, sp, group):
    w_query, w_key, w_value, kv_came, kv_other, *quarters = weights
    rows = jnp.concatenate([block[...] for block in blocks], axis=0)
    own_query = plain(rows, w_query[...])
    own_kv = turned(rows, jnp.concatenate([w_key[...], w_value[...]], axis=0))
    size = quarters[0].shape[0]
    pair_query = None
    for i, weight in enumerate(quarters):
        at = (sp ^ (i >> 1)) * 2 + (group ^ (i & 1))
        term = plain(rows_at(blocks, at * size, size), weight[...])
        pair_query = term if pair_query is None else pair_query + term
    depth = kv_came.shape[1]
    pair_kv = turned(rows_at(blocks, sp * depth, depth), kv_came[...]) + turned(
        rows_at(blocks, (1 - sp) * depth, depth), kv_other[...]
    )
    return own_query, own_kv, pair_query, pair_kv


def early_kernel(flags, *refs):
    blocks, weights, out = refs[:-10], refs[-10:-1], refs[-1]
    head = weights[0].shape[1]
    for i, part in enumerate(products(blocks, weights, flags[0], flags[3])):
        out[:, i * head : (i + 1) * head] = part


def tail_kernel(flags, early, middle, relayed, cosine, sine_part, *refs):
    weights, (queries, key_value, last) = refs[:9], refs[9:]
    side, inner = flags[1], flags[2]
    head = weights[0].shape[1]
    half_head = head // 2
    last[...] = jnp.where(inner != 0, middle[...], relayed[...])
    late = products([last], weights, flags[0], flags[3])
    join = lambda i: jnp.concatenate([early[:, i * head : (i + 1) * head], late[i]], axis=0)
    own_query, own_kv, pair_query, pair_kv = [join(i) for i in range(4)]
    spin = lambda v: v * cosine[...] + pltpu.roll(v, half_head, 1) * sine_part[...]
    scale = PRE_SCALE ** (-0.5)
    count = own_query.shape[0]
    queries[:count] = (spin(own_query) * scale).astype(queries.dtype)
    queries[count:] = (spin(pair_query) * scale).astype(queries.dtype)
    lane = lax.broadcasted_iota(jnp.int32, own_kv.shape, 1)
    low = lane < half_head
    even = side == 0
    first = jnp.where(even, own_kv, pair_kv)
    second = jnp.where(even, pair_kv, own_kv)
    key_raw = jnp.where(low, first, pltpu.roll(second, half_head, 1))
    key_raw = key_raw.astype(jnp.bfloat16).astype(jnp.float32)
    key_value[:, :head] = spin(key_raw).astype(key_value.dtype)
    value = jnp.where(low, pltpu.roll(first, half_head, 1), second)
    key_value[:, head:] = value.astype(key_value.dtype)


def place_of(flags, index, flip_side, flip_core, slabs, rows, cores):
    block = jnp.zeros_like(index)
    for k in range(1, slabs):
        block = block + (index >= k * rows).astype(jnp.int32)
    at = (flags[5] ^ block) * 2 + (flags[1] ^ flip_side)
    return (at * cores + (flags[0] ^ flip_core)) * rows + index - block * rows


def tables_kernel(slabs, cores, flags, spread, cosine, sine_part):
    shape = cosine.shape
    index = lax.broadcasted_iota(jnp.int32, shape, 0)
    places = place_of(flags, index, 0, 0, slabs, shape[0] // slabs, cores)
    angles = places.astype(jnp.float32) * spread[...]
    cosine[...] = jnp.cos(angles)
    sines = jnp.sin(angles)
    low = lax.broadcasted_iota(jnp.int32, shape, 1) < shape[1] // 2
    sine_part[...] = jnp.where(low, -sines, sines)


def attend_kernel(slabs, cores, flags, lengths, queries, *refs):
    pieces, outs = refs[:4], refs[4:]
    count, head = pieces[0].shape[0], queries.shape[1]
    rows = count // slabs
    end = 0
    ends = []
    for i in range(lengths.shape[0]):
        end = end + lengths[i]
        ends.append(end)
    even = flags[1] == 0
    reach = max(1, -(-slabs // 4))
    for j in range(slabs):
        slab = flags[5] ^ j
        index = j * rows + lax.broadcasted_iota(jnp.int32, (rows, 1), 0)
        query_places = place_of(flags, index, 0, 0, slabs, rows, cores)
        starts = jnp.zeros_like(query_places)
        for end in ends:
            starts = jnp.where(query_places >= end, end, starts)
        keys, values, key_places = [], [], []
        for back in range(reach + 1):
            held = jnp.maximum(slab - back, 0)
            at = pl.ds(pl.multiple_of((held ^ flags[5]) * rows, 16), rows)
            for c, piece in enumerate(pieces):
                keys.append(piece[at, :head])
                values.append(piece[at, head:])
                first = ((slab - back) * 2 + (flags[1] ^ (c % 2))) * cores + (flags[0] ^ (c // 2))
                key_places.append(first * rows)
        lane = lax.broadcasted_iota(jnp.int32, (1, len(keys) * rows), 1)
        place = key_places[0] + lane
        for i in range(1, len(keys)):
            place = jnp.where(lane >= i * rows, key_places[i] + lane - i * rows, place)
        mask = (place <= query_places) & (place >= starts)
        mask = jnp.concatenate([mask, mask], axis=0)
        query = jnp.concatenate(
            [queries[h * count + j * rows : h * count + (j + 1) * rows] for h in range(2)], axis=0
        )
        scores = turned(query, jnp.concatenate(keys, axis=0))
        scores = jnp.where(mask, scores, masked_low)
        largest = jnp.max(scores, axis=1, keepdims=True)
        e = jnp.where(mask, jnp.exp(scores - largest), 0.0)
        total = jnp.sum(e, axis=1, keepdims=True)
        mixed = plain(e.astype(jnp.bfloat16), jnp.concatenate(values, axis=0)) / total
        mixed = mixed.astype(jnp.bfloat16)
        outs[j][:, :head] = jnp.where(even, mixed[:rows], mixed[rows:])
        outs[j][:, head:] = jnp.where(even, mixed[rows:], mixed[:rows])


def cut_kernel(flags, w_query, w_key, w_value, w_out, share_q, share_kv, out_sent, sems):
    sp, group = flags[0], flags[3]
    head = w_key.shape[0]
    quarter_depth, depth = share_q.shape[0], share_kv.shape[1]
    half_rows, quarter = out_sent.shape
    rows = pl.ds(pl.multiple_of((sp * 2 + group) * quarter_depth, 128), quarter_depth)
    deep = pl.ds(pl.multiple_of(sp * depth, 128), depth)
    columns = pl.ds(pl.multiple_of((flags[4] ^ 1) * quarter, 128), quarter)
    heads = pl.ds(pl.multiple_of(sp * half_rows, half_rows), half_rows)
    moves = (
        (w_query.at[rows], share_q),
        (w_key.at[:, deep], share_kv.at[:head]),
        (w_value.at[:, deep], share_kv.at[head:]),
        (w_out.at[heads, columns], out_sent),
    )
    copies = [pltpu.make_async_copy(a, b, sems.at[i]) for i, (a, b) in enumerate(moves)]
    for copy in copies:
        copy.start()
    for copy in copies:
        copy.wait()


def head_kernel(flags, came, other, w_out, out, sem):
    head, quarter = w_out.shape[0], out.shape[1]
    half_rows = came.shape[0]
    own = pl.ds(pl.multiple_of(flags[1] * head, head), head)
    columns = pl.ds(pl.multiple_of(flags[4] * quarter, 128), quarter)
    copy = pltpu.make_async_copy(w_out.at[:, columns], out.at[own], sem)
    copy.start()
    for i, piece in enumerate((came, other)):
        at = (1 - flags[1]) * head + (flags[0] ^ i) * half_rows
        out[pl.ds(pl.multiple_of(at, half_rows), half_rows)] = piece[...]
    copy.wait()


def tiles_of(width):
    step = 384 if width % 384 == 0 else width
    return [(at, at + step) for at in range(0, width, step)]


def begin_kernel(peers, flags, *refs):
    stacked, pieces, out = refs[:peers], refs[peers:-1], refs[-1]
    inner = sum(piece.shape[0] for piece in pieces)
    rows = jnp.concatenate([m[:, :inner] for m in stacked], axis=0)
    for a, b in tiles_of(out.shape[1]):
        out[:, a:b] = plain(rows, jnp.concatenate([p[:, a:b] for p in pieces], axis=0))


def finish_kernel(peers, flags, *refs):
    stacked, (begun, came, other), outs = refs[:peers], refs[peers:-peers], refs[-peers:]
    count, width = outs[0].shape
    inner = stacked[0].shape[1] - came.shape[0]
    rows = jnp.concatenate([m[:, inner:] for m in stacked], axis=0)
    received = flags[2] != flags[0]
    for a, b in tiles_of(width):
        weight = jnp.where(received, came[:, a:b], other[:, a:b])
        total = begun[:, a:b] + plain(rows, weight)
        for i, out in enumerate(outs):
            out[:, a:b] = total[i * count : (i + 1) * count].astype(out.dtype)


def assemble_kernel(flags, *refs):
    pieces, out, sems = refs[:-2], refs[-2], refs[-1]
    width = pieces[0].shape[1]
    copies = []
    for i, piece in enumerate(pieces):
        at = pl.multiple_of((flags[4] ^ i) * width, 128)
        copies.append(pltpu.make_async_copy(piece, out.at[:, pl.ds(at, width)], sems.at[i]))
        copies[-1].start()
    for copy in copies:
        copy.wait()


def local(tokens, w_query, w_key, w_value, w_out, doc_lengths):
    rows, width = tokens.shape
    tp_count = lax.axis_size("tp")
    sp_count = lax.axis_size("sp")
    sp_place = lax.axis_index("sp")
    tp_place = lax.axis_index("tp")
    group = lax.axis_index("groups") % 2
    slabs = tp_count // 2
    slab = tp_place // 2
    side = tp_place % 2
    head_dim = w_query.shape[1]
    short = slabs == 4
    is_inner = lambda t: (t >> 1) in (1, 2)

    if short:
        far = swap_tp(tokens, 4)
        near = swap_tp(tokens, 2)
        middle = swap_tp(tokens, 6, is_inner)
        relayed = swap_tp(far, 2, is_inner)
        firsts, last = [tokens, near, far], [middle, relayed]
    else:
        came = [swap_tp(tokens, 2 * k) for k in range(1, slabs)]
        firsts, last = [tokens] + came[:-1], [came[-1], came[-1]]

    depth = width // sp_count
    quarter = w_out.shape[1] // 4
    half_rows = head_dim // sp_count
    mine = group * 2 + side
    inner = ((slab == 1) | (slab == 2)).astype(jnp.int32)
    flags = jnp.stack([sp_place, side, inner, group, mine, slab]).astype(jnp.int32)
    turned_kv = [w_key.T, w_value.T]
    core_low = sp_place == 0
    flags, doc_lengths, core_low = fence(flags, doc_lengths, core_low)
    share_q, share_kv, out_sent = call(
        cut_kernel,
        [
            ((depth // 2, head_dim), jnp.bfloat16),
            ((head_dim, depth), jnp.bfloat16),
            ((half_rows, quarter), jnp.bfloat16),
        ],
        [flags],
        [],
        [pltpu.SemaphoreType.DMA((4,))],
        pltpu.VMEM if short else pl.ANY,
        [pltpu.with_memory_space_constraint(x, pltpu.HBM) for x in (w_query, *turned_kv, w_out)],
    )
    came_q = swap_tp(share_q, 1)
    cross_q = swap_in_slab(came_q, 1, 0)
    came_kv = swap_tp(share_kv, 1)
    out_came = swap_tp(out_sent, 1)
    out_other = swap_sp(out_came)
    weights = [w_query, *turned_kv, came_kv, swap_sp(came_kv), came_q, cross_q]
    weights += [swap_sp(came_q), swap_sp(cross_q)]
    early = call(
        early_kernel, [((len(firsts) * rows, 4 * head_dim), jnp.float32)], [flags], firsts + weights
    )[0]

    in_order = lambda a, b, flag: [jnp.where(flag, a, b), jnp.where(flag, b, a)]
    out_own = call(
        head_kernel,
        [((2 * head_dim, quarter), jnp.bfloat16)],
        [flags],
        [out_came, out_other],
        [pltpu.SemaphoreType.DMA(())],
        far=[w_out],
    )[0]
    if short:
        out_first = swap_by_core(out_own, (2, 4))
        out_swapped = swap_sp(out_first)

    count = slabs * rows
    half_head = head_dim // 2
    powers = np.arange(head_dim, dtype=np.float32) % half_head * np.float32(2.0 / head_dim)
    spread = jnp.asarray(np.power(np.float32(10000.0), -powers)[None, :])
    tables = call(
        lambda *refs: tables_kernel(slabs, sp_count, *refs),
        [((count, head_dim), jnp.float32)] * 2,
        [flags],
        [spread],
    )
    queries, key_value = call(
        tail_kernel,
        [((2 * count, head_dim), jnp.bfloat16), ((count, 2 * head_dim), jnp.bfloat16)],
        [flags],
        [early, *last, *tables] + weights,
        [pltpu.VMEM((rows, width), jnp.bfloat16)],
    )

    beside = swap_tp(key_value, 1)
    every = [key_value, beside, swap_sp(key_value), swap_sp(beside)]
    mixed = call(
        lambda *refs: attend_kernel(slabs, sp_count, *refs),
        [((rows, 2 * head_dim), jnp.bfloat16)] * slabs,
        [flags, doc_lengths],
        [queries] + every,
        limit=16 if short else 56,
    )

    parts = [mixed[0]]
    for k in range(1, slabs):
        parts.append(swap_tp(mixed[k], 2 * k))
    if short:
        parts[1:3] = in_order(parts[1], parts[2], core_low)
    merged = jnp.concatenate(parts, axis=1)
    peers = ((0, 0), (0, 1), (1, 0), (1, 1))
    stacked = [merged] + [swap_in_slab(merged, g, t) for g, t in peers[1:]]
    if short:
        out_sent = jnp.where(core_low, out_own, out_first)
        out_last = swap_by_core(out_sent, (6, 2), is_inner)
        out_last, stacked[2] = fence(out_last, stacked[2])
        pieces = [out_own, out_first, out_swapped, out_last, swap_sp(out_last)]
    else:
        pieces = [out_own]
        mine_of = lax.dynamic_slice_in_dim(out_own, sp_place * head_dim, head_dim, 0)
        for k in range(1, slabs):
            piece = swap_tp(mine_of, 2 * k)
            both = in_order(piece, swap_sp(piece), core_low)
            pieces.append(jnp.concatenate(both, axis=0))
    if not short:
        pieces.append(pieces[-1])
    count, kept = len(peers), pieces[:-2]
    begun = call(
        lambda *refs: begin_kernel(count, *refs),
        [((count * rows, quarter), jnp.float32)],
        [flags],
        stacked + kept,
    )
    outs = call(
        lambda *refs: finish_kernel(count, *refs),
        [((rows, quarter), jnp.bfloat16)] * count,
        [flags],
        stacked + list(begun) + pieces[-2:],
    )
    outs = [outs[0]] + [swap_in_slab(o, g, t) for o, (g, t) in zip(outs[1:], peers[1:])]
    sems = [pltpu.SemaphoreType.DMA((len(outs),))]
    shape = ((rows, width), jnp.bfloat16)
    return call(assemble_kernel, [shape], [flags], outs, sems, pl.ANY)[0]


def solution(mesh):
    placed = (
        P(("groups", "tp", "sp"), None),
        P(None, "tp"),
        P(None, "tp"),
        P(None, "tp"),
        P("tp", None),
        P("groups"),
    )

    return jax.shard_map(
        local,
        mesh=mesh,
        in_specs=placed,
        out_specs=P(("groups", "tp", "sp"), None),
        check_vma=False,
    )
```

```python
import jax
import jax.numpy as jnp
import numpy as np
from jax import lax
from jax.experimental import pallas as pl
from jax.experimental.pallas import tpu as pltpu
from jax.sharding import PartitionSpec as P

PRE_SCALE = 144

masked_low = -1e30


def swap_tp(block, flip, only=None):
    count = lax.axis_size("tp")
    route = [(t, t ^ flip) for t in range(count) if only is None or only(t)]
    return lax.ppermute(block, "tp", route)


def swap_sp(block):
    count = lax.axis_size("sp")
    return lax.ppermute(block, "sp", [(s, s ^ 1) for s in range(count)])


def swap_by_core(block, flips, only=lambda t: True):
    count, cores = lax.axis_size("tp"), lax.axis_size("sp")
    route = [
        (t * cores + s, (t ^ flips[s]) * cores + s)
        for t in range(count)
        for s in range(cores)
        if only(t)
    ]
    return lax.ppermute(block, ("tp", "sp"), route)


def swap_in_slab(block, group_flip, tp_flip):
    groups = lax.axis_size("groups")
    count = lax.axis_size("tp")
    route = [
        (g * count + t, (g ^ group_flip) * count + (t ^ tp_flip))
        for g in range(groups)
        for t in range(count)
    ]
    return lax.ppermute(block, ("groups", "tp"), route)


def fence(*values):
    return lax.optimization_barrier(values)


def call(kernel, shapes, scalars, operands, scratch=(), outs=pltpu.VMEM, far=(), limit=16):
    size = sum(x.size * x.dtype.itemsize for x in operands)
    params = None
    if size < 8 << 20:
        operands = [pltpu.with_memory_space_constraint(x, pltpu.VMEM) for x in operands]
        params = pltpu.CompilerParams(vmem_limit_bytes=limit << 20)
    specs = [pl.BlockSpec(memory_space=pltpu.SMEM)] * len(scalars)
    specs += [pl.BlockSpec(memory_space=pltpu.VMEM)] * len(operands)
    specs += [pl.BlockSpec(memory_space=pl.ANY)] * len(far)
    return pl.pallas_call(
        kernel,
        in_specs=specs,
        out_specs=[pl.BlockSpec(memory_space=outs)] * len(shapes),
        out_shape=[jax.ShapeDtypeStruct(*shape) for shape in shapes],
        scratch_shapes=list(scratch),
        compiler_params=params,
    )(*scalars, *operands, *far)


def plain(a, w):
    return jnp.dot(a, w, preferred_element_type=jnp.float32)


def turned(a, w):
    return lax.dot_general(a, w, (((1,), (1,)), ((), ())), preferred_element_type=jnp.float32)


def rows_at(blocks, offset, size):
    parts = [block[:, pl.ds(pl.multiple_of(offset, 128), size)] for block in blocks]
    return jnp.concatenate(parts, axis=0) if len(parts) > 1 else parts[0]


def products(blocks, weights, sp, group):
    w_query, w_key, w_value, kv_came, kv_other, *quarters = weights
    rows = jnp.concatenate([block[...] for block in blocks], axis=0)
    own_query = plain(rows, w_query[...])
    own_kv = turned(rows, jnp.concatenate([w_key[...], w_value[...]], axis=0))
    size = quarters[0].shape[0]
    pair_query = None
    for i, weight in enumerate(quarters):
        at = (sp ^ (i >> 1)) * 2 + (group ^ (i & 1))
        term = plain(rows_at(blocks, at * size, size), weight[...])
        pair_query = term if pair_query is None else pair_query + term
    depth = kv_came.shape[1]
    pair_kv = turned(rows_at(blocks, sp * depth, depth), kv_came[...]) + turned(
        rows_at(blocks, (1 - sp) * depth, depth), kv_other[...]
    )
    return own_query, own_kv, pair_query, pair_kv


def early_kernel(flags, *refs):
    blocks, weights, out = refs[:-10], refs[-10:-1], refs[-1]
    head = weights[0].shape[1]
    for i, part in enumerate(products(blocks, weights, flags[0], flags[3])):
        out[:, i * head : (i + 1) * head] = part


def tail_kernel(flags, early, middle, relayed, cosine, sine_part, *refs):
    weights, (queries, key_value, last) = refs[:9], refs[9:]
    side, inner = flags[1], flags[2]
    head = weights[0].shape[1]
    half_head = head // 2
    last[...] = jnp.where(inner != 0, middle[...], relayed[...])
    late = products([last], weights, flags[0], flags[3])
    join = lambda i: jnp.concatenate([early[:, i * head : (i + 1) * head], late[i]], axis=0)
    own_query, own_kv, pair_query, pair_kv = [join(i) for i in range(4)]
    spin = lambda v: v * cosine[...] + pltpu.roll(v, half_head, 1) * sine_part[...]
    scale = PRE_SCALE ** (-0.5)
    count = own_query.shape[0]
    queries[:count] = (spin(own_query) * scale).astype(queries.dtype)
    queries[count:] = (spin(pair_query) * scale).astype(queries.dtype)
    lane = lax.broadcasted_iota(jnp.int32, own_kv.shape, 1)
    low = lane < half_head
    even = side == 0
    first = jnp.where(even, own_kv, pair_kv)
    second = jnp.where(even, pair_kv, own_kv)
    key_raw = jnp.where(low, first, pltpu.roll(second, half_head, 1))
    key_raw = key_raw.astype(jnp.bfloat16).astype(jnp.float32)
    key_value[:, :head] = spin(key_raw).astype(key_value.dtype)
    value = jnp.where(low, pltpu.roll(first, half_head, 1), second)
    key_value[:, head:] = value.astype(key_value.dtype)


def place_of(flags, index, flip_side, flip_core, slabs, rows, cores):
    block = jnp.zeros_like(index)
    for k in range(1, slabs):
        block = block + (index >= k * rows).astype(jnp.int32)
    at = (flags[5] ^ block) * 2 + (flags[1] ^ flip_side)
    return (at * cores + (flags[0] ^ flip_core)) * rows + index - block * rows


def tables_kernel(slabs, cores, flags, spread, cosine, sine_part):
    shape = cosine.shape
    index = lax.broadcasted_iota(jnp.int32, shape, 0)
    places = place_of(flags, index, 0, 0, slabs, shape[0] // slabs, cores)
    angles = places.astype(jnp.float32) * spread[...]
    cosine[...] = jnp.cos(angles)
    sines = jnp.sin(angles)
    low = lax.broadcasted_iota(jnp.int32, shape, 1) < shape[1] // 2
    sine_part[...] = jnp.where(low, -sines, sines)


def attend_kernel(slabs, cores, flags, lengths, queries, *refs):
    pieces, outs = refs[:4], refs[4:]
    count, head = pieces[0].shape[0], queries.shape[1]
    rows = count // slabs
    place = lambda shape, axis, a, b: place_of(
        flags, lax.broadcasted_iota(jnp.int32, shape, axis), a, b, slabs, rows, cores
    )
    end = 0
    ends = []
    for i in range(lengths.shape[0]):
        end = end + lengths[i]
        ends.append(end)
    step = min(count, 4 * rows)
    even = flags[1] == 0
    for at in range(0, count, step):
        index = at + lax.broadcasted_iota(jnp.int32, (step, 1), 0)
        query_places = place_of(flags, index, 0, 0, slabs, rows, cores)
        starts = jnp.zeros_like(query_places)
        for end in ends:
            starts = jnp.where(query_places >= end, end, starts)
        masks = []
        for c in range(4):
            key_places = place((1, count), 1, c % 2, c // 2)
            masks.append((key_places <= query_places) & (key_places >= starts))
        mixed = []
        for h in range(2):
            query = queries[h * count + at : h * count + at + step]
            scores = [
                jnp.where(mask, turned(query, piece[:, :head]), masked_low)
                for piece, mask in zip(pieces, masks)
            ]
            largest = scores[0]
            for part in scores[1:]:
                largest = jnp.maximum(largest, part)
            largest = jnp.max(largest, axis=1, keepdims=True)
            total, acc = 0.0, 0.0
            for part, piece, mask in zip(scores, pieces, masks):
                e = jnp.where(mask, jnp.exp(part - largest), 0.0)
                total = total + e
                acc = acc + plain(e.astype(jnp.bfloat16), piece[:, head:])
            total = jnp.sum(total, axis=1, keepdims=True)
            mixed.append((acc / total).astype(jnp.bfloat16))
        low = jnp.where(even, mixed[0], mixed[1])
        high = jnp.where(even, mixed[1], mixed[0])
        for k in range(step // rows):
            out = outs[at // rows + k]
            out[:, :head] = low[k * rows : (k + 1) * rows]
            out[:, head:] = high[k * rows : (k + 1) * rows]


def cut_kernel(flags, w_query, w_key, w_value, w_out, share_q, share_kv, out_sent, sems):
    sp, group = flags[0], flags[3]
    head = w_key.shape[0]
    quarter_depth, depth = share_q.shape[0], share_kv.shape[1]
    half_rows, quarter = out_sent.shape
    rows = pl.ds(pl.multiple_of((sp * 2 + group) * quarter_depth, 128), quarter_depth)
    deep = pl.ds(pl.multiple_of(sp * depth, 128), depth)
    columns = pl.ds(pl.multiple_of((flags[4] ^ 1) * quarter, 128), quarter)
    heads = pl.ds(pl.multiple_of(sp * half_rows, half_rows), half_rows)
    moves = (
        (w_query.at[rows], share_q),
        (w_key.at[:, deep], share_kv.at[:head]),
        (w_value.at[:, deep], share_kv.at[head:]),
        (w_out.at[heads, columns], out_sent),
    )
    copies = [pltpu.make_async_copy(a, b, sems.at[i]) for i, (a, b) in enumerate(moves)]
    for copy in copies:
        copy.start()
    for copy in copies:
        copy.wait()


def head_kernel(flags, came, other, w_out, out, sem):
    head, quarter = w_out.shape[0], out.shape[1]
    half_rows = came.shape[0]
    own = pl.ds(pl.multiple_of(flags[1] * head, head), head)
    columns = pl.ds(pl.multiple_of(flags[4] * quarter, 128), quarter)
    copy = pltpu.make_async_copy(w_out.at[:, columns], out.at[own], sem)
    copy.start()
    for i, piece in enumerate((came, other)):
        at = (1 - flags[1]) * head + (flags[0] ^ i) * half_rows
        out[pl.ds(pl.multiple_of(at, half_rows), half_rows)] = piece[...]
    copy.wait()


def project_kernel(peers, split, flags, *refs):
    stacked, pieces, outs = refs[:peers], list(refs[peers:-peers]), refs[-peers:]
    count, width = outs[0].shape
    rows = jnp.concatenate([m[...] for m in stacked], axis=0)
    step = 384 if width % 384 == 0 else width
    received = flags[2] != flags[0]
    for at in range(0, width, step):
        parts = [p[:, at : at + step] for p in pieces]
        if split:
            parts[-2:] = [jnp.where(received, parts[-2], parts[-1])]
        total = plain(rows, jnp.concatenate(parts, axis=0))
        for i, out in enumerate(outs):
            out[:, at : at + step] = total[i * count : (i + 1) * count].astype(out.dtype)


def assemble_kernel(flags, *refs):
    pieces, out, sems = refs[:-2], refs[-2], refs[-1]
    width = pieces[0].shape[1]
    copies = []
    for i, piece in enumerate(pieces):
        at = pl.multiple_of((flags[4] ^ i) * width, 128)
        copies.append(pltpu.make_async_copy(piece, out.at[:, pl.ds(at, width)], sems.at[i]))
        copies[-1].start()
    for copy in copies:
        copy.wait()


def local(tokens, w_query, w_key, w_value, w_out, doc_lengths):
    rows, width = tokens.shape
    tp_count = lax.axis_size("tp")
    sp_count = lax.axis_size("sp")
    sp_place = lax.axis_index("sp")
    tp_place = lax.axis_index("tp")
    group = lax.axis_index("groups") % 2
    slabs = tp_count // 2
    slab = tp_place // 2
    side = tp_place % 2
    head_dim = w_query.shape[1]
    short = slabs == 4
    is_inner = lambda t: (t >> 1) in (1, 2)

    if short:
        far = swap_tp(tokens, 4)
        near = swap_tp(tokens, 2)
        middle = swap_tp(tokens, 6, is_inner)
        relayed = swap_tp(far, 2, is_inner)
        firsts, last = [tokens, near, far], [middle, relayed]
    else:
        came = [swap_tp(tokens, 2 * k) for k in range(1, slabs)]
        firsts, last = [tokens] + came[:-1], [came[-1], came[-1]]

    depth = width // sp_count
    quarter = w_out.shape[1] // 4
    half_rows = head_dim // sp_count
    mine = group * 2 + side
    inner = ((slab == 1) | (slab == 2)).astype(jnp.int32)
    flags = jnp.stack([sp_place, side, inner, group, mine, slab]).astype(jnp.int32)
    turned_kv = [w_key.T, w_value.T]
    core_low = sp_place == 0
    flags, doc_lengths, core_low = fence(flags, doc_lengths, core_low)
    share_q, share_kv, out_sent = call(
        cut_kernel,
        [
            ((depth // 2, head_dim), jnp.bfloat16),
            ((head_dim, depth), jnp.bfloat16),
            ((half_rows, quarter), jnp.bfloat16),
        ],
        [flags],
        [],
        [pltpu.SemaphoreType.DMA((4,))],
        pltpu.VMEM if short else pl.ANY,
        [pltpu.with_memory_space_constraint(x, pltpu.HBM) for x in (w_query, *turned_kv, w_out)],
    )
    came_q = swap_tp(share_q, 1)
    cross_q = swap_in_slab(came_q, 1, 0)
    came_kv = swap_tp(share_kv, 1)
    out_came = swap_tp(out_sent, 1)
    out_other = swap_sp(out_came)
    weights = [w_query, *turned_kv, came_kv, swap_sp(came_kv), came_q, cross_q]
    weights += [swap_sp(came_q), swap_sp(cross_q)]
    early = call(
        early_kernel, [((len(firsts) * rows, 4 * head_dim), jnp.float32)], [flags], firsts + weights
    )[0]

    in_order = lambda a, b, flag: [jnp.where(flag, a, b), jnp.where(flag, b, a)]
    out_own = call(
        head_kernel,
        [((2 * head_dim, quarter), jnp.bfloat16)],
        [flags],
        [out_came, out_other],
        [pltpu.SemaphoreType.DMA(())],
        far=[w_out],
    )[0]
    if short:
        out_first = swap_by_core(out_own, (2, 4))
        out_swapped = swap_sp(out_first)

    count = slabs * rows
    half_head = head_dim // 2
    powers = np.arange(head_dim, dtype=np.float32) % half_head * np.float32(2.0 / head_dim)
    spread = jnp.asarray(np.power(np.float32(10000.0), -powers)[None, :])
    tables = call(
        lambda *refs: tables_kernel(slabs, sp_count, *refs),
        [((count, head_dim), jnp.float32)] * 2,
        [flags],
        [spread],
    )
    queries, key_value = call(
        tail_kernel,
        [((2 * count, head_dim), jnp.bfloat16), ((count, 2 * head_dim), jnp.bfloat16)],
        [flags],
        [early, *last, *tables] + weights,
        [pltpu.VMEM((rows, width), jnp.bfloat16)],
    )

    beside = swap_tp(key_value, 1)
    every = [key_value, beside, swap_sp(key_value), swap_sp(beside)]
    mixed = call(
        lambda *refs: attend_kernel(slabs, sp_count, *refs),
        [((rows, 2 * head_dim), jnp.bfloat16)] * slabs,
        [flags, doc_lengths],
        [queries] + every,
        limit=16 if short else 56,
    )

    parts = [mixed[0]]
    for k in range(1, slabs):
        parts.append(swap_tp(mixed[k], 2 * k))
    if short:
        parts[1:3] = in_order(parts[1], parts[2], core_low)
    merged = jnp.concatenate(parts, axis=1)
    peers = ((0, 0), (0, 1), (1, 0), (1, 1))
    stacked = [merged] + [swap_in_slab(merged, g, t) for g, t in peers[1:]]
    if short:
        out_sent = jnp.where(core_low, out_own, out_first)
        out_last = swap_by_core(out_sent, (6, 2), is_inner)
        out_last, stacked[3] = fence(out_last, stacked[3])
        pieces = [out_own, out_first, out_swapped, out_last, swap_sp(out_last)]
    else:
        pieces = [out_own]
        mine_of = lax.dynamic_slice_in_dim(out_own, sp_place * head_dim, head_dim, 0)
        for k in range(1, slabs):
            piece = swap_tp(mine_of, 2 * k)
            both = in_order(piece, swap_sp(piece), core_low)
            pieces.append(jnp.concatenate(both, axis=0))
    outs = call(
        lambda *refs: project_kernel(len(peers), short, *refs),
        [((rows, quarter), jnp.bfloat16)] * len(peers),
        [flags],
        stacked + pieces,
    )
    outs = [outs[0]] + [swap_in_slab(o, g, t) for o, (g, t) in zip(outs[1:], peers[1:])]
    sems = [pltpu.SemaphoreType.DMA((len(outs),))]
    shape = ((rows, width), jnp.bfloat16)
    return call(assemble_kernel, [shape], [flags], outs, sems, pl.ANY)[0]


def solution(mesh):
    placed = (
        P(("groups", "tp", "sp"), None),
        P(None, "tp"),
        P(None, "tp"),
        P(None, "tp"),
        P("tp", None),
        P("groups"),
    )

    return jax.shard_map(
        local,
        mesh=mesh,
        in_specs=placed,
        out_specs=P(("groups", "tp", "sp"), None),
        check_vma=False,
    )
```

```python
import jax
import jax.numpy as jnp
import numpy as np
from jax import lax
from jax.experimental import pallas as pl
from jax.experimental.pallas import tpu as pltpu
from jax.sharding import PartitionSpec as P

PRE_SCALE = 144

masked_low = -1e30


def swap_tp(block, flip, only=None):
    count = lax.axis_size("tp")
    route = [(t, t ^ flip) for t in range(count) if only is None or only(t)]
    return lax.ppermute(block, "tp", route)


def swap_sp(block):
    count = lax.axis_size("sp")
    return lax.ppermute(block, "sp", [(s, s ^ 1) for s in range(count)])


def swap_by_core(block, flips, only=lambda t: True):
    count, cores = lax.axis_size("tp"), lax.axis_size("sp")
    route = [
        (t * cores + s, (t ^ flips[s]) * cores + s)
        for t in range(count)
        for s in range(cores)
        if only(t)
    ]
    return lax.ppermute(block, ("tp", "sp"), route)


def swap_in_slab(block, group_flip, tp_flip):
    groups = lax.axis_size("groups")
    count = lax.axis_size("tp")
    route = [
        (g * count + t, (g ^ group_flip) * count + (t ^ tp_flip))
        for g in range(groups)
        for t in range(count)
    ]
    return lax.ppermute(block, ("groups", "tp"), route)


def fence(*values):
    return lax.optimization_barrier(values)


def call(kernel, shapes, scalars, operands, scratch=(), outs=pltpu.VMEM, far=(), limit=16):
    size = sum(x.size * x.dtype.itemsize for x in operands)
    params = None
    if size < 8 << 20:
        operands = [pltpu.with_memory_space_constraint(x, pltpu.VMEM) for x in operands]
        params = pltpu.CompilerParams(vmem_limit_bytes=limit << 20)
    specs = [pl.BlockSpec(memory_space=pltpu.SMEM)] * len(scalars)
    specs += [pl.BlockSpec(memory_space=pltpu.VMEM)] * len(operands)
    specs += [pl.BlockSpec(memory_space=pl.ANY)] * len(far)
    return pl.pallas_call(
        kernel,
        in_specs=specs,
        out_specs=[pl.BlockSpec(memory_space=outs)] * len(shapes),
        out_shape=[jax.ShapeDtypeStruct(*shape) for shape in shapes],
        scratch_shapes=list(scratch),
        compiler_params=params,
    )(*scalars, *operands, *far)


def plain(a, w):
    return jnp.dot(a, w, preferred_element_type=jnp.float32)


def turned(a, w):
    return lax.dot_general(a, w, (((1,), (1,)), ((), ())), preferred_element_type=jnp.float32)


def rows_at(blocks, offset, size):
    parts = [block[:, pl.ds(pl.multiple_of(offset, 128), size)] for block in blocks]
    return jnp.concatenate(parts, axis=0) if len(parts) > 1 else parts[0]


def products(blocks, weights, sp, group):
    w_query, w_key, w_value, kv_came, kv_other, *quarters = weights
    rows = jnp.concatenate([block[...] for block in blocks], axis=0)
    own_query = plain(rows, w_query[...])
    own_kv = turned(rows, jnp.concatenate([w_key[...], w_value[...]], axis=0))
    size = quarters[0].shape[0]
    pair_query = None
    for i, weight in enumerate(quarters):
        at = (sp ^ (i >> 1)) * 2 + (group ^ (i & 1))
        term = plain(rows_at(blocks, at * size, size), weight[...])
        pair_query = term if pair_query is None else pair_query + term
    depth = kv_came.shape[1]
    pair_kv = turned(rows_at(blocks, sp * depth, depth), kv_came[...]) + turned(
        rows_at(blocks, (1 - sp) * depth, depth), kv_other[...]
    )
    return own_query, own_kv, pair_query, pair_kv


def early_kernel(short, flags, *refs):
    blocks, weights, (out, far) = list(refs[:-11]), refs[-11:-2], refs[-2:]
    if short:
        far[...] = jnp.where(flags[2] != 0, blocks[2][...], blocks[3][...])
        blocks[2:4] = [far]
    head = weights[0].shape[1]
    for i, part in enumerate(products(blocks, weights, flags[0], flags[3])):
        out[:, i * head : (i + 1) * head] = part


def tail_kernel(flags, early, middle, relayed, cosine, sine_part, *refs):
    weights, (queries, key_value, last) = refs[:9], refs[9:]
    side, inner = flags[1], flags[2]
    head = weights[0].shape[1]
    half_head = head // 2
    last[...] = jnp.where(inner != 0, middle[...], relayed[...])
    late = products([last], weights, flags[0], flags[3])
    join = lambda i: jnp.concatenate([early[:, i * head : (i + 1) * head], late[i]], axis=0)
    own_query, own_kv, pair_query, pair_kv = [join(i) for i in range(4)]
    spin = lambda v: v * cosine[...] + pltpu.roll(v, half_head, 1) * sine_part[...]
    scale = PRE_SCALE ** (-0.5)
    count = own_query.shape[0]
    queries[:count] = (spin(own_query) * scale).astype(queries.dtype)
    queries[count:] = (spin(pair_query) * scale).astype(queries.dtype)
    lane = lax.broadcasted_iota(jnp.int32, own_kv.shape, 1)
    low = lane < half_head
    even = side == 0
    first = jnp.where(even, own_kv, pair_kv)
    second = jnp.where(even, pair_kv, own_kv)
    key_raw = jnp.where(low, first, pltpu.roll(second, half_head, 1))
    key_raw = key_raw.astype(jnp.bfloat16).astype(jnp.float32)
    key_value[:, :head] = spin(key_raw).astype(key_value.dtype)
    value = jnp.where(low, pltpu.roll(first, half_head, 1), second)
    key_value[:, head:] = value.astype(key_value.dtype)


def place_of(flags, index, flip_side, flip_core, slabs, rows, cores):
    block = jnp.zeros_like(index)
    for k in range(1, slabs):
        block = block + (index >= k * rows).astype(jnp.int32)
    at = (flags[5] ^ block) * 2 + (flags[1] ^ flip_side)
    return (at * cores + (flags[0] ^ flip_core)) * rows + index - block * rows


def tables_kernel(slabs, cores, flags, spread, cosine, sine_part):
    shape = cosine.shape
    index = lax.broadcasted_iota(jnp.int32, shape, 0)
    places = place_of(flags, index, 0, 0, slabs, shape[0] // slabs, cores)
    angles = places.astype(jnp.float32) * spread[...]
    cosine[...] = jnp.cos(angles)
    sines = jnp.sin(angles)
    low = lax.broadcasted_iota(jnp.int32, shape, 1) < shape[1] // 2
    sine_part[...] = jnp.where(low, -sines, sines)


def attend_kernel(slabs, cores, flags, lengths, queries, *refs):
    pieces, outs = refs[:4], refs[4:]
    count, head = pieces[0].shape[0], queries.shape[1]
    rows = count // slabs
    place = lambda shape, axis, a, b: place_of(
        flags, lax.broadcasted_iota(jnp.int32, shape, axis), a, b, slabs, rows, cores
    )
    end = 0
    ends = []
    for i in range(lengths.shape[0]):
        end = end + lengths[i]
        ends.append(end)
    step = min(count, 4 * rows)
    even = flags[1] == 0
    for at in range(0, count, step):
        index = at + lax.broadcasted_iota(jnp.int32, (step, 1), 0)
        query_places = place_of(flags, index, 0, 0, slabs, rows, cores)
        starts = jnp.zeros_like(query_places)
        for end in ends:
            starts = jnp.where(query_places >= end, end, starts)
        masks = []
        for c in range(4):
            key_places = place((1, count), 1, c % 2, c // 2)
            masks.append((key_places <= query_places) & (key_places >= starts))
        mixed = []
        for h in range(2):
            query = queries[h * count + at : h * count + at + step]
            scores = [
                jnp.where(mask, turned(query, piece[:, :head]), masked_low)
                for piece, mask in zip(pieces, masks)
            ]
            largest = scores[0]
            for part in scores[1:]:
                largest = jnp.maximum(largest, part)
            largest = jnp.max(largest, axis=1, keepdims=True)
            total, acc = 0.0, 0.0
            for part, piece, mask in zip(scores, pieces, masks):
                e = jnp.where(mask, jnp.exp(part - largest), 0.0)
                total = total + e
                acc = acc + plain(e.astype(jnp.bfloat16), piece[:, head:])
            total = jnp.sum(total, axis=1, keepdims=True)
            mixed.append((acc / total).astype(jnp.bfloat16))
        low = jnp.where(even, mixed[0], mixed[1])
        high = jnp.where(even, mixed[1], mixed[0])
        for k in range(step // rows):
            out = outs[at // rows + k]
            out[:, :head] = low[k * rows : (k + 1) * rows]
            out[:, head:] = high[k * rows : (k + 1) * rows]


def cut_kernel(flags, w_query, w_key, w_value, w_out, share_q, share_kv, out_sent, sems):
    sp, group = flags[0], flags[3]
    head = w_key.shape[0]
    quarter_depth, depth = share_q.shape[0], share_kv.shape[1]
    half_rows, quarter = out_sent.shape
    rows = pl.ds(pl.multiple_of((sp * 2 + group) * quarter_depth, 128), quarter_depth)
    deep = pl.ds(pl.multiple_of(sp * depth, 128), depth)
    columns = pl.ds(pl.multiple_of((flags[4] ^ 1) * quarter, 128), quarter)
    heads = pl.ds(pl.multiple_of(sp * half_rows, half_rows), half_rows)
    moves = (
        (w_query.at[rows], share_q),
        (w_key.at[:, deep], share_kv.at[:head]),
        (w_value.at[:, deep], share_kv.at[head:]),
        (w_out.at[heads, columns], out_sent),
    )
    copies = [pltpu.make_async_copy(a, b, sems.at[i]) for i, (a, b) in enumerate(moves)]
    for copy in copies:
        copy.start()
    for copy in copies:
        copy.wait()


def head_kernel(flags, came, other, w_out, out, sem):
    head, quarter = w_out.shape[0], out.shape[1]
    half_rows = came.shape[0]
    own = pl.ds(pl.multiple_of(flags[1] * head, head), head)
    columns = pl.ds(pl.multiple_of(flags[4] * quarter, 128), quarter)
    copy = pltpu.make_async_copy(w_out.at[:, columns], out.at[own], sem)
    copy.start()
    for i, piece in enumerate((came, other)):
        at = (1 - flags[1]) * head + (flags[0] ^ i) * half_rows
        out[pl.ds(pl.multiple_of(at, half_rows), half_rows)] = piece[...]
    copy.wait()


def project_kernel(peers, split, flags, *refs):
    stacked, pieces, outs = refs[:peers], list(refs[peers:-peers]), refs[-peers:]
    count, width = outs[0].shape
    rows = jnp.concatenate([m[...] for m in stacked], axis=0)
    step = 384 if width % 384 == 0 else width
    received = flags[2] != flags[0]
    for at in range(0, width, step):
        parts = [p[:, at : at + step] for p in pieces]
        if split:
            parts[-2:] = [jnp.where(received, parts[-2], parts[-1])]
        total = plain(rows, jnp.concatenate(parts, axis=0))
        for i, out in enumerate(outs):
            out[:, at : at + step] = total[i * count : (i + 1) * count].astype(out.dtype)


def assemble_kernel(flags, *refs):
    pieces, out, sems = refs[:-2], refs[-2], refs[-1]
    width = pieces[0].shape[1]
    copies = []
    for i, piece in enumerate(pieces):
        at = pl.multiple_of((flags[4] ^ i) * width, 128)
        copies.append(pltpu.make_async_copy(piece, out.at[:, pl.ds(at, width)], sems.at[i]))
        copies[-1].start()
    for copy in copies:
        copy.wait()


def local(tokens, w_query, w_key, w_value, w_out, doc_lengths):
    rows, width = tokens.shape
    tp_count = lax.axis_size("tp")
    sp_count = lax.axis_size("sp")
    sp_place = lax.axis_index("sp")
    tp_place = lax.axis_index("tp")
    group = lax.axis_index("groups") % 2
    slabs = tp_count // 2
    slab = tp_place // 2
    side = tp_place % 2
    head_dim = w_query.shape[1]
    short = slabs == 4
    is_inner = lambda t: (t >> 1) in (1, 2)

    if short:
        far_out = swap_tp(tokens, 4, lambda t: not is_inner(t))
        far_in = swap_tp(tokens, 4, is_inner)
        near = swap_tp(tokens, 2)
        middle = swap_tp(tokens, 6, is_inner)
        relayed = swap_tp(far_out, 2, is_inner)
        firsts, last = [tokens, near, far_out, far_in], [middle, relayed]
    else:
        came = [swap_tp(tokens, 2 * k) for k in range(1, slabs)]
        firsts, last = [tokens] + came[:-1], [came[-1], came[-1]]

    depth = width // sp_count
    quarter = w_out.shape[1] // 4
    half_rows = head_dim // sp_count
    mine = group * 2 + side
    inner = ((slab == 1) | (slab == 2)).astype(jnp.int32)
    flags = jnp.stack([sp_place, side, inner, group, mine, slab]).astype(jnp.int32)
    turned_kv = [w_key.T, w_value.T]
    core_low = sp_place == 0
    flags, doc_lengths, core_low = fence(flags, doc_lengths, core_low)
    share_q, share_kv, out_sent = call(
        cut_kernel,
        [
            ((depth // 2, head_dim), jnp.bfloat16),
            ((head_dim, depth), jnp.bfloat16),
            ((half_rows, quarter), jnp.bfloat16),
        ],
        [flags],
        [],
        [pltpu.SemaphoreType.DMA((4,))],
        pltpu.VMEM if short else pl.ANY,
        [pltpu.with_memory_space_constraint(x, pltpu.HBM) for x in (w_query, *turned_kv, w_out)],
    )
    came_q = swap_tp(share_q, 1)
    cross_q = swap_in_slab(came_q, 1, 0)
    came_kv = swap_tp(share_kv, 1)
    out_came = swap_tp(out_sent, 1)
    out_other = swap_sp(out_came)
    weights = [w_query, *turned_kv, came_kv, swap_sp(came_kv), came_q, cross_q]
    weights += [swap_sp(came_q), swap_sp(cross_q)]
    early = call(
        lambda *refs: early_kernel(short, *refs),
        [(((slabs - 1) * rows, 4 * head_dim), jnp.float32)],
        [flags],
        firsts + weights,
        [pltpu.VMEM((rows, width), jnp.bfloat16)],
    )[0]

    in_order = lambda a, b, flag: [jnp.where(flag, a, b), jnp.where(flag, b, a)]
    out_own = call(
        head_kernel,
        [((2 * head_dim, quarter), jnp.bfloat16)],
        [flags],
        [out_came, out_other],
        [pltpu.SemaphoreType.DMA(())],
        far=[w_out],
    )[0]
    if short:
        out_first = swap_by_core(out_own, (2, 4))
        out_swapped = swap_sp(out_first)

    count = slabs * rows
    half_head = head_dim // 2
    powers = np.arange(head_dim, dtype=np.float32) % half_head * np.float32(2.0 / head_dim)
    spread = jnp.asarray(np.power(np.float32(10000.0), -powers)[None, :])
    tables = call(
        lambda *refs: tables_kernel(slabs, sp_count, *refs),
        [((count, head_dim), jnp.float32)] * 2,
        [flags],
        [spread],
    )
    queries, key_value = call(
        tail_kernel,
        [((2 * count, head_dim), jnp.bfloat16), ((count, 2 * head_dim), jnp.bfloat16)],
        [flags],
        [early, *last, *tables] + weights,
        [pltpu.VMEM((rows, width), jnp.bfloat16)],
    )

    beside = swap_tp(key_value, 1)
    every = [key_value, beside, swap_sp(key_value), swap_sp(beside)]
    mixed = call(
        lambda *refs: attend_kernel(slabs, sp_count, *refs),
        [((rows, 2 * head_dim), jnp.bfloat16)] * slabs,
        [flags, doc_lengths],
        [queries] + every,
        limit=16 if short else 56,
    )

    parts = [mixed[0]]
    for k in range(1, slabs):
        parts.append(swap_tp(mixed[k], 2 * k))
    if short:
        parts[1:3] = in_order(parts[1], parts[2], core_low)
    merged = jnp.concatenate(parts, axis=1)
    peers = ((0, 0), (0, 1), (1, 0), (1, 1))
    stacked = [merged] + [swap_in_slab(merged, g, t) for g, t in peers[1:]]
    if short:
        out_sent = jnp.where(core_low, out_own, out_first)
        out_last = swap_by_core(out_sent, (6, 2), is_inner)
        out_last, stacked[3] = fence(out_last, stacked[3])
        pieces = [out_own, out_first, out_swapped, out_last, swap_sp(out_last)]
    else:
        pieces = [out_own]
        mine_of = lax.dynamic_slice_in_dim(out_own, sp_place * head_dim, head_dim, 0)
        for k in range(1, slabs):
            piece = swap_tp(mine_of, 2 * k)
            both = in_order(piece, swap_sp(piece), core_low)
            pieces.append(jnp.concatenate(both, axis=0))
    outs = call(
        lambda *refs: project_kernel(len(peers), short, *refs),
        [((rows, quarter), jnp.bfloat16)] * len(peers),
        [flags],
        stacked + pieces,
    )
    outs = [outs[0]] + [swap_in_slab(o, g, t) for o, (g, t) in zip(outs[1:], peers[1:])]
    sems = [pltpu.SemaphoreType.DMA((len(outs),))]
    shape = ((rows, width), jnp.bfloat16)
    return call(assemble_kernel, [shape], [flags], outs, sems, pl.ANY)[0]


def solution(mesh):
    placed = (
        P(("groups", "tp", "sp"), None),
        P(None, "tp"),
        P(None, "tp"),
        P(None, "tp"),
        P("tp", None),
        P("groups"),
    )

    return jax.shard_map(
        local,
        mesh=mesh,
        in_specs=placed,
        out_specs=P(("groups", "tp", "sp"), None),
        check_vma=False,
    )
```

```python
import jax
import jax.numpy as jnp
import numpy as np
from jax import lax
from jax.experimental import pallas as pl
from jax.experimental.pallas import tpu as pltpu
from jax.sharding import PartitionSpec as P

PRE_SCALE = 144

masked_low = -1e30


def swap_tp(block, flip, only=None):
    count = lax.axis_size("tp")
    route = [(t, t ^ flip) for t in range(count) if only is None or only(t)]
    return lax.ppermute(block, "tp", route)


def swap_sp(block):
    count = lax.axis_size("sp")
    return lax.ppermute(block, "sp", [(s, s ^ 1) for s in range(count)])


def swap_by_core(block, flips, only=lambda t: True):
    count, cores = lax.axis_size("tp"), lax.axis_size("sp")
    route = [
        (t * cores + s, (t ^ flips[s]) * cores + s)
        for t in range(count)
        for s in range(cores)
        if only(t)
    ]
    return lax.ppermute(block, ("tp", "sp"), route)


def swap_in_slab(block, group_flip, tp_flip):
    groups = lax.axis_size("groups")
    count = lax.axis_size("tp")
    route = [
        (g * count + t, (g ^ group_flip) * count + (t ^ tp_flip))
        for g in range(groups)
        for t in range(count)
    ]
    return lax.ppermute(block, ("groups", "tp"), route)


def fence(*values):
    return lax.optimization_barrier(values)


def call(kernel, shapes, scalars, operands, scratch=(), outs=pltpu.VMEM, far=(), limit=16):
    size = sum(x.size * x.dtype.itemsize for x in operands)
    params = None
    if size < 8 << 20:
        operands = [pltpu.with_memory_space_constraint(x, pltpu.VMEM) for x in operands]
        params = pltpu.CompilerParams(vmem_limit_bytes=limit << 20)
    specs = [pl.BlockSpec(memory_space=pltpu.SMEM)] * len(scalars)
    specs += [pl.BlockSpec(memory_space=pltpu.VMEM)] * len(operands)
    specs += [pl.BlockSpec(memory_space=pl.ANY)] * len(far)
    return pl.pallas_call(
        kernel,
        in_specs=specs,
        out_specs=[pl.BlockSpec(memory_space=outs)] * len(shapes),
        out_shape=[jax.ShapeDtypeStruct(*shape) for shape in shapes],
        scratch_shapes=list(scratch),
        compiler_params=params,
    )(*scalars, *operands, *far)


def plain(a, w):
    return jnp.dot(a, w, preferred_element_type=jnp.float32)


def turned(a, w):
    return lax.dot_general(a, w, (((1,), (1,)), ((), ())), preferred_element_type=jnp.float32)


def rows_at(blocks, offset, size):
    parts = [block[:, pl.ds(pl.multiple_of(offset, 128), size)] for block in blocks]
    return jnp.concatenate(parts, axis=0) if len(parts) > 1 else parts[0]


def products(blocks, weights, sp, group):
    w_query, w_key, w_value, kv_came, kv_other, *quarters = weights
    rows = jnp.concatenate([block[...] for block in blocks], axis=0)
    own_query = plain(rows, w_query[...])
    own_kv = turned(rows, jnp.concatenate([w_key[...], w_value[...]], axis=0))
    size = quarters[0].shape[0]
    pair_query = None
    for i, weight in enumerate(quarters):
        at = (sp ^ (i >> 1)) * 2 + (group ^ (i & 1))
        term = plain(rows_at(blocks, at * size, size), weight[...])
        pair_query = term if pair_query is None else pair_query + term
    depth = kv_came.shape[1]
    pair_kv = turned(rows_at(blocks, sp * depth, depth), kv_came[...]) + turned(
        rows_at(blocks, (1 - sp) * depth, depth), kv_other[...]
    )
    return own_query, own_kv, pair_query, pair_kv


def early_kernel(short, flags, *refs):
    blocks, weights, (out, far) = list(refs[:-11]), refs[-11:-2], refs[-2:]
    if short:
        far[...] = jnp.where(flags[2] != 0, blocks[2][...], blocks[3][...])
        blocks[2:4] = [far]
    head = weights[0].shape[1]
    for i, part in enumerate(products(blocks, weights, flags[0], flags[3])):
        out[:, i * head : (i + 1) * head] = part


def tail_kernel(flags, early, middle, relayed, cosine, sine_part, *refs):
    weights, (queries, key_value, last) = refs[:9], refs[9:]
    side, inner = flags[1], flags[2]
    head = weights[0].shape[1]
    half_head = head // 2
    last[...] = jnp.where(inner != 0, middle[...], relayed[...])
    late = products([last], weights, flags[0], flags[3])
    join = lambda i: jnp.concatenate([early[:, i * head : (i + 1) * head], late[i]], axis=0)
    own_query, own_kv, pair_query, pair_kv = [join(i) for i in range(4)]
    spin = lambda v: v * cosine[...] + pltpu.roll(v, half_head, 1) * sine_part[...]
    scale = PRE_SCALE ** (-0.5)
    count = own_query.shape[0]
    queries[:count] = (spin(own_query) * scale).astype(queries.dtype)
    queries[count:] = (spin(pair_query) * scale).astype(queries.dtype)
    lane = lax.broadcasted_iota(jnp.int32, own_kv.shape, 1)
    low = lane < half_head
    even = side == 0
    first = jnp.where(even, own_kv, pair_kv)
    second = jnp.where(even, pair_kv, own_kv)
    key_raw = jnp.where(low, first, pltpu.roll(second, half_head, 1))
    key_raw = key_raw.astype(jnp.bfloat16).astype(jnp.float32)
    key_value[:, :head] = spin(key_raw).astype(key_value.dtype)
    value = jnp.where(low, pltpu.roll(first, half_head, 1), second)
    key_value[:, head:] = value.astype(key_value.dtype)


def place_of(flags, index, flip_side, flip_core, slabs, rows, cores):
    block = jnp.zeros_like(index)
    for k in range(1, slabs):
        block = block + (index >= k * rows).astype(jnp.int32)
    at = (flags[5] ^ block) * 2 + (flags[1] ^ flip_side)
    return (at * cores + (flags[0] ^ flip_core)) * rows + index - block * rows


def tables_kernel(slabs, cores, flags, spread, cosine, sine_part):
    shape = cosine.shape
    index = lax.broadcasted_iota(jnp.int32, shape, 0)
    places = place_of(flags, index, 0, 0, slabs, shape[0] // slabs, cores)
    angles = places.astype(jnp.float32) * spread[...]
    cosine[...] = jnp.cos(angles)
    sines = jnp.sin(angles)
    low = lax.broadcasted_iota(jnp.int32, shape, 1) < shape[1] // 2
    sine_part[...] = jnp.where(low, -sines, sines)


def attend_kernel(slabs, cores, flags, lengths, queries, *refs):
    pieces, outs = refs[:4], refs[4:]
    count, head = pieces[0].shape[0], queries.shape[1]
    rows = count // slabs
    place = lambda shape, axis, a, b: place_of(
        flags, lax.broadcasted_iota(jnp.int32, shape, axis), a, b, slabs, rows, cores
    )
    end = 0
    ends = []
    for i in range(lengths.shape[0]):
        end = end + lengths[i]
        ends.append(end)
    step = min(count, 4 * rows)
    even = flags[1] == 0
    for at in range(0, count, step):
        index = at + lax.broadcasted_iota(jnp.int32, (step, 1), 0)
        query_places = place_of(flags, index, 0, 0, slabs, rows, cores)
        starts = jnp.zeros_like(query_places)
        for end in ends:
            starts = jnp.where(query_places >= end, end, starts)
        masks = []
        for c in range(4):
            key_places = place((1, count), 1, c % 2, c // 2)
            masks.append((key_places <= query_places) & (key_places >= starts))
        mixed = []
        for h in range(2):
            query = queries[h * count + at : h * count + at + step]
            scores = [
                jnp.where(mask, turned(query, piece[:, :head]), masked_low)
                for piece, mask in zip(pieces, masks)
            ]
            largest = scores[0]
            for part in scores[1:]:
                largest = jnp.maximum(largest, part)
            largest = jnp.max(largest, axis=1, keepdims=True)
            total, acc = 0.0, 0.0
            for part, piece, mask in zip(scores, pieces, masks):
                e = jnp.where(mask, jnp.exp(part - largest), 0.0)
                total = total + e
                acc = acc + plain(e.astype(jnp.bfloat16), piece[:, head:])
            total = jnp.sum(total, axis=1, keepdims=True)
            mixed.append((acc / total).astype(jnp.bfloat16))
        low = jnp.where(even, mixed[0], mixed[1])
        high = jnp.where(even, mixed[1], mixed[0])
        for k in range(step // rows):
            out = outs[at // rows + k]
            out[:, :head] = low[k * rows : (k + 1) * rows]
            out[:, head:] = high[k * rows : (k + 1) * rows]


def cut_kernel(flags, w_query, w_key, w_value, w_out, share_q, share_kv, out_sent, sems):
    sp, group = flags[0], flags[3]
    head = w_key.shape[0]
    quarter_depth, depth = share_q.shape[0], share_kv.shape[1]
    half_rows, quarter = out_sent.shape
    rows = pl.ds(pl.multiple_of((sp * 2 + group) * quarter_depth, 128), quarter_depth)
    deep = pl.ds(pl.multiple_of(sp * depth, 128), depth)
    columns = pl.ds(pl.multiple_of((flags[4] ^ 1) * quarter, 128), quarter)
    heads = pl.ds(pl.multiple_of(sp * half_rows, half_rows), half_rows)
    moves = (
        (w_query.at[rows], share_q),
        (w_key.at[:, deep], share_kv.at[:head]),
        (w_value.at[:, deep], share_kv.at[head:]),
        (w_out.at[heads, columns], out_sent),
    )
    copies = [pltpu.make_async_copy(a, b, sems.at[i]) for i, (a, b) in enumerate(moves)]
    for copy in copies:
        copy.start()
    for copy in copies:
        copy.wait()


def head_kernel(flags, came, other, w_out, out, sem):
    head, quarter = w_out.shape[0], out.shape[1]
    half_rows = came.shape[0]
    own = pl.ds(pl.multiple_of(flags[1] * head, head), head)
    columns = pl.ds(pl.multiple_of(flags[4] * quarter, 128), quarter)
    copy = pltpu.make_async_copy(w_out.at[:, columns], out.at[own], sem)
    copy.start()
    for i, piece in enumerate((came, other)):
        at = (1 - flags[1]) * head + (flags[0] ^ i) * half_rows
        out[pl.ds(pl.multiple_of(at, half_rows), half_rows)] = piece[...]
    copy.wait()


def tiles_of(width):
    step = 384 if width % 384 == 0 else width
    return [(at, at + step) for at in range(0, width, step)]


def begin_kernel(peers, flags, *refs):
    stacked, pieces, out = refs[:peers], refs[peers:-1], refs[-1]
    inner = sum(piece.shape[0] for piece in pieces)
    rows = jnp.concatenate([m[:, :inner] for m in stacked], axis=0)
    for a, b in tiles_of(out.shape[1]):
        out[:, a:b] = plain(rows, jnp.concatenate([p[:, a:b] for p in pieces], axis=0))


def finish_kernel(peers, flags, *refs):
    stacked, (begun, came, other), outs = refs[:peers], refs[peers:-peers], refs[-peers:]
    count, width = outs[0].shape
    inner = stacked[0].shape[1] - came.shape[0]
    rows = jnp.concatenate([m[:, inner:] for m in stacked], axis=0)
    received = flags[2] != flags[0]
    for a, b in tiles_of(width):
        weight = jnp.where(received, came[:, a:b], other[:, a:b])
        total = begun[:, a:b] + plain(rows, weight)
        for i, out in enumerate(outs):
            out[:, a:b] = total[i * count : (i + 1) * count].astype(out.dtype)


def assemble_kernel(flags, *refs):
    pieces, out, sems = refs[:-2], refs[-2], refs[-1]
    width = pieces[0].shape[1]
    copies = []
    for i, piece in enumerate(pieces):
        at = pl.multiple_of((flags[4] ^ i) * width, 128)
        copies.append(pltpu.make_async_copy(piece, out.at[:, pl.ds(at, width)], sems.at[i]))
        copies[-1].start()
    for copy in copies:
        copy.wait()


def local(tokens, w_query, w_key, w_value, w_out, doc_lengths):
    rows, width = tokens.shape
    tp_count = lax.axis_size("tp")
    sp_count = lax.axis_size("sp")
    sp_place = lax.axis_index("sp")
    tp_place = lax.axis_index("tp")
    group = lax.axis_index("groups") % 2
    slabs = tp_count // 2
    slab = tp_place // 2
    side = tp_place % 2
    head_dim = w_query.shape[1]
    short = slabs == 4
    is_inner = lambda t: (t >> 1) in (1, 2)

    if short:
        far_out = swap_tp(tokens, 4, lambda t: not is_inner(t))
        far_in = swap_tp(tokens, 4, is_inner)
        near = swap_tp(tokens, 2)
        middle = swap_tp(tokens, 6, is_inner)
        relayed = swap_tp(far_out, 2, is_inner)
        firsts, last = [tokens, near, far_out, far_in], [middle, relayed]
    else:
        came = [swap_tp(tokens, 2 * k) for k in range(1, slabs)]
        firsts, last = [tokens] + came[:-1], [came[-1], came[-1]]

    depth = width // sp_count
    quarter = w_out.shape[1] // 4
    half_rows = head_dim // sp_count
    mine = group * 2 + side
    inner = ((slab == 1) | (slab == 2)).astype(jnp.int32)
    flags = jnp.stack([sp_place, side, inner, group, mine, slab]).astype(jnp.int32)
    turned_kv = [w_key.T, w_value.T]
    core_low = sp_place == 0
    flags, doc_lengths, core_low = fence(flags, doc_lengths, core_low)
    share_q, share_kv, out_sent = call(
        cut_kernel,
        [
            ((depth // 2, head_dim), jnp.bfloat16),
            ((head_dim, depth), jnp.bfloat16),
            ((half_rows, quarter), jnp.bfloat16),
        ],
        [flags],
        [],
        [pltpu.SemaphoreType.DMA((4,))],
        pltpu.VMEM if short else pl.ANY,
        [pltpu.with_memory_space_constraint(x, pltpu.HBM) for x in (w_query, *turned_kv, w_out)],
    )
    came_q = swap_tp(share_q, 1)
    cross_q = swap_in_slab(came_q, 1, 0)
    came_kv = swap_tp(share_kv, 1)
    out_came = swap_tp(out_sent, 1)
    out_other = swap_sp(out_came)
    weights = [w_query, *turned_kv, came_kv, swap_sp(came_kv), came_q, cross_q]
    weights += [swap_sp(came_q), swap_sp(cross_q)]
    early = call(
        lambda *refs: early_kernel(short, *refs),
        [(((slabs - 1) * rows, 4 * head_dim), jnp.float32)],
        [flags],
        firsts + weights,
        [pltpu.VMEM((rows, width), jnp.bfloat16)],
    )[0]

    in_order = lambda a, b, flag: [jnp.where(flag, a, b), jnp.where(flag, b, a)]
    out_own = call(
        head_kernel,
        [((2 * head_dim, quarter), jnp.bfloat16)],
        [flags],
        [out_came, out_other],
        [pltpu.SemaphoreType.DMA(())],
        far=[w_out],
    )[0]
    if short:
        out_first = swap_by_core(out_own, (2, 4))
        out_swapped = swap_sp(out_first)

    count = slabs * rows
    half_head = head_dim // 2
    powers = np.arange(head_dim, dtype=np.float32) % half_head * np.float32(2.0 / head_dim)
    spread = jnp.asarray(np.power(np.float32(10000.0), -powers)[None, :])
    tables = call(
        lambda *refs: tables_kernel(slabs, sp_count, *refs),
        [((count, head_dim), jnp.float32)] * 2,
        [flags],
        [spread],
    )
    queries, key_value = call(
        tail_kernel,
        [((2 * count, head_dim), jnp.bfloat16), ((count, 2 * head_dim), jnp.bfloat16)],
        [flags],
        [early, *last, *tables] + weights,
        [pltpu.VMEM((rows, width), jnp.bfloat16)],
    )

    beside = swap_tp(key_value, 1)
    every = [key_value, beside, swap_sp(key_value), swap_sp(beside)]
    mixed = call(
        lambda *refs: attend_kernel(slabs, sp_count, *refs),
        [((rows, 2 * head_dim), jnp.bfloat16)] * slabs,
        [flags, doc_lengths],
        [queries] + every,
        limit=16 if short else 56,
    )

    parts = [mixed[0]]
    for k in range(1, slabs):
        parts.append(swap_tp(mixed[k], 2 * k))
    if short:
        parts[1:3] = in_order(parts[1], parts[2], core_low)
    merged = jnp.concatenate(parts, axis=1)
    peers = ((0, 0), (0, 1), (1, 0), (1, 1))
    stacked = [merged] + [swap_in_slab(merged, g, t) for g, t in peers[1:]]
    if short:
        out_sent = jnp.where(core_low, out_own, out_first)
        out_last = swap_by_core(out_sent, (6, 2), is_inner)
        out_last, stacked[3] = fence(out_last, stacked[3])
        pieces = [out_own, out_first, out_swapped, out_last, swap_sp(out_last)]
    else:
        pieces = [out_own]
        mine_of = lax.dynamic_slice_in_dim(out_own, sp_place * head_dim, head_dim, 0)
        for k in range(1, slabs):
            piece = swap_tp(mine_of, 2 * k)
            both = in_order(piece, swap_sp(piece), core_low)
            pieces.append(jnp.concatenate(both, axis=0))
    if not short:
        pieces.append(pieces[-1])
    count, kept = len(peers), pieces[:-2]
    begun = call(
        lambda *refs: begin_kernel(count, *refs),
        [((count * rows, quarter), jnp.float32)],
        [flags],
        stacked + kept,
    )
    outs = call(
        lambda *refs: finish_kernel(count, *refs),
        [((rows, quarter), jnp.bfloat16)] * count,
        [flags],
        stacked + list(begun) + pieces[-2:],
    )
    outs = [outs[0]] + [swap_in_slab(o, g, t) for o, (g, t) in zip(outs[1:], peers[1:])]
    sems = [pltpu.SemaphoreType.DMA((len(outs),))]
    shape = ((rows, width), jnp.bfloat16)
    return call(assemble_kernel, [shape], [flags], outs, sems, pl.ANY)[0]


def solution(mesh):
    placed = (
        P(("groups", "tp", "sp"), None),
        P(None, "tp"),
        P(None, "tp"),
        P(None, "tp"),
        P("tp", None),
        P("groups"),
    )

    return jax.shard_map(
        local,
        mesh=mesh,
        in_specs=placed,
        out_specs=P(("groups", "tp", "sp"), None),
        check_vma=False,
    )
```

```python
import jax
import jax.numpy as jnp
import numpy as np
from jax import lax
from jax.experimental import pallas as pl
from jax.experimental.pallas import tpu as pltpu
from jax.sharding import PartitionSpec as P

PRE_SCALE = 144

masked_low = -1e30


def swap_tp(block, flip, only=None):
    count = lax.axis_size("tp")
    route = [(t, t ^ flip) for t in range(count) if only is None or only(t)]
    return lax.ppermute(block, "tp", route)


def swap_sp(block):
    count = lax.axis_size("sp")
    return lax.ppermute(block, "sp", [(s, s ^ 1) for s in range(count)])


def swap_by_core(block, flips, only=lambda t: True):
    count, cores = lax.axis_size("tp"), lax.axis_size("sp")
    route = [
        (t * cores + s, (t ^ flips[s]) * cores + s)
        for t in range(count)
        for s in range(cores)
        if only(t)
    ]
    return lax.ppermute(block, ("tp", "sp"), route)


def swap_in_slab(block, group_flip, tp_flip):
    groups = lax.axis_size("groups")
    count = lax.axis_size("tp")
    route = [
        (g * count + t, (g ^ group_flip) * count + (t ^ tp_flip))
        for g in range(groups)
        for t in range(count)
    ]
    return lax.ppermute(block, ("groups", "tp"), route)


def fence(*values):
    return lax.optimization_barrier(values)


def call(kernel, shapes, scalars, operands, scratch=(), outs=pltpu.VMEM, far=(), limit=16):
    size = sum(x.size * x.dtype.itemsize for x in operands)
    params = None
    if size < 8 << 20:
        operands = [pltpu.with_memory_space_constraint(x, pltpu.VMEM) for x in operands]
        params = pltpu.CompilerParams(vmem_limit_bytes=limit << 20)
    specs = [pl.BlockSpec(memory_space=pltpu.SMEM)] * len(scalars)
    specs += [pl.BlockSpec(memory_space=pltpu.VMEM)] * len(operands)
    specs += [pl.BlockSpec(memory_space=pl.ANY)] * len(far)
    return pl.pallas_call(
        kernel,
        in_specs=specs,
        out_specs=[pl.BlockSpec(memory_space=outs)] * len(shapes),
        out_shape=[jax.ShapeDtypeStruct(*shape) for shape in shapes],
        scratch_shapes=list(scratch),
        compiler_params=params,
    )(*scalars, *operands, *far)


def plain(a, w):
    return jnp.dot(a, w, preferred_element_type=jnp.float32)


def turned(a, w):
    return lax.dot_general(a, w, (((1,), (1,)), ((), ())), preferred_element_type=jnp.float32)


def rows_at(blocks, offset, size):
    parts = [block[:, pl.ds(pl.multiple_of(offset, 128), size)] for block in blocks]
    return jnp.concatenate(parts, axis=0) if len(parts) > 1 else parts[0]


def products(blocks, weights, sp, group):
    w_query, w_key, w_value, kv_came, kv_other, *quarters = weights
    rows = jnp.concatenate([block[...] for block in blocks], axis=0)
    own_query = plain(rows, w_query[...])
    own_kv = turned(rows, jnp.concatenate([w_key[...], w_value[...]], axis=0))
    size = quarters[0].shape[0]
    pair_query = None
    for i, weight in enumerate(quarters):
        at = (sp ^ (i >> 1)) * 2 + (group ^ (i & 1))
        term = plain(rows_at(blocks, at * size, size), weight[...])
        pair_query = term if pair_query is None else pair_query + term
    depth = kv_came.shape[1]
    pair_kv = turned(rows_at(blocks, sp * depth, depth), kv_came[...]) + turned(
        rows_at(blocks, (1 - sp) * depth, depth), kv_other[...]
    )
    return own_query, own_kv, pair_query, pair_kv


def early_kernel(short, flags, *refs):
    blocks, weights, (out, far) = list(refs[:-11]), refs[-11:-2], refs[-2:]
    if short:
        far[...] = jnp.where(flags[2] != 0, blocks[2][...], blocks[3][...])
        blocks[2:4] = [far]
    head = weights[0].shape[1]
    for i, part in enumerate(products(blocks, weights, flags[0], flags[3])):
        out[:, i * head : (i + 1) * head] = part


def tail_kernel(flags, early, middle, relayed, cosine, sine_part, *refs):
    weights, (queries, key_value, last) = refs[:9], refs[9:]
    side, inner = flags[1], flags[2]
    head = weights[0].shape[1]
    half_head = head // 2
    last[...] = jnp.where(inner != 0, middle[...], relayed[...])
    late = products([last], weights, flags[0], flags[3])
    join = lambda i: jnp.concatenate([early[:, i * head : (i + 1) * head], late[i]], axis=0)
    own_query, own_kv, pair_query, pair_kv = [join(i) for i in range(4)]
    spin = lambda v: v * cosine[...] + pltpu.roll(v, half_head, 1) * sine_part[...]
    scale = PRE_SCALE ** (-0.5)
    count = own_query.shape[0]
    queries[:count] = (spin(own_query) * scale).astype(queries.dtype)
    queries[count:] = (spin(pair_query) * scale).astype(queries.dtype)
    lane = lax.broadcasted_iota(jnp.int32, own_kv.shape, 1)
    low = lane < half_head
    even = side == 0
    first = jnp.where(even, own_kv, pair_kv)
    second = jnp.where(even, pair_kv, own_kv)
    key_raw = jnp.where(low, first, pltpu.roll(second, half_head, 1))
    key_raw = key_raw.astype(jnp.bfloat16).astype(jnp.float32)
    key_value[:, :head] = spin(key_raw).astype(key_value.dtype)
    value = jnp.where(low, pltpu.roll(first, half_head, 1), second)
    key_value[:, head:] = value.astype(key_value.dtype)


def place_of(flags, index, flip_side, flip_core, slabs, rows, cores):
    block = jnp.zeros_like(index)
    for k in range(1, slabs):
        block = block + (index >= k * rows).astype(jnp.int32)
    at = (flags[5] ^ block) * 2 + (flags[1] ^ flip_side)
    return (at * cores + (flags[0] ^ flip_core)) * rows + index - block * rows


def tables_kernel(slabs, cores, flags, spread, cosine, sine_part):
    shape = cosine.shape
    index = lax.broadcasted_iota(jnp.int32, shape, 0)
    places = place_of(flags, index, 0, 0, slabs, shape[0] // slabs, cores)
    angles = places.astype(jnp.float32) * spread[...]
    cosine[...] = jnp.cos(angles)
    sines = jnp.sin(angles)
    low = lax.broadcasted_iota(jnp.int32, shape, 1) < shape[1] // 2
    sine_part[...] = jnp.where(low, -sines, sines)


def attend_kernel(slabs, cores, flags, lengths, queries, *refs):
    pieces, outs = refs[:4], refs[4:]
    count, head = pieces[0].shape[0], queries.shape[1]
    rows = count // slabs
    place = lambda shape, axis, a, b: place_of(
        flags, lax.broadcasted_iota(jnp.int32, shape, axis), a, b, slabs, rows, cores
    )
    end = 0
    ends = []
    for i in range(lengths.shape[0]):
        end = end + lengths[i]
        ends.append(end)
    step = min(count, 4 * rows)
    even = flags[1] == 0
    for at in range(0, count, step):
        index = at + lax.broadcasted_iota(jnp.int32, (step, 1), 0)
        query_places = place_of(flags, index, 0, 0, slabs, rows, cores)
        starts = jnp.zeros_like(query_places)
        for end in ends:
            starts = jnp.where(query_places >= end, end, starts)
        masks = []
        for c in range(4):
            key_places = place((1, count), 1, c % 2, c // 2)
            masks.append((key_places <= query_places) & (key_places >= starts))
        mixed = []
        for h in range(2):
            query = queries[h * count + at : h * count + at + step]
            scores = [
                jnp.where(mask, turned(query, piece[:, :head]), masked_low)
                for piece, mask in zip(pieces, masks)
            ]
            largest = scores[0]
            for part in scores[1:]:
                largest = jnp.maximum(largest, part)
            largest = jnp.max(largest, axis=1, keepdims=True)
            total, acc = 0.0, 0.0
            for part, piece, mask in zip(scores, pieces, masks):
                e = jnp.where(mask, jnp.exp(part - largest), 0.0)
                total = total + e
                acc = acc + plain(e.astype(jnp.bfloat16), piece[:, head:])
            total = jnp.sum(total, axis=1, keepdims=True)
            mixed.append((acc / total).astype(jnp.bfloat16))
        low = jnp.where(even, mixed[0], mixed[1])
        high = jnp.where(even, mixed[1], mixed[0])
        for k in range(step // rows):
            out = outs[at // rows + k]
            out[:, :head] = low[k * rows : (k + 1) * rows]
            out[:, head:] = high[k * rows : (k + 1) * rows]


def cut_query_kernel(flags, w_query, share_q, sem):
    quarter_depth = share_q.shape[0]
    at = pl.multiple_of((flags[0] * 2 + flags[3]) * quarter_depth, 128)
    copy = pltpu.make_async_copy(w_query.at[pl.ds(at, quarter_depth)], share_q, sem)
    copy.start()
    copy.wait()


def cut_kernel(flags, w_key, w_value, w_out, share_kv, out_sent, sems):
    sp = flags[0]
    head, depth = w_key.shape[0], share_kv.shape[1]
    half_rows, quarter = out_sent.shape
    deep = pl.ds(pl.multiple_of(sp * depth, 128), depth)
    columns = pl.ds(pl.multiple_of((flags[4] ^ 1) * quarter, 128), quarter)
    heads = pl.ds(pl.multiple_of(sp * half_rows, half_rows), half_rows)
    moves = (
        (w_key.at[:, deep], share_kv.at[:head]),
        (w_value.at[:, deep], share_kv.at[head:]),
        (w_out.at[heads, columns], out_sent),
    )
    copies = [pltpu.make_async_copy(a, b, sems.at[i]) for i, (a, b) in enumerate(moves)]
    for copy in copies:
        copy.start()
    for copy in copies:
        copy.wait()


def head_kernel(flags, came, other, w_out, out, sem):
    head, quarter = w_out.shape[0], out.shape[1]
    half_rows = came.shape[0]
    own = pl.ds(pl.multiple_of(flags[1] * head, head), head)
    columns = pl.ds(pl.multiple_of(flags[4] * quarter, 128), quarter)
    copy = pltpu.make_async_copy(w_out.at[:, columns], out.at[own], sem)
    copy.start()
    for i, piece in enumerate((came, other)):
        at = (1 - flags[1]) * head + (flags[0] ^ i) * half_rows
        out[pl.ds(pl.multiple_of(at, half_rows), half_rows)] = piece[...]
    copy.wait()


def tiles_of(width):
    step = 384 if width % 384 == 0 else width
    return [(at, at + step) for at in range(0, width, step)]


def begin_kernel(peers, flags, *refs):
    stacked, pieces, out = refs[:peers], refs[peers:-1], refs[-1]
    inner = sum(piece.shape[0] for piece in pieces)
    rows = jnp.concatenate([m[:, :inner] for m in stacked], axis=0)
    for a, b in tiles_of(out.shape[1]):
        out[:, a:b] = plain(rows, jnp.concatenate([p[:, a:b] for p in pieces], axis=0))


def finish_kernel(peers, flags, *refs):
    stacked, (begun, came, other), outs = refs[:peers], refs[peers:-peers], refs[-peers:]
    count, width = outs[0].shape
    inner = stacked[0].shape[1] - came.shape[0]
    rows = jnp.concatenate([m[:, inner:] for m in stacked], axis=0)
    received = flags[2] != flags[0]
    for a, b in tiles_of(width):
        weight = jnp.where(received, came[:, a:b], other[:, a:b])
        total = begun[:, a:b] + plain(rows, weight)
        for i, out in enumerate(outs):
            out[:, a:b] = total[i * count : (i + 1) * count].astype(out.dtype)


def assemble_kernel(flags, *refs):
    pieces, out, sems = refs[:-2], refs[-2], refs[-1]
    width = pieces[0].shape[1]
    copies = []
    for i, piece in enumerate(pieces):
        at = pl.multiple_of((flags[4] ^ i) * width, 128)
        copies.append(pltpu.make_async_copy(piece, out.at[:, pl.ds(at, width)], sems.at[i]))
        copies[-1].start()
    for copy in copies:
        copy.wait()


def local(tokens, w_query, w_key, w_value, w_out, doc_lengths):
    rows, width = tokens.shape
    tp_count = lax.axis_size("tp")
    sp_count = lax.axis_size("sp")
    sp_place = lax.axis_index("sp")
    tp_place = lax.axis_index("tp")
    group = lax.axis_index("groups") % 2
    slabs = tp_count // 2
    slab = tp_place // 2
    side = tp_place % 2
    head_dim = w_query.shape[1]
    short = slabs == 4
    is_inner = lambda t: (t >> 1) in (1, 2)

    if short:
        far_out = swap_tp(tokens, 4, lambda t: not is_inner(t))
        far_in = swap_tp(tokens, 4, is_inner)
        near = swap_tp(tokens, 2)
        middle = swap_tp(tokens, 6, is_inner)
        relayed = swap_tp(far_out, 2, is_inner)
        firsts, last = [tokens, near, far_out, far_in], [middle, relayed]
    else:
        came = [swap_tp(tokens, 2 * k) for k in range(1, slabs)]
        firsts, last = [tokens] + came[:-1], [came[-1], came[-1]]

    depth = width // sp_count
    quarter = w_out.shape[1] // 4
    half_rows = head_dim // sp_count
    mine = group * 2 + side
    inner = ((slab == 1) | (slab == 2)).astype(jnp.int32)
    flags = jnp.stack([sp_place, side, inner, group, mine, slab]).astype(jnp.int32)
    turned_kv = [w_key.T, w_value.T]
    core_low = sp_place == 0
    flags, doc_lengths, core_low = fence(flags, doc_lengths, core_low)
    in_hbm = lambda *arrays: [pltpu.with_memory_space_constraint(x, pltpu.HBM) for x in arrays]
    place = pltpu.VMEM if short else pl.ANY
    share_q = call(
        cut_query_kernel,
        [((depth // 2, head_dim), jnp.bfloat16)],
        [flags],
        [],
        [pltpu.SemaphoreType.DMA(())],
        place,
        in_hbm(w_query),
    )[0]
    share_kv, out_sent = call(
        cut_kernel,
        [((head_dim, depth), jnp.bfloat16), ((half_rows, quarter), jnp.bfloat16)],
        [flags],
        [],
        [pltpu.SemaphoreType.DMA((3,))],
        place,
        in_hbm(*turned_kv, w_out),
    )
    came_q = swap_tp(share_q, 1)
    cross_q = swap_in_slab(came_q, 1, 0)
    came_kv = swap_tp(share_kv, 1)
    out_came = swap_tp(out_sent, 1)
    out_other = swap_sp(out_came)
    weights = [w_query, *turned_kv, came_kv, swap_sp(came_kv), came_q, cross_q]
    weights += [swap_sp(came_q), swap_sp(cross_q)]
    early = call(
        lambda *refs: early_kernel(short, *refs),
        [(((slabs - 1) * rows, 4 * head_dim), jnp.float32)],
        [flags],
        firsts + weights,
        [pltpu.VMEM((rows, width), jnp.bfloat16)],
    )[0]

    in_order = lambda a, b, flag: [jnp.where(flag, a, b), jnp.where(flag, b, a)]
    out_own = call(
        head_kernel,
        [((2 * head_dim, quarter), jnp.bfloat16)],
        [flags],
        [out_came, out_other],
        [pltpu.SemaphoreType.DMA(())],
        far=[w_out],
    )[0]
    if short:
        out_first = swap_by_core(out_own, (2, 4))
        out_swapped = swap_sp(out_first)

    count = slabs * rows
    half_head = head_dim // 2
    powers = np.arange(head_dim, dtype=np.float32) % half_head * np.float32(2.0 / head_dim)
    spread = jnp.asarray(np.power(np.float32(10000.0), -powers)[None, :])
    tables = call(
        lambda *refs: tables_kernel(slabs, sp_count, *refs),
        [((count, head_dim), jnp.float32)] * 2,
        [flags],
        [spread],
    )
    queries, key_value = call(
        tail_kernel,
        [((2 * count, head_dim), jnp.bfloat16), ((count, 2 * head_dim), jnp.bfloat16)],
        [flags],
        [early, *last, *tables] + weights,
        [pltpu.VMEM((rows, width), jnp.bfloat16)],
    )

    beside = swap_tp(key_value, 1)
    every = [key_value, beside, swap_sp(key_value), swap_sp(beside)]
    mixed = call(
        lambda *refs: attend_kernel(slabs, sp_count, *refs),
        [((rows, 2 * head_dim), jnp.bfloat16)] * slabs,
        [flags, doc_lengths],
        [queries] + every,
        limit=16 if short else 56,
    )

    parts = [mixed[0]]
    for k in range(1, slabs):
        parts.append(swap_tp(mixed[k], 2 * k))
    if short:
        parts[1:3] = in_order(parts[1], parts[2], core_low)
    merged = jnp.concatenate(parts, axis=1)
    peers = ((0, 0), (0, 1), (1, 0), (1, 1))
    stacked = [merged] + [swap_in_slab(merged, g, t) for g, t in peers[1:]]
    if short:
        out_sent = jnp.where(core_low, out_own, out_first)
        out_last = swap_by_core(out_sent, (6, 2), is_inner)
        out_last, stacked[3] = fence(out_last, stacked[3])
        pieces = [out_own, out_first, out_swapped, out_last, swap_sp(out_last)]
    else:
        pieces = [out_own]
        mine_of = lax.dynamic_slice_in_dim(out_own, sp_place * head_dim, head_dim, 0)
        for k in range(1, slabs):
            piece = swap_tp(mine_of, 2 * k)
            both = in_order(piece, swap_sp(piece), core_low)
            pieces.append(jnp.concatenate(both, axis=0))
    if not short:
        pieces.append(pieces[-1])
    count, kept = len(peers), pieces[:-2]
    begun = call(
        lambda *refs: begin_kernel(count, *refs),
        [((count * rows, quarter), jnp.float32)],
        [flags],
        stacked + kept,
    )
    outs = call(
        lambda *refs: finish_kernel(count, *refs),
        [((rows, quarter), jnp.bfloat16)] * count,
        [flags],
        stacked + list(begun) + pieces[-2:],
    )
    outs = [outs[0]] + [swap_in_slab(o, g, t) for o, (g, t) in zip(outs[1:], peers[1:])]
    sems = [pltpu.SemaphoreType.DMA((len(outs),))]
    shape = ((rows, width), jnp.bfloat16)
    return call(assemble_kernel, [shape], [flags], outs, sems, pl.ANY)[0]


def solution(mesh):
    placed = (
        P(("groups", "tp", "sp"), None),
        P(None, "tp"),
        P(None, "tp"),
        P(None, "tp"),
        P("tp", None),
        P("groups"),
    )

    return jax.shard_map(
        local,
        mesh=mesh,
        in_specs=placed,
        out_specs=P(("groups", "tp", "sp"), None),
        check_vma=False,
    )
```
